32 devices in a mesh: req: 4 (over x, core), exp: 8 (over z, y).
Axes of the slice: x: 2, y: 2, z: 4, core: 2. Of those that a mesh axis runs over, the one named last changes fastest.
Arguments:
- tokens: bfloat16 [32, 256, 1024], P(('req', 'exp')), may hold values from -6 to 6
- attention_norm_gain: float32 [1024], replicated, may hold values from 0.4 to 1.6
- expert_norm_gain: float32 [1024], replicated, may hold values from 0.4 to 1.6
- query_key_value_weight: bfloat16 [1024, 16, 192], P(None, 'exp'), may hold values from -0.1875 to 0.1875
- output_weight: bfloat16 [16, 64, 1024], replicated, may hold values from -0.1875 to 0.1875
- prompt_key_value_cache: bfloat16 [4, 1024, 16, 128], P(None, None, 'exp'), may hold values from -160 to 160
- shared_prompt_length: int32 [4], replicated, may hold values from 1 to 1024, 2560 in all
- prompt_per_request: int32 [32], P('req'), may hold values from 0 to 3
- adapter_per_request: int32 [32], replicated, may hold values from 0 to 31
- adapter_slot_rows: int32 [32], replicated, may hold values from 0 to 31, each once
- adapter_down_qkv: bfloat16 [32, 1024, 48], P('req'), may hold values from -0.1875 to 0.1875
- adapter_up_qkv: bfloat16 [32, 3, 16, 16, 64], P('req', None, None, 'exp'), may hold values from -1.5 to 1.5
- adapter_down_output: bfloat16 [32, 16, 64, 16], P('req'), may hold values from -0.1875 to 0.1875
- adapter_up_output: bfloat16 [32, 16, 1024], P('req'), may hold values from -1.5 to 1.5
- router_weight: bfloat16 [1024, 8], replicated, may hold values from -0.1875 to 0.1875
- expert_gate_up_weight: bfloat16 [8, 1024, 5632], P('exp'), may hold values from -0.1875 to 0.1875
- expert_down_weight: bfloat16 [8, 2816, 1024], P('exp'), may hold values from -0.109375 to 0.109375
- routes: int32 [32, 256, 2], P(('req', 'exp')), may hold values from 0 to 7, as said below
- slots: int32 [32, 256, 2], P(('req', 'exp')), may hold values from -1 to 79, as said below
Outputs:
- mixed: bfloat16 [32, 256, 1024], P(('req', 'exp'))
The draws below stay inside these ranges and needn't reach their ends.
Inputs may be any that keep to these rules, and one draw needn't show every extreme that they name: `shared_prompt_length`: the largest length is 1024. `adapter_slot_rows`: each adapter id has its own table row. `routes`: each token names 2 different experts; every expert is named. Among the tokens of one device (one index of req and one of exp) the non-negative slots of one expert are distinct; in every index of req some expert receives 80 slots from every device.
All inputs are finite; a program needn't handle non-finite values.
Results may differ from the reference program's by a relative error of at most 0.012.
The reference program's roundings to bfloat16 on the way count: a program that leaves them out, or rounds other values in their place, can miss the bound.
Values may be sent and summed in bfloat16 or wider, within the bound.
A program may use at most 128 MiB of HBM per device.

```python
import math
import jax
import jax.numpy as jnp
import numpy as np
from jax import lax

MODEL_WIDTH = 1024
HEAD_COUNT = 16
HEAD_WIDTH = 64
FF = 2816
ADAPTER_RANK = 16
TOP = 2
PROMPTS = 4
PMAX = 1024
REQ_DEV = 1
NEW_LENGTH = 256
EXPERTS = 8
ADAPTER_COUNT = 32
REQUESTS = 32
CAP = 80
N_REQ = 4
N_EXP = 8


def draw_prompt_key_value_cache(key, part):
    normal_key = jax.random.fold_in(jax.random.fold_in(key, 3), 0)
    shape_all = (PROMPTS, PMAX, HEAD_COUNT, 2 * HEAD_WIDTH)
    entries = jnp.clip(jax.random.normal(normal_key, shape_all, jnp.float32), -4.0, 4.0)
    return entries.astype(jnp.bfloat16)


def route_tables(key):
    devices = REQUESTS // REQ_DEV
    groups = devices // N_EXP
    rows_dev = REQ_DEV * NEW_LENGTH
    assigned = rows_dev * TOP
    capacity = 5 * assigned // (4 * EXPERTS)
    spread = assigned - 2 * capacity
    hot_key, order_key, row_key = jax.random.split(jax.random.fold_in(key, 17), 3)
    hottest = jnp.repeat(jax.random.randint(hot_key, (groups,), 0, EXPERTS), N_EXP)

    def shuffle_rest(sub_key):
        return jax.random.permutation(sub_key, EXPERTS - 1).astype(jnp.int32) + 1
    offsets = jax.vmap(shuffle_rest)(jax.random.split(order_key, devices))
    offsets = jnp.concatenate([jnp.zeros((devices, 1), jnp.int32), offsets], axis=1)
    order = (hottest[:, None] + offsets) % EXPERTS
    place = jnp.arange(assigned, dtype=jnp.int32)
    beyond = jnp.maximum(place - 2 * capacity, 0)
    bucket = jnp.where(place < 2 * capacity, 0, 1 + beyond * (EXPERTS - 1) // spread)
    first = jnp.where(bucket == 0, 0, 2 * capacity + ((bucket - 1) * spread + EXPERTS - 2) // (EXPERTS - 1))
    position = place - first
    slot_line = jnp.where(position < capacity, position, -1)
    expert_line = jnp.take_along_axis(order, jnp.broadcast_to(bucket[None, :], (devices, assigned)), axis=1)
    expert_rows = jnp.transpose(expert_line.reshape(devices, TOP, rows_dev), (0, 2, 1))
    slot_rows = jnp.broadcast_to(jnp.transpose(slot_line.reshape(TOP, rows_dev))[None], (devices, rows_dev, TOP))

    def shuffle_rows(sub_key):
        return jax.random.permutation(sub_key, rows_dev).astype(jnp.int32)
    row_order = jax.vmap(shuffle_rows)(jax.random.split(row_key, devices))
    row_index = jnp.broadcast_to(row_order[:, :, None], (devices, rows_dev, TOP))
    expert_rows = jnp.take_along_axis(expert_rows, row_index, axis=1)
    slot_rows = jnp.take_along_axis(slot_rows, row_index, axis=1)
    return (expert_rows.reshape(REQUESTS, NEW_LENGTH, TOP).astype(jnp.int32), slot_rows.reshape(REQUESTS, NEW_LENGTH, TOP).astype(jnp.int32))


def draw_routes(key, part):
    return route_tables(key)[0]


def draw_slots(key, part):
    return route_tables(key)[1]


def set_ends(drawn, rng, least, high):
    extent = drawn.shape
    index_at = [jax.random.randint(jax.random.fold_in(rng, axis), (), 0, extent[axis]) for axis in range(len(extent))]
    drawn = drawn.at[tuple(index_at)].set(least)
    longest = extent.index(max(extent))
    index_at[longest] = (index_at[longest] + 1) % extent[longest]
    return drawn.at[tuple(index_at)].set(high)


def shard_levels(key, dims, shards, least, top_value):
    loudness, own = 1.0, jax.random.fold_in(key, 6)
    for axis_at, shards_of in shards:
        draws = jnp.exp(jax.random.uniform(jax.random.fold_in(own, axis_at), (shards_of,), jnp.float32, least / len(shards), top_value / len(shards)))
        loudness = loudness * jnp.repeat(draws, dims[axis_at] // shards_of).reshape([-1 if axis == axis_at else 1 for axis in range(len(dims))])
    return loudness


def cumulative_ranks(number_of, skew):
    weights = [(1 << 20) // math.isqrt(grade ** skew) + 1 for grade in range(1, number_of + 1)]
    scale = 1 + sum(weights) // (1 << 30)
    return np.cumsum(np.array([max(1, weight // scale) for weight in weights]))


def skewed_ids(own_key, extent, count, slope):
    table = cumulative_ranks(count, slope)
    lot = jax.random.randint(jax.random.fold_in(own_key, 1), extent, 0, int(table[count - 1]))
    rank = jnp.searchsorted(jnp.asarray(table, jnp.int32), lot, side="right")
    return jax.random.permutation(jax.random.fold_in(own_key, 2), count)[rank].astype(jnp.int32)


def length_profile(number_of, total, most, lean):
    portions = [(1 << 20) // math.isqrt(rank ** lean) + 1 for rank in range(2, number_of + 1)]
    spare, counts = total - most - (number_of - 1), [1] * (number_of - 1)
    while spare > 0:
        movable = [i for i in range(number_of - 1) if counts[i] < most]
        whole, remaining = sum([portions[i] for i in movable]), spare
        for i in movable:
            extra = min(most - counts[i], max(1, remaining * portions[i] // whole), spare)
            counts[i] = counts[i] + extra
            spare = spare - extra
    return np.array([most] + counts)


def ragged_sizes(stream_key, count, total, limit, slope):
    if count == 2:
        one = jax.random.randint(stream_key, (), max(1, total - limit), min(limit, total - 1) + 1)
        return jnp.stack([one, total - one])
    lengths = jnp.asarray(length_profile(count, total, limit, slope), jnp.int32)
    pairs = (count - 1) // 2
    donor, taker = lengths[1:1 + 2 * pairs:2], lengths[2:2 + 2 * pairs:2]
    room = jnp.minimum(donor - 1, limit - taker)
    moved = jax.random.randint(jax.random.fold_in(stream_key, 1), (pairs,), 0, 1 << 20) % (room + 1)
    lengths = lengths.at[1:1 + 2 * pairs:2].set(donor - moved).at[2:2 + 2 * pairs:2].set(taker + moved)
    return lengths[jax.random.permutation(jax.random.fold_in(stream_key, 2), count)]


def centred(own_key, shape, deviation, bound, cuts=(), kind=jnp.bfloat16):
    result = jax.random.normal(own_key, shape, jnp.float32) * deviation
    if len(cuts) > 0:
        result = shard_levels(own_key, shape, cuts, -0.22, 0.18) * result
    return jnp.clip(result, min=-bound, max=bound).astype(kind)


def setup_inputs(seed: int = 0) -> dict:
    keys = jax.random.split(jax.random.key(seed), 20)
    return {
        "tokens": centred(keys[0], (REQUESTS, NEW_LENGTH, MODEL_WIDTH), 1.0, 6.0, ((0, 32),)),
        "attention_norm_gain": jnp.clip(1.0 + 0.12 * jax.random.normal(keys[1], (MODEL_WIDTH,), jnp.float32), 0.4, 1.6),
        "expert_norm_gain": jnp.clip(1.0 + 0.12 * jax.random.normal(keys[2], (MODEL_WIDTH,), jnp.float32), 0.4, 1.6),
        "query_key_value_weight": centred(keys[3], (MODEL_WIDTH, HEAD_COUNT, 3 * HEAD_WIDTH), MODEL_WIDTH ** -0.5, 0.1875, ((1, 8),)),
        "output_weight": centred(keys[4], (HEAD_COUNT, HEAD_WIDTH, MODEL_WIDTH), (HEAD_COUNT * HEAD_WIDTH) ** -0.5, 0.1875),
        "prompt_key_value_cache": draw_prompt_key_value_cache(jax.random.fold_in(keys[19], 71), 0),
        "shared_prompt_length": ragged_sizes(keys[6], PROMPTS, 5 * PMAX // 2, PMAX, 1).astype(jnp.int32),
        "prompt_per_request": set_ends(jax.random.randint(keys[7], (REQUESTS,), 0, PROMPTS), jax.random.fold_in(keys[7], 1), 0, PROMPTS - 1).astype(jnp.int32),
        "adapter_per_request": set_ends(skewed_ids(keys[8], (REQUESTS,), ADAPTER_COUNT, 2), jax.random.fold_in(keys[8], 3), 0, ADAPTER_COUNT - 1).astype(jnp.int32),
        "adapter_slot_rows": jax.random.permutation(keys[9], ADAPTER_COUNT).astype(jnp.int32),
        "adapter_down_qkv": centred(keys[10], (ADAPTER_COUNT, MODEL_WIDTH, 3 * ADAPTER_RANK), MODEL_WIDTH ** -0.5, 0.1875, ((0, 4),)),
        "adapter_up_qkv": centred(keys[11], (ADAPTER_COUNT, 3, ADAPTER_RANK, HEAD_COUNT, HEAD_WIDTH), ADAPTER_RANK ** -0.5, 1.5, ((0, 4), (3, 8))),
        "adapter_down_output": centred(keys[12], (ADAPTER_COUNT, HEAD_COUNT, HEAD_WIDTH, ADAPTER_RANK), (HEAD_COUNT * HEAD_WIDTH) ** -0.5, 0.1875, ((0, 4),)),
        "adapter_up_output": centred(keys[13], (ADAPTER_COUNT, ADAPTER_RANK, MODEL_WIDTH), ADAPTER_RANK ** -0.5, 1.5, ((0, 4),)),
        "router_weight": centred(keys[14], (MODEL_WIDTH, EXPERTS), MODEL_WIDTH ** -0.5, 0.1875),
        "expert_gate_up_weight": centred(keys[15], (EXPERTS, MODEL_WIDTH, 2 * FF), MODEL_WIDTH ** -0.5, 0.1875, ((0, 8),)),
        "expert_down_weight": centred(keys[16], (EXPERTS, FF, MODEL_WIDTH), FF ** -0.5, 0.109375, ((0, 8),)),
        "routes": draw_routes(jax.random.fold_in(keys[19], 71), 0),
        "slots": draw_slots(jax.random.fold_in(keys[19], 71), 0),
    }


adapter_scale = 0.5
norm_eps = 1e-06
masked_score = -1e+30

def rms_norm(values, gain):
    widened = values.astype(jnp.float32)
    factor = lax.rsqrt(lax.optimization_barrier(jnp.mean(widened * widened, axis=-1, keepdims=True)) + norm_eps)
    return (widened * factor * gain).astype(jnp.bfloat16)

def reference(tokens, attention_norm_gain, expert_norm_gain, query_key_value_weight, output_weight, prompt_key_value_cache, shared_prompt_length, prompt_per_request, adapter_per_request, adapter_slot_rows, adapter_down_qkv, adapter_up_qkv, adapter_down_output, adapter_up_output, router_weight, expert_gate_up_weight, expert_down_weight, routes, slots):
    normed = rms_norm(tokens, attention_norm_gain)
    adapter_table_rows = adapter_slot_rows[adapter_per_request]
    selected_down_qkv = adapter_down_qkv[adapter_table_rows]
    selected_up_qkv = adapter_up_qkv[adapter_table_rows]
    selected_down_output = adapter_down_output[adapter_table_rows]
    selected_up_output = adapter_up_output[adapter_table_rows]
    low_rank = jnp.einsum('jsd,jdr->jsr', normed.astype(jnp.float32), selected_down_qkv.astype(jnp.float32)).astype(jnp.bfloat16)
    att_scale = HEAD_WIDTH ** (-0.5)
    cached_pos = jnp.arange(PMAX, dtype=jnp.int32)
    causal = jnp.arange(NEW_LENGTH, dtype=jnp.int32)[:, None] >= jnp.arange(NEW_LENGTH, dtype=jnp.int32)[None, :]
    w_qkv_wide = query_key_value_weight.astype(jnp.float32)

    def attend_one(packed):
        normed_one, low_one, up_single, ao_one, bo_one, prompt_one = packed
        base_query_key_value = jnp.einsum('sd,dhc->shc', normed_one.astype(jnp.float32), w_qkv_wide)
        rank_pieces = low_one.astype(jnp.float32).reshape(NEW_LENGTH, 3, ADAPTER_RANK)
        adapter_increment = jnp.einsum('lya,yazj->lzyj', rank_pieces, up_single.astype(jnp.float32)).reshape(NEW_LENGTH, HEAD_COUNT, 3 * HEAD_WIDTH)
        rounded_length = lax.optimization_barrier((base_query_key_value + adapter_scale * adapter_increment).astype(jnp.bfloat16))
        qkv_wide = rounded_length.astype(jnp.float32)
        queries = qkv_wide[:, :, :HEAD_WIDTH]
        own_keys = qkv_wide[:, :, HEAD_WIDTH:2 * HEAD_WIDTH]
        own_values = qkv_wide[:, :, 2 * HEAD_WIDTH:]
        prefix_one = lax.dynamic_index_in_dim(prompt_key_value_cache, prompt_one, 0, keepdims=False).astype(jnp.float32)
        length_one = lax.dynamic_index_in_dim(shared_prompt_length, prompt_one, 0, keepdims=False)
        pre_scores = jnp.einsum('she,the->hst', queries, prefix_one[:, :, :HEAD_WIDTH]) * att_scale
        pre_scores = jnp.where((cached_pos < length_one)[None, None, :], pre_scores, masked_score)
        own_scores = jnp.einsum('she,the->hst', queries, own_keys) * att_scale
        own_scores = jnp.where(causal[None], own_scores, masked_score)
        row_peak = jnp.maximum(lax.optimization_barrier(jnp.max(pre_scores, axis=-1, keepdims=True)), lax.optimization_barrier(jnp.max(own_scores, axis=-1, keepdims=True)))
        pre_exp = jnp.exp(pre_scores - row_peak)
        own_exp = jnp.exp(own_scores - row_peak)
        denominator = lax.optimization_barrier(jnp.sum(pre_exp, axis=-1, keepdims=True)) + lax.optimization_barrier(jnp.sum(own_exp, axis=-1, keepdims=True))
        pre_weight = lax.optimization_barrier((pre_exp / denominator).astype(jnp.bfloat16)).astype(jnp.float32)
        own_weight = lax.optimization_barrier((own_exp / denominator).astype(jnp.bfloat16)).astype(jnp.float32)
        attended = jnp.einsum('hst,the->she', pre_weight, prefix_one[:, :, HEAD_WIDTH:]) + jnp.einsum('hst,the->she', own_weight, own_values)
        flat_att = attended.astype(jnp.bfloat16).reshape(NEW_LENGTH, HEAD_COUNT * HEAD_WIDTH)
        projected_rows = jnp.dot(flat_att, output_weight.reshape(HEAD_COUNT * HEAD_WIDTH, MODEL_WIDTH), preferred_element_type=jnp.float32)
        low_out = jnp.dot(flat_att, ao_one.reshape(HEAD_COUNT * HEAD_WIDTH, ADAPTER_RANK), preferred_element_type=jnp.float32)
        surplus_rows = jnp.dot(low_out, bo_one.astype(jnp.float32), precision=lax.Precision.HIGHEST)
        return projected_rows + adapter_scale * surplus_rows
    projected_all = lax.map(attend_one, (normed, low_rank, selected_up_qkv, selected_down_output, selected_up_output, prompt_per_request))
    hidden = (tokens.astype(jnp.float32) + projected_all).astype(jnp.bfloat16)
    moe_in = rms_norm(hidden, expert_norm_gain)
    flat_in = moe_in.reshape(REQUESTS * NEW_LENGTH, MODEL_WIDTH)
    gate_vals = jax.nn.sigmoid(jnp.dot(flat_in, router_weight, preferred_element_type=jnp.float32)).reshape(REQUESTS, NEW_LENGTH, EXPERTS)
    devices_all = N_REQ * N_EXP
    row_ids = jnp.arange(REQUESTS, dtype=jnp.int32)[:, None]
    col_ids = jnp.arange(NEW_LENGTH, dtype=jnp.int32)[None, :]
    source = row_ids // REQ_DEV + 0 * col_ids
    token_ids = row_ids * NEW_LENGTH + col_ids
    places = EXPERTS * devices_all * CAP
    target = jnp.where(slots >= 0, (routes * devices_all + source[:, :, None]) * CAP + slots, places).astype(jnp.int32)
    fill_ids = jnp.broadcast_to(token_ids[:, :, None], target.shape).reshape(-1)
    table = jnp.full((places + 1,), REQUESTS * NEW_LENGTH, jnp.int32).at[target.reshape(-1)].set(fill_ids)
    table = table[:places].reshape(EXPERTS, devices_all * CAP)
    padded = jnp.concatenate([flat_in, jnp.zeros((1, MODEL_WIDTH), jnp.bfloat16)], axis=0)

    def expert_one(packed):
        index_rows, gate_up_one, down_one = packed
        gathered = padded[index_rows]
        both_parts = jnp.dot(gathered, gate_up_one, preferred_element_type=jnp.float32)
        activated = (jax.nn.gelu(both_parts[:, :FF], approximate=True) * both_parts[:, FF:]).astype(jnp.bfloat16)
        return jnp.dot(activated, down_one, preferred_element_type=jnp.float32).astype(jnp.bfloat16)
    results = lax.map(expert_one, (table, expert_gate_up_weight, expert_down_weight)).reshape(places, MODEL_WIDTH)
    fetched = results[jnp.minimum(target, places - 1)].astype(jnp.float32)
    chosen_gate = jnp.take_along_axis(gate_vals, routes, axis=-1)
    weight_used = jnp.where(slots >= 0, chosen_gate, 0.0)
    moe_sum = lax.optimization_barrier(jnp.sum(weight_used[:, :, :, None] * fetched, axis=2))
    return (hidden.astype(jnp.float32) + moe_sum).astype(jnp.bfloat16)
```

```python
import functools

import jax
import jax.numpy as jnp
from jax import lax
from jax.experimental import pallas as pl
from jax.experimental.pallas import tpu as pltpu
from jax.sharding import PartitionSpec as P

MODEL_WIDTH = 1024
HEAD_WIDTH = 64
FF = 2816
ADAPTER_RANK = 16
TOP = 2
REQ_DEV = 1


adapter_scale = 0.5
norm_eps = 1e-06
MESH = pl.DeviceIdType.MESH
masked_score = -1e30


def rms_norm(values, gain):
    widened = values.astype(jnp.float32)
    factor = lax.rsqrt(jnp.mean(widened * widened, axis=-1, keepdims=True) + norm_eps)
    return (widened * factor * gain).astype(jnp.bfloat16)


def ring_device(spot, count):
    turned = spot // (count // 2)
    return 2 * (spot + turned * (count - 1 - 2 * spot)) + turned


def layer_kernel(
    sizes,
    prompts,
    lengths,
    rows_wanted,
    tokens_ref,
    gain_ref,
    weight_ref,
    cache_ref,
    down_ref,
    lift_ref,
    narrow_ref,
    up_ref,
    out_ref,
    lift_out_ref,
    narrow_out_ref,
    wide,
    rows,
    low,
    att_out,
    att_in,
    staging,
    offered,
    staging_narrow,
    offered_narrow,
    up_all,
    row_send,
    row_recv,
    low_send,
    low_recv,
    att_send,
    att_recv,
    down_send,
    down_recv,
    narrow_send,
    narrow_recv,
    up_send,
    up_recv,
):
    count, req_count, heads = sizes
    half = count // 2
    last = count - 1
    seq = tokens_ref.shape[1]
    mid = seq // 2
    table_rows = down_ref.shape[0]
    rank = 3 * ADAPTER_RANK
    my_req = lax.axis_index("req")
    my_exp = lax.axis_index("exp")
    my_side = my_exp % 2
    my_spot = my_exp // 2 + my_side * (count - 1 - 2 * (my_exp // 2))

    def at_spot(offset):
        return ring_device((my_spot + offset + count) % count, count)

    def at_req(offset):
        return (my_req + offset) % req_count

    barrier = pltpu.get_barrier_semaphore()
    for step in range(1, count):
        pl.semaphore_signal(barrier, inc=1, device_id=(my_req, at_spot(step)), device_id_type=MESH)
    for step in range(1, req_count):
        pl.semaphore_signal(barrier, inc=1, device_id=(at_req(step), my_exp), device_id_type=MESH)

    widened = tokens_ref[0].astype(jnp.float32)
    factor = lax.rsqrt(jnp.mean(widened * widened, axis=-1, keepdims=True) + norm_eps)
    rows[0] = (widened * factor * gain_ref[...]).astype(jnp.bfloat16)
    up_all[0] = up_ref[...]
    for step in range(req_count):
        wanted_row = rows_wanted[at_req(step) * count + my_exp]
        row = wanted_row % table_rows
        staging[step, :rank] = down_ref[row]
        staging[step, rank:] = lift_ref[row]
        staging_narrow[step] = narrow_ref[row]
    offered[0] = staging[0]
    offered_narrow[0] = staging_narrow[0]
    pl.semaphore_wait(barrier, count - 1 + req_count - 1)

    def send_rows(source, target, towards):
        return pltpu.make_async_remote_copy(
            src_ref=rows.at[source],
            dst_ref=rows.at[target],
            send_sem=row_send.at[target],
            recv_sem=row_recv.at[target],
            device_id=(my_req, at_spot(towards)),
            device_id_type=MESH,
        )

    def send_part(source, side, towards):
        part = pl.ds(side * mid, mid)
        return pltpu.make_async_remote_copy(
            src_ref=rows.at[source, part],
            dst_ref=rows.at[last, part],
            send_sem=row_send.at[last + side],
            recv_sem=row_recv.at[last + side],
            device_id=(my_req, at_spot(towards)),
            device_id_type=MESH,
        )

    def send_low(source, target, towards):
        return pltpu.make_async_remote_copy(
            src_ref=low.at[source],
            dst_ref=low.at[target],
            send_sem=low_send.at[target],
            recv_sem=low_recv.at[target],
            device_id=(my_req, at_spot(towards)),
            device_id_type=MESH,
        )

    def send_down(step):
        return pltpu.make_async_remote_copy(
            src_ref=staging.at[step],
            dst_ref=offered.at[step],
            send_sem=down_send.at[step],
            recv_sem=down_recv.at[step],
            device_id=(at_req(step), my_exp),
            device_id_type=MESH,
        )

    def send_narrow(step):
        return pltpu.make_async_remote_copy(
            src_ref=staging_narrow.at[step],
            dst_ref=offered_narrow.at[step],
            send_sem=narrow_send.at[step],
            recv_sem=narrow_recv.at[step],
            device_id=(at_req(step), my_exp),
            device_id_type=MESH,
        )

    def send_up(step):
        return pltpu.make_async_remote_copy(
            src_ref=up_ref,
            dst_ref=up_all.at[step],
            send_sem=up_send.at[step],
            recv_sem=up_recv.at[step],
            device_id=(at_req(step), my_exp),
            device_id_type=MESH,
        )

    def send_att(slot):
        distance = (slot + 1) // 2 * (1 - 2 * (slot % 2))
        return pltpu.make_async_remote_copy(
            src_ref=att_out.at[slot],
            dst_ref=att_in.at[slot],
            send_sem=att_send.at[slot],
            recv_sem=att_recv.at[slot],
            device_id=(my_req, at_spot(distance)),
            device_id_type=MESH,
        )

    send_rows(0, 1, 1).start()
    send_rows(0, 2, -1).start()
    for step in range(1, req_count):
        send_down(step).start()
    for step in range(1, req_count):
        send_up(step).start()
        send_narrow(step).start()
    for head in range(heads):
        wide[:, head * 256 : head * 256 + 128] = weight_ref[head, :128].T
        wide[:, head * 256 + 128 : head * 256 + 256] = weight_ref[head, HEAD_WIDTH:].T
    for step in range(1, req_count):
        send_down(step).wait_recv()
    own_row = rows_wanted[my_req * count + my_exp]
    source = (my_req - own_row // table_rows + req_count) % req_count
    mine = offered[source]
    lift_out_ref[...] = mine[rank:]
    contract = (((1,), (1,)), ((), ()))
    low[0] = lax.dot_general(
        mine[:rank], rows[0], contract, preferred_element_type=jnp.float32
    ).astype(jnp.bfloat16)
    send_low(0, 1, 1).start()
    send_low(0, 2, -1).start()
    for step in range(1, req_count):
        send_up(step).wait_recv()
        send_narrow(step).wait_recv()
    narrow_out_ref[...] = offered_narrow[source]

    causal = lax.broadcasted_iota(jnp.int32, (seq, seq), 0) >= lax.broadcasted_iota(
        jnp.int32, (seq, seq), 1
    )
    cached_at = lax.broadcasted_iota(jnp.int32, (1, cache_ref.shape[2]), 1)
    kind = lax.broadcasted_iota(jnp.int32, (rank, 128), 0) // ADAPTER_RANK
    first = lax.broadcasted_iota(jnp.int32, (rank, 128), 1) < HEAD_WIDTH
    is_query = (kind == 0) & first
    is_kv = ((kind == 1) & first) | ((kind == 2) & jnp.logical_not(first))
    by_rank = (((0,), (0,)), ((), ()))
    front = lax.broadcasted_iota(jnp.int32, (1, 128), 1) < HEAD_WIDTH
    att_scale = HEAD_WIDTH ** (-0.5)

    def process(slot, carry):
        @pl.when((slot % 2 == 1) & (slot < last))
        def _():
            send_rows(0, slot, 1).wait_recv()

            @pl.when(slot < last - 2)
            def _():
                send_rows(slot, slot + 2, 1).start()

            @pl.when(slot == last - 2)
            def _():
                send_part(slot, 0, 1).start()

            send_rows(0, slot + 1, -1).wait_recv()

            @pl.when(slot < last - 2)
            def _():
                send_rows(slot + 1, slot + 3, -1).start()

            @pl.when(slot == last - 2)
            def _():
                send_part(slot + 1, 1, -1).start()

            send_low(0, slot, 1).wait_recv()
            send_low(slot, slot + 2, 1).start()
            send_low(0, slot + 1, -1).wait_recv()

            @pl.when(slot < last - 2)
            def _():
                send_low(slot + 1, slot + 3, -1).start()

        @pl.when(slot == last)
        def _():
            send_part(0, 0, 1).wait_recv()
            send_part(0, 1, -1).wait_recv()
            send_low(0, last, 1).wait_recv()

        distance = (slot + 1) // 2 * (1 - 2 * (slot % 2))
        owner = at_spot(distance)
        prompt = prompts[owner]
        length = lengths[prompt]
        wanted_row = rows_wanted[my_req * count + owner]
        up_one = up_all[
            (my_req - wanted_row // table_rows + req_count) % req_count, wanted_row % table_rows
        ]
        row_block = rows[slot]
        low_block = low[slot]
        visible = cached_at < length
        parts = []
        for head in range(heads):
            base = jnp.dot(
                row_block,
                wide[:, head * 256 : head * 256 + 256],
                preferred_element_type=jnp.float32,
            )
            up_head = up_one[:, head * 128 : head * 128 + 128]
            zero = jnp.zeros_like(up_head)
            extra_query = lax.dot_general(
                low_block,
                jnp.where(is_query, up_head, zero),
                by_rank,
                preferred_element_type=jnp.float32,
            )
            extra_kv = lax.dot_general(
                low_block,
                jnp.where(is_kv, up_head, zero),
                by_rank,
                preferred_element_type=jnp.float32,
            )
            query = jnp.where(front, base[:, :128], 0.0) + adapter_scale * extra_query
            query = query.astype(jnp.bfloat16)
            query = query * jnp.bfloat16(att_scale)
            own = (base[:, 128:] + adapter_scale * extra_kv).astype(jnp.bfloat16)
            cached = cache_ref[prompt, head]
            pre_scores = lax.dot_general(
                query, cached, contract, preferred_element_type=jnp.float32
            )
            own_scores = lax.dot_general(query, own, contract, preferred_element_type=jnp.float32)
            pre_scores = jnp.where(visible, pre_scores, masked_score)
            own_scores = jnp.where(causal, own_scores, masked_score)
            row_peak = jnp.maximum(
                jnp.max(pre_scores, axis=-1, keepdims=True),
                jnp.max(own_scores, axis=-1, keepdims=True),
            )
            pre_exp = jnp.exp(pre_scores - row_peak)
            own_exp = jnp.exp(own_scores - row_peak)
            denominator = jnp.sum(pre_exp, axis=-1, keepdims=True) + jnp.sum(
                own_exp, axis=-1, keepdims=True
            )
            total = jnp.dot(
                pre_exp.astype(jnp.bfloat16), cached, preferred_element_type=jnp.float32
            )
            total = total + jnp.dot(
                own_exp.astype(jnp.bfloat16), own, preferred_element_type=jnp.float32
            )
            parts.append((total / denominator)[:, HEAD_WIDTH:])
        joined = parts[0] if heads == 1 else jnp.concatenate(parts, axis=1)
        att_out[slot] = joined.astype(jnp.bfloat16)

        @pl.when(slot > 0)
        def _():
            send_att(slot).start()

        return carry

    lax.fori_loop(0, count, process, 0)

    out_ref[my_exp] = att_out[0]
    for slot in range(1, count):
        send_att(slot).wait_recv()
        distance = (slot + 1) // 2 * (2 * (slot % 2) - 1)
        out_ref[at_spot(distance)] = att_in[slot]
    for slot in range(1, last):
        send_rows(0, slot, 1).wait_send()
    send_part(0, 0, 1).wait_send()
    send_part(0, 1, -1).wait_send()
    for slot in range(1, count):
        send_low(0, slot, 1).wait_send()
        send_att(slot).wait_send()
    for step in range(1, req_count):
        send_down(step).wait_send()
        send_narrow(step).wait_send()
        send_up(step).wait_send()


def attend(tokens, gain, weight, cache, down, lift, narrow, up, prompts, lengths, rows_wanted):
    count = lax.axis_size("exp")
    req_count = lax.axis_size("req")
    _, seq, width = tokens.shape
    heads = cache.shape[1]
    wide = heads * HEAD_WIDTH
    rank = down.shape[1]
    packed = (req_count, rank + lift.shape[1], width)
    smem = pl.BlockSpec(memory_space=pltpu.SMEM)
    vmem = pl.BlockSpec(memory_space=pltpu.VMEM)
    dma = pltpu.SemaphoreType.DMA
    return pl.pallas_call(
        functools.partial(layer_kernel, (count, req_count, heads)),
        out_shape=(
            jax.ShapeDtypeStruct((count, seq, wide), jnp.bfloat16),
            jax.ShapeDtypeStruct(lift.shape[1:], jnp.bfloat16),
            jax.ShapeDtypeStruct(narrow.shape[1:], jnp.bfloat16),
        ),
        in_specs=[smem] * 3 + [vmem] * 8,
        out_specs=(vmem, vmem, vmem),
        scratch_shapes=[
            pltpu.VMEM((width, heads * 256), jnp.bfloat16),
            pltpu.VMEM((count, seq, width), jnp.bfloat16),
            pltpu.VMEM((count, rank, seq), jnp.bfloat16),
            pltpu.VMEM((count, seq, wide), jnp.bfloat16),
            pltpu.VMEM((count, seq, wide), jnp.bfloat16),
            pltpu.VMEM(packed, jnp.bfloat16),
            pltpu.VMEM(packed, jnp.bfloat16),
            pltpu.VMEM((req_count,) + narrow.shape[1:], jnp.bfloat16),
            pltpu.VMEM((req_count,) + narrow.shape[1:], jnp.bfloat16),
            pltpu.VMEM((req_count,) + up.shape, jnp.bfloat16),
            dma((count + 1,)),
            dma((count + 1,)),
            dma((count,)),
            dma((count,)),
            dma((count,)),
            dma((count,)),
            dma((req_count,)),
            dma((req_count,)),
            dma((req_count,)),
            dma((req_count,)),
            dma((req_count,)),
            dma((req_count,)),
        ],
        compiler_params=pltpu.CompilerParams(
            collective_id=0, has_side_effects=True, vmem_limit_bytes=52 * 1024 * 1024
        ),
        name="attend",
    )(prompts, lengths, rows_wanted, tokens, gain, weight, cache, down, lift, narrow, up)


def block_kernel(
    prompts,
    lengths,
    adapters,
    slot_rows,
    tokens_ref,
    gain_ref,
    weight_ref,
    cache_ref,
    down_ref,
    lift_ref,
    narrow_ref,
    up_ref,
    out_ref,
    lift_out_ref,
    narrow_out_ref,
    wide_own,
    wide_far,
    keys_own,
    keys_far,
    rows,
    low,
    far_qkv,
    att_out,
    att_in,
    staging,
    offered,
    staging_lift,
    offered_lift,
    staging_narrow,
    offered_narrow,
    up_all,
    up_stage,
    up_far,
    weight_far,
    cache_stage,
    cache_far,
    row_send,
    row_recv,
    low_send,
    low_recv,
    att_send,
    att_recv,
    down_send,
    down_recv,
    lift_send,
    lift_recv,
    narrow_send,
    narrow_recv,
    up_send,
    up_recv,
    far_send,
    far_recv,
    across_send,
    across_recv,
    core_send,
    core_recv,
):
    count, req_count, prompt_rows = 8, 4, 2 * 1024
    seq = tokens_ref.shape[1]
    mid = seq // 2
    table_rows = down_ref.shape[0]
    rank = 3 * ADAPTER_RANK
    my_req = lax.axis_index("req")
    my_exp = lax.axis_index("exp")
    half = my_exp // 4
    my_y = my_exp % 2
    my_z = (my_exp // 2) % 2
    far_exp = (1 - half) * 4 + (1 - my_z) * 2 + my_y
    core_req = my_req + 1 - 2 * (my_req % 2)
    across_req = (my_req + 2) % req_count

    def at_slot(slot):
        return half * 4 + ((my_z + slot // 2) % 2) * 2 + (my_y + slot) % 2

    def mirrored(slot):
        return (1 - half) * 4 + ((my_z + slot // 2 + 1) % 2) * 2 + (my_y + slot) % 2

    def at_req(offset):
        return (my_req + offset) % req_count

    def row_of(request):
        return slot_rows[adapters[request]]

    def remote(source, target, sem_send, sem_recv, device):
        return pltpu.make_async_remote_copy(
            src_ref=source,
            dst_ref=target,
            send_sem=sem_send,
            recv_sem=sem_recv,
            device_id=device,
            device_id_type=MESH,
        )

    barrier = pltpu.get_barrier_semaphore()
    for slot in range(1, 4):
        pl.semaphore_signal(barrier, inc=1, device_id=(my_req, at_slot(slot)), device_id_type=MESH)
    pl.semaphore_signal(barrier, inc=1, device_id=(my_req, far_exp), device_id_type=MESH)
    for step in range(1, req_count):
        pl.semaphore_signal(barrier, inc=1, device_id=(at_req(step), my_exp), device_id_type=MESH)

    for step in range(req_count):
        row = row_of(at_req(step) * count + my_exp) % table_rows
        staging[step] = down_ref[row]
        staging_lift[step] = lift_ref[row]
        staging_narrow[step] = narrow_ref[row]
    offered[0] = staging[0]
    offered_lift[0] = staging_lift[0]
    offered_narrow[0] = staging_narrow[0]
    up_all[0] = up_ref[...]
    widened = tokens_ref[0].astype(jnp.float32)
    factor = lax.rsqrt(jnp.mean(widened * widened, axis=-1, keepdims=True) + norm_eps)
    rows[0] = (widened * factor * gain_ref[...]).astype(jnp.bfloat16)
    wq = weight_ref.shape[0] // req_count
    quarter = cache_stage.shape[0]
    third = quarter // 3
    granule = 32
    blocks = 1024 // granule
    ends = []
    total = 0
    for prompt in range(4):
        total = total + (lengths[prompt] + granule - 1) // granule
        ends.append(total)
    starts = [0] + ends[:3]

    def source_of(index):
        prompt = 0
        begin = 0
        for p in range(1, 4):
            past = index >= starts[p]
            prompt = jnp.where(past, p, prompt)
            begin = jnp.where(past, starts[p], begin)
        return prompt * blocks + jnp.minimum(index - begin, blocks - 1)

    def stage(index, carry):
        source = source_of(my_req * quarter + index)
        cache_stage[index] = cache_ref[source]
        return carry

    lax.fori_loop(0, quarter, stage, 0)
    pl.semaphore_wait(barrier, 7)

    def send_row_y():
        return remote(
            rows.at[0], rows.at[1], row_send.at[0], row_recv.at[0], (my_req, at_slot(1))
        )

    def send_row_z():
        return remote(
            rows.at[0], rows.at[2], row_send.at[1], row_recv.at[1], (my_req, at_slot(2))
        )

    def send_row_on():
        return remote(
            rows.at[2], rows.at[3], row_send.at[2], row_recv.at[2], (my_req, at_slot(1))
        )

    def send_low(slot):
        return remote(
            low.at[0], low.at[slot], low_send.at[slot], low_recv.at[slot], (my_req, at_slot(slot))
        )

    def send_att(kind, slot):
        return remote(
            att_out.at[kind, slot],
            att_in.at[kind, slot],
            att_send.at[kind, slot],
            att_recv.at[kind, slot],
            (my_req, at_slot(slot)),
        )

    def to_req(source, target, sem_send, sem_recv, step):
        return remote(
            source, target, sem_send.at[step], sem_recv.at[step], (at_req(step), my_exp)
        )

    def send_down(step):
        return to_req(staging.at[step], offered.at[step], down_send, down_recv, step)

    def send_lift(step):
        return to_req(staging_lift.at[step], offered_lift.at[step], lift_send, lift_recv, step)

    def send_narrow(step):
        return to_req(
            staging_narrow.at[step], offered_narrow.at[step], narrow_send, narrow_recv, step
        )

    def send_up(step):
        return to_req(up_ref, up_all.at[step], up_send, up_recv, step)

    def send_up_far():
        return remote(up_stage, up_far, far_send.at[4], far_recv.at[4], (my_req, far_exp))

    def piece(owner, part):
        if part == 0:
            return weight_far.at[pl.ds(pl.multiple_of(owner * wq, 32), wq)]
        return cache_far.at[pl.ds(owner * quarter + (part - 1) * third, third)]

    def send_far(part):
        if part == 0:
            source = weight_ref.at[pl.ds(pl.multiple_of(my_req * wq, 32), wq)]
        else:
            source = cache_stage.at[pl.ds((part - 1) * third, third)]
        return remote(
            source,
            piece(my_req, part),
            far_send.at[part],
            far_recv.at[part],
            (my_req, far_exp),
        )

    def send_across(part):
        return remote(
            piece(my_req, part),
            piece(my_req, part),
            across_send.at[part],
            across_recv.at[part],
            (across_req, my_exp),
        )

    def take_across(part):
        return remote(
            piece(across_req, part),
            piece(across_req, part),
            across_send.at[part],
            across_recv.at[part],
            (across_req, my_exp),
        )

    def send_core(kind, part):
        owner = my_req if kind == 0 else across_req
        return remote(
            piece(owner, part),
            piece(owner, part),
            core_send.at[kind, part],
            core_recv.at[kind, part],
            (core_req, my_exp),
        )

    def take_core(kind, part):
        owner = core_req if kind == 0 else (core_req + 2) % req_count
        return remote(
            piece(owner, part),
            piece(owner, part),
            core_send.at[kind, part],
            core_recv.at[kind, part],
            (core_req, my_exp),
        )

    def pass_far(part):
        send_far(part).wait_recv()
        send_across(part).start()
        send_core(0, part).start()

    def pass_across(part):
        take_across(part).wait_recv()
        send_core(1, part).start()

    outer = my_z == half
    inner = my_z != half
    send_row_z().start()
    send_row_y().start()
    for step in range(1, req_count):
        send_down(step).start()
    for step in range(1, req_count):
        send_up(step).start()

    @pl.when(inner)
    def _():
        for part in range(4):
            send_far(part).start()

    top = lax.broadcasted_iota(jnp.int32, (128, 1), 0) < HEAD_WIDTH

    def widen(source_ref, target_ref):
        for head in range(2):
            block = source_ref[head * 192 : head * 192 + 128]
            block = jnp.where(top, block, jnp.zeros_like(block))
            target_ref[:, head * 128 : head * 128 + 128] = block.T
            target_ref[:, 256 + head * 128 : 384 + head * 128] = source_ref[
                head * 192 + 64 : head * 192 + 192
            ].T

    row_kind = lax.broadcasted_iota(jnp.int32, (256, 128), 0) % 2
    first_rows = (row_kind == 0).astype(jnp.bfloat16)
    second_rows = (row_kind == 1).astype(jnp.bfloat16)

    def own_keys(index, carry):
        block = cache_ref[pl.ds(index * 4, 4)].reshape(256, 128)
        at = pl.ds(pl.multiple_of(index % 8 * 256, 256), 256)
        keys_own[index // 8, at, :128] = block * first_rows
        keys_own[index // 8, at, 128:] = block * second_rows
        return carry

    widen(weight_ref, wide_own)
    lax.fori_loop(0, 32, own_keys, 0)

    for step in range(1, req_count):
        send_down(step).wait_recv()
    own_row = row_of(my_req * count + my_exp)
    source = (my_req - own_row // table_rows + req_count) % req_count
    contract = (((1,), (1,)), ((), ()))
    low[0] = lax.dot_general(
        offered[source], rows[0], contract, preferred_element_type=jnp.float32
    ).astype(jnp.bfloat16)
    for slot in range(1, 4):
        send_low(slot).start()

    for step in range(1, req_count):
        send_up(step).wait_recv()

    def up_of(request):
        row = row_of(request)
        return up_all[(my_req - row // table_rows + req_count) % req_count, row % table_rows]

    for index in range(4):
        up_stage[index] = up_of(my_req * count + (1 - half) * 4 + index)
    send_up_far().start()
    for step in range(1, req_count):
        send_lift(step).start()
        send_narrow(step).start()

    @pl.when(inner)
    def _():
        pass_far(0)


    column = lax.broadcasted_iota(jnp.int32, (128, 512), 1)
    lane = lax.broadcasted_iota(jnp.int32, (128, 512), 0)
    spread = (lane == (column // 128 % 2) * HEAD_WIDTH + column % HEAD_WIDTH).astype(jnp.bfloat16)
    column = lax.broadcasted_iota(jnp.int32, (rank, 512), 1)
    kind = lax.broadcasted_iota(jnp.int32, (rank, 512), 0) // ADAPTER_RANK
    back = column % 128 // HEAD_WIDTH
    kept = kind == jnp.where(column < 256, 3 * back, 1 + back)
    by_rank = (((0,), (0,)), ((), ()))
    causal = lax.broadcasted_iota(jnp.int32, (seq, seq), 0) >= lax.broadcasted_iota(
        jnp.int32, (seq, seq), 1
    )
    cached_at = lax.broadcasted_iota(jnp.int32, (1, prompt_rows), 1)
    even = lax.broadcasted_iota(jnp.int32, (1, 128), 1) % 2 == 0
    att_scale = HEAD_WIDTH ** (-0.5)

    def project(slot, wide_ref, up_one):
        base = jnp.dot(rows[slot], wide_ref[...], preferred_element_type=jnp.float32)
        up_wide = jnp.dot(up_one, spread, preferred_element_type=jnp.float32)
        up_wide = jnp.where(kept, up_wide, 0.0).astype(jnp.bfloat16)
        extra = lax.dot_general(low[slot], up_wide, by_rank, preferred_element_type=jnp.float32)
        return (base + adapter_scale * extra).astype(jnp.bfloat16)

    def attention(qkv, keys, length):
        query = qkv[:, :256] * jnp.bfloat16(att_scale)
        scores = lax.dot_general(query, keys, contract, preferred_element_type=jnp.float32)
        scores = jnp.where(cached_at < 2 * length, scores, masked_score)
        own_scores = []
        for head in range(2):
            at = slice(head * 128, head * 128 + 128)
            own = qkv[:, 256 + head * 128 : 384 + head * 128]
            one = lax.dot_general(query[:, at], own, contract, preferred_element_type=jnp.float32)
            own_scores.append(jnp.where(causal, one, masked_score))
        tiles = prompt_rows // 128
        most = scores[:, :128]
        for tile in range(1, tiles):
            most = jnp.maximum(most, scores[:, tile * 128 : tile * 128 + 128])
        peaks = []
        for head in range(2):
            mine = even if head == 0 else jnp.logical_not(even)
            peaks.append(
                jnp.maximum(
                    jnp.max(jnp.where(mine, most, masked_score), axis=-1, keepdims=True),
                    jnp.max(own_scores[head], axis=-1, keepdims=True),
                )
            )
        peak = jnp.where(even, peaks[0], peaks[1])
        weights = []
        summed = jnp.zeros((seq, 128), jnp.float32)
        for tile in range(tiles):
            one = jnp.exp(scores[:, tile * 128 : tile * 128 + 128] - peak)
            summed = summed + one
            weights.append(one.astype(jnp.bfloat16))
        total = jnp.dot(
            jnp.concatenate(weights, axis=1), keys, preferred_element_type=jnp.float32
        )
        parts = []
        for head in range(2):
            mine = even if head == 0 else jnp.logical_not(even)
            own = qkv[:, 256 + head * 128 : 384 + head * 128]
            own_exp = jnp.exp(own_scores[head] - peaks[head])
            denominator = jnp.sum(
                jnp.where(mine, summed, 0.0), axis=-1, keepdims=True
            ) + jnp.sum(own_exp, axis=-1, keepdims=True)
            both = total[:, head * 128 : head * 128 + 128] + jnp.dot(
                own_exp.astype(jnp.bfloat16), own, preferred_element_type=jnp.float32
            )
            parts.append((both / denominator)[:, HEAD_WIDTH:])
        return jnp.concatenate(parts, axis=1).astype(jnp.bfloat16)

    def own_heads(slot, carry):
        @pl.when(slot == 1)
        def _():
            send_row_z().wait_recv()
            send_row_on().start()

            @pl.when(outer)
            def _():
                send_row_z().wait_send()
                for part in range(4):
                    send_far(part).start()

            @pl.when(inner)
            def _():
                pass_far(1)
                pass_across(0)

            send_row_y().wait_recv()
            send_low(1).wait_recv()

        @pl.when(slot == 2)
        def _():
            send_low(2).wait_recv()

            @pl.when(inner)
            def _():
                pass_far(2)
                pass_far(3)
                pass_across(1)

        @pl.when(slot == 3)
        def _():
            @pl.when(outer)
            def _():
                pass_far(0)
                pass_far(1)
                pass_across(0)
                pass_far(2)

            send_row_on().wait_recv()
            send_low(3).wait_recv()

            @pl.when(inner)
            def _():
                pass_across(2)

        owner = at_slot(slot)
        prompt = prompts[owner]
        qkv = project(slot, wide_own, up_of(my_req * count + owner))
        att_out[0, slot] = attention(qkv, keys_own[prompt], lengths[prompt])

        @pl.when(slot > 0)
        def _():
            send_att(0, slot).start()

        return carry

    lax.fori_loop(0, 4, own_heads, 0)

    @pl.when(outer)
    def _():
        pass_far(3)
        pass_across(1)
        pass_across(2)

    take_core(0, 0).wait_recv()
    take_core(1, 0).wait_recv()
    send_up_far().wait_recv()
    widen(weight_far, wide_far)

    def far_project(slot, carry):
        index = ((my_z + slot // 2) % 2) * 2 + (my_y + slot) % 2
        far_qkv[slot] = project(slot, wide_far, up_far[index])
        return carry

    lax.fori_loop(0, 4, far_project, 0)

    pass_across(3)

    for part in range(1, 4):
        take_core(0, part).wait_recv()
        take_core(1, part).wait_recv()

    def unpack(index, carry):
        for prompt in range(4):
            for lane in range(4):
                block = cache_far[jnp.minimum(starts[prompt] + index * 4 + lane, 4 * quarter - 1)]
                at = pl.ds(pl.multiple_of(index * 256 + lane * 64, 64), 64)
                keys_far[prompt, at, :128] = block * first_rows[:64]
                keys_far[prompt, at, 128:] = block * second_rows[:64]
        return carry

    lax.fori_loop(0, blocks // 4, unpack, 0)

    def far_keys(slot):
        prompt = prompts[at_slot(slot)]
        return keys_far[prompt], lengths[prompt]

    def far_heads(step, carry):
        first, second = 3 - 2 * step, 2 - 2 * step
        att_first = attention(far_qkv[first], *far_keys(first))
        att_second = attention(far_qkv[second], *far_keys(second))
        att_out[1, first] = att_first
        att_out[1, second] = att_second
        send_att(1, first).start()

        @pl.when(second > 0)
        def _():
            send_att(1, second).start()

        return carry

    lax.fori_loop(0, 2, far_heads, 0)

    for step in range(1, req_count):
        send_lift(step).wait_recv()
        send_narrow(step).wait_recv()
    lift_out_ref[...] = offered_lift[source]
    narrow_out_ref[...] = offered_narrow[source]
    for kind in range(2):
        for slot in range(4):
            if slot > 0:
                send_att(kind, slot).wait_recv()
            at = pl.ds(pl.multiple_of((at_slot(slot) if kind == 0 else mirrored(slot)) * 128, 128), 128)
            out_ref[:, at] = att_out[kind, 0] if slot == 0 else att_in[kind, slot]

    send_row_y().wait_send()
    send_row_on().wait_send()

    @pl.when(inner)
    def _():
        send_row_z().wait_send()

    for slot in range(1, 4):
        send_low(slot).wait_send()
        for kind in range(2):
            send_att(kind, slot).wait_send()
    for step in range(1, req_count):
        send_down(step).wait_send()
        send_lift(step).wait_send()
        send_narrow(step).wait_send()
        send_up(step).wait_send()
    send_up_far().wait_send()
    for part in range(4):
        send_far(part).wait_send()
    for part in range(4):
        send_across(part).wait_send()
        send_core(0, part).wait_send()
        send_core(1, part).wait_send()


def attend_block(
    tokens, gain, weight, cache, down, lift, narrow, up, prompts, lengths, adapters, slot_rows
):
    _, seq, width = tokens.shape
    rank = down.shape[1]
    smem = pl.BlockSpec(memory_space=pltpu.SMEM)
    vmem = pl.BlockSpec(memory_space=pltpu.VMEM)
    dma = pltpu.SemaphoreType.DMA

    def bf16(*shape):
        return pltpu.VMEM(shape, jnp.bfloat16)

    return pl.pallas_call(
        block_kernel,
        out_shape=(
            jax.ShapeDtypeStruct((seq, width), jnp.bfloat16),
            jax.ShapeDtypeStruct(lift.shape[1:], jnp.bfloat16),
            jax.ShapeDtypeStruct(narrow.shape[1:], jnp.bfloat16),
        ),
        in_specs=[smem] * 4 + [vmem] * 8,
        out_specs=(vmem, vmem, vmem),
        scratch_shapes=[
            bf16(width, 512),
            bf16(width, 512),
            bf16(4, 2048, 256),
            bf16(4, 2048, 256),
            bf16(4, seq, width),
            bf16(4, rank, seq),
            bf16(4, seq, 512),
            bf16(2, 4, seq, 128),
            bf16(2, 4, seq, 128),
            bf16(4, rank, width),
            bf16(4, rank, width),
            bf16(4, *lift.shape[1:]),
            bf16(4, *lift.shape[1:]),
            bf16(4, *narrow.shape[1:]),
            bf16(4, *narrow.shape[1:]),
            bf16(4, *up.shape),
            bf16(4, *up.shape[1:]),
            bf16(4, *up.shape[1:]),
            bf16(*weight.shape),
            bf16(21, *cache.shape[1:]),
            bf16(84, *cache.shape[1:]),
            dma((5,)),
            dma((5,)),
            dma((4,)),
            dma((4,)),
            dma((2, 4)),
            dma((2, 4)),
            dma((4,)),
            dma((4,)),
            dma((4,)),
            dma((4,)),
            dma((4,)),
            dma((4,)),
            dma((4,)),
            dma((4,)),
            dma((5,)),
            dma((5,)),
            dma((4,)),
            dma((4,)),
            dma((2, 4)),
            dma((2, 4)),
        ],
        compiler_params=pltpu.CompilerParams(
            collective_id=2, has_side_effects=True, vmem_limit_bytes=56 * 1024 * 1024
        ),
        name="attend_block",
    )(
        prompts,
        lengths,
        adapters,
        slot_rows,
        tokens,
        gain,
        weight,
        cache,
        down,
        lift,
        narrow,
        up,
    )


def expert_kernel(
    count,
    outgoing_ref,
    gate_up_hbm,
    down_hbm,
    out_ref,
    gate_up,
    down,
    inbox,
    outbox,
    back,
    weight_sem,
    there_send,
    there_recv,
    back_send,
    back_recv,
):
    my_req = lax.axis_index("req")
    my_exp = lax.axis_index("exp")
    load_gate_up = pltpu.make_async_copy(gate_up_hbm.at[0], gate_up, weight_sem.at[0])
    load_down = pltpu.make_async_copy(down_hbm.at[0], down, weight_sem.at[1])
    load_gate_up.start()
    load_down.start()

    def at_exp(offset):
        return (my_exp + offset + count) % count

    barrier = pltpu.get_barrier_semaphore()
    for step in range(1, count):
        pl.semaphore_signal(barrier, inc=1, device_id=(my_req, at_exp(step)), device_id_type=MESH)
    inbox[0] = outgoing_ref[my_exp]
    pl.semaphore_wait(barrier, count - 1)

    def send_there(step):
        return pltpu.make_async_remote_copy(
            src_ref=outgoing_ref.at[at_exp(step)],
            dst_ref=inbox.at[step],
            send_sem=there_send.at[step],
            recv_sem=there_recv.at[step],
            device_id=(my_req, at_exp(step)),
            device_id_type=MESH,
        )

    def send_back(step):
        return pltpu.make_async_remote_copy(
            src_ref=outbox.at[step],
            dst_ref=back.at[step],
            send_sem=back_send.at[step],
            recv_sem=back_recv.at[step],
            device_id=(my_req, at_exp(-step)),
            device_id_type=MESH,
        )

    for step in range(1, count):
        send_there(step).start()
    load_gate_up.wait()
    load_down.wait()
    cap, width = inbox.shape[1:]
    chunk = FF // 2

    def process(pair, carry):
        @pl.when(pair > 0)
        def _():
            send_there(2 * pair).wait_recv()

        send_there(2 * pair + 1).wait_recv()
        received = inbox[pl.ds(2 * pair, 2)].reshape(2 * cap, width)
        total = jnp.zeros((2 * cap, width), jnp.float32)
        for part in range(2):
            gate = jnp.dot(
                received,
                gate_up[:, part * chunk : (part + 1) * chunk],
                preferred_element_type=jnp.float32,
            )
            up = jnp.dot(
                received,
                gate_up[:, FF + part * chunk : FF + (part + 1) * chunk],
                preferred_element_type=jnp.float32,
            )
            activated = (jax.nn.gelu(gate, approximate=True) * up).astype(jnp.bfloat16)
            total = total + jnp.dot(
                activated,
                down[part * chunk : (part + 1) * chunk],
                preferred_element_type=jnp.float32,
            )
        outbox[pl.ds(2 * pair, 2)] = total.reshape(2, cap, width).astype(jnp.bfloat16)

        @pl.when(pair > 0)
        def _():
            send_back(2 * pair).start()

        send_back(2 * pair + 1).start()
        return carry

    lax.fori_loop(0, count // 2, process, 0)
    out_ref[my_exp] = outbox[0]
    for step in range(1, count):
        send_back(step).wait_recv()
        out_ref[at_exp(step)] = back[step]
    for step in range(1, count):
        send_there(step).wait_send()
        send_back(step).wait_send()


def run_experts(outgoing, gate_up, down):
    count, cap, width = outgoing.shape
    vmem = pl.BlockSpec(memory_space=pltpu.VMEM)
    hbm = pl.BlockSpec(memory_space=pl.ANY)
    dma = pltpu.SemaphoreType.DMA
    block = pltpu.VMEM(outgoing.shape, jnp.bfloat16)
    return pl.pallas_call(
        functools.partial(expert_kernel, count),
        out_shape=jax.ShapeDtypeStruct(outgoing.shape, jnp.bfloat16),
        in_specs=[vmem, hbm, hbm],
        out_specs=vmem,
        scratch_shapes=[
            pltpu.VMEM(gate_up.shape[1:], jnp.bfloat16),
            pltpu.VMEM(down.shape[1:], jnp.bfloat16),
            block,
            block,
            block,
            dma((2,)),
            dma((count,)),
            dma((count,)),
            dma((count,)),
            dma((count,)),
        ],
        compiler_params=pltpu.CompilerParams(
            collective_id=1, has_side_effects=True, vmem_limit_bytes=52 * 1024 * 1024
        ),
        name="experts",
    )(outgoing, gate_up, down)


def body(
    tokens,
    attention_norm_gain,
    expert_norm_gain,
    query_key_value_weight,
    output_weight,
    prompt_key_value_cache,
    shared_prompt_length,
    prompt_per_request,
    adapter_per_request,
    adapter_slot_rows,
    adapter_down_qkv,
    adapter_up_qkv,
    adapter_down_output,
    adapter_up_output,
    router_weight,
    expert_gate_up_weight,
    expert_down_weight,
    routes,
    slots,
):
    heads_here = query_key_value_weight.shape[1]
    seq_whole = tokens.shape[1]
    table_rows = adapter_down_qkv.shape[0]
    count = lax.axis_size("exp")
    narrow = jnp.swapaxes(adapter_down_output, 2, 3).reshape(table_rows, -1, HEAD_WIDTH)
    if (count, lax.axis_size("req"), heads_here) == (8, 4, 2):
        flat_att, own_bo, own_ao = attend_block(
            tokens,
            attention_norm_gain[None],
            jnp.transpose(query_key_value_weight, (1, 2, 0)).reshape(-1, MODEL_WIDTH),
            prompt_key_value_cache.reshape(-1, 64, 2 * HEAD_WIDTH),
            jnp.swapaxes(adapter_down_qkv, 1, 2),
            adapter_up_output,
            narrow,
            adapter_up_qkv.reshape(table_rows, 3 * ADAPTER_RANK, heads_here * HEAD_WIDTH),
            prompt_per_request,
            shared_prompt_length,
            adapter_per_request,
            adapter_slot_rows,
        )
    else:
        up_twice = jnp.concatenate([adapter_up_qkv, adapter_up_qkv], axis=-1).reshape(
            table_rows, 3 * ADAPTER_RANK, heads_here * 2 * HEAD_WIDTH
        )
        gathered, own_bo, own_ao = attend(
            tokens,
            attention_norm_gain[None],
            jnp.transpose(query_key_value_weight, (1, 2, 0)),
            jnp.swapaxes(prompt_key_value_cache, 1, 2),
            jnp.swapaxes(adapter_down_qkv, 1, 2),
            adapter_up_output,
            narrow,
            up_twice,
            prompt_per_request,
            shared_prompt_length,
            adapter_slot_rows[adapter_per_request],
        )
        flat_att = jnp.swapaxes(gathered, 0, 1).reshape(seq_whole, -1)
    plain_out = jnp.dot(
        flat_att, output_weight.reshape(-1, MODEL_WIDTH), preferred_element_type=jnp.float32
    )
    own_ao = jnp.swapaxes(own_ao.reshape(-1, ADAPTER_RANK, HEAD_WIDTH), 1, 2)
    low_out = jnp.dot(
        flat_att, own_ao.reshape(-1, ADAPTER_RANK), preferred_element_type=jnp.float32
    )
    surplus = lax.dot_general(
        low_out,
        own_bo.astype(jnp.float32),
        (((1,), (0,)), ((), ())),
        precision=lax.Precision.HIGHEST,
    )
    projected_rows = (plain_out + adapter_scale * surplus)[None]
    hidden = (tokens.astype(jnp.float32) + projected_rows).astype(jnp.bfloat16)
    moe_in = rms_norm(hidden, expert_norm_gain)
    rows_here = REQ_DEV * seq_whole
    flat_in = moe_in.reshape(rows_here, MODEL_WIDTH)
    gate_vals = jax.nn.sigmoid(jnp.dot(flat_in, router_weight, preferred_element_type=jnp.float32))
    expert_count = router_weight.shape[1]
    capacity = 5 * rows_here * TOP // (4 * expert_count)
    route_flat = routes.reshape(rows_here, TOP)
    slot_flat = slots.reshape(rows_here, TOP)
    target = jnp.where(slot_flat >= 0, route_flat * capacity + slot_flat, -1)
    cells = jnp.arange(expert_count * capacity, dtype=jnp.int32)
    matched = target[:, :, None] == cells[None, None, :]
    named = route_flat[:, :, None] == jnp.arange(expert_count, dtype=jnp.int32)[None, None, :]
    chosen_gate = jnp.sum(jnp.where(named, gate_vals[:, None, :], 0.0), axis=2)
    combine = jnp.sum(jnp.where(matched, chosen_gate[:, :, None], 0.0), axis=1)
    sending = jnp.any(matched, axis=1).astype(jnp.bfloat16)
    outgoing = jnp.einsum("rc,rd->cd", sending, flat_in, preferred_element_type=jnp.float32).astype(
        jnp.bfloat16
    )
    returned = run_experts(
        outgoing.reshape(expert_count, capacity, MODEL_WIDTH),
        expert_gate_up_weight,
        expert_down_weight,
    )
    returned_wide = returned.reshape(expert_count * capacity, MODEL_WIDTH).astype(jnp.float32)
    moe_sum = jnp.dot(combine, returned_wide, precision=lax.Precision.HIGHEST)
    mixed = (hidden.reshape(rows_here, MODEL_WIDTH).astype(jnp.float32) + moe_sum).astype(
        jnp.bfloat16
    )
    return mixed.reshape(tokens.shape)


def solution(mesh):
    in_specs = (
        P(("req", "exp"), None, None),
        P(),
        P(),
        P(None, "exp", None),
        P(),
        P(None, None, "exp", None),
        P(),
        P("req"),
        P(),
        P(),
        P("req", None, None),
        P("req", None, None, "exp", None),
        P("req", None, None, None),
        P("req", None, None),
        P(),
        P("exp", None, None),
        P("exp", None, None),
        P(("req", "exp"), None, None),
        P(("req", "exp"), None, None),
    )
    out_specs = P(("req", "exp"), None, None)
    return jax.shard_map(body, mesh=mesh, in_specs=in_specs, out_specs=out_specs, check_vma=False)
```

```python
import functools

import jax
import jax.numpy as jnp
from jax import lax
from jax.experimental import pallas as pl
from jax.experimental.pallas import tpu as pltpu
from jax.sharding import PartitionSpec as P

MODEL_WIDTH = 1024
HEAD_WIDTH = 64
FF = 2816
ADAPTER_RANK = 16
TOP = 2
REQ_DEV = 1


adapter_scale = 0.5
norm_eps = 1e-06
MESH = pl.DeviceIdType.MESH
masked_score = -1e30


def rms_norm(values, gain):
    widened = values.astype(jnp.float32)
    factor = lax.rsqrt(jnp.mean(widened * widened, axis=-1, keepdims=True) + norm_eps)
    return (widened * factor * gain).astype(jnp.bfloat16)


def ring_device(spot, count):
    turned = spot // (count // 2)
    return 2 * (spot + turned * (count - 1 - 2 * spot)) + turned


def layer_kernel(
    sizes,
    prompts,
    lengths,
    rows_wanted,
    tokens_ref,
    gain_ref,
    weight_ref,
    cache_ref,
    down_ref,
    lift_ref,
    narrow_ref,
    up_ref,
    out_ref,
    lift_out_ref,
    narrow_out_ref,
    wide,
    rows,
    low,
    att_out,
    att_in,
    staging,
    offered,
    staging_narrow,
    offered_narrow,
    up_all,
    row_send,
    row_recv,
    low_send,
    low_recv,
    att_send,
    att_recv,
    down_send,
    down_recv,
    narrow_send,
    narrow_recv,
    up_send,
    up_recv,
):
    count, req_count, heads = sizes
    half = count // 2
    last = count - 1
    seq = tokens_ref.shape[1]
    mid = seq // 2
    table_rows = down_ref.shape[0]
    rank = 3 * ADAPTER_RANK
    my_req = lax.axis_index("req")
    my_exp = lax.axis_index("exp")
    my_side = my_exp % 2
    my_spot = my_exp // 2 + my_side * (count - 1 - 2 * (my_exp // 2))

    def at_spot(offset):
        return ring_device((my_spot + offset + count) % count, count)

    def at_req(offset):
        return (my_req + offset) % req_count

    barrier = pltpu.get_barrier_semaphore()
    for step in range(1, count):
        pl.semaphore_signal(barrier, inc=1, device_id=(my_req, at_spot(step)), device_id_type=MESH)
    for step in range(1, req_count):
        pl.semaphore_signal(barrier, inc=1, device_id=(at_req(step), my_exp), device_id_type=MESH)

    widened = tokens_ref[0].astype(jnp.float32)
    factor = lax.rsqrt(jnp.mean(widened * widened, axis=-1, keepdims=True) + norm_eps)
    rows[0] = (widened * factor * gain_ref[...]).astype(jnp.bfloat16)
    up_all[0] = up_ref[...]
    for step in range(req_count):
        wanted_row = rows_wanted[at_req(step) * count + my_exp]
        row = wanted_row % table_rows
        staging[step, :rank] = down_ref[row]
        staging[step, rank:] = lift_ref[row]
        staging_narrow[step] = narrow_ref[row]
    offered[0] = staging[0]
    offered_narrow[0] = staging_narrow[0]
    pl.semaphore_wait(barrier, count - 1 + req_count - 1)

    def send_rows(source, target, towards):
        return pltpu.make_async_remote_copy(
            src_ref=rows.at[source],
            dst_ref=rows.at[target],
            send_sem=row_send.at[target],
            recv_sem=row_recv.at[target],
            device_id=(my_req, at_spot(towards)),
            device_id_type=MESH,
        )

    def send_part(source, side, towards):
        part = pl.ds(side * mid, mid)
        return pltpu.make_async_remote_copy(
            src_ref=rows.at[source, part],
            dst_ref=rows.at[last, part],
            send_sem=row_send.at[last + side],
            recv_sem=row_recv.at[last + side],
            device_id=(my_req, at_spot(towards)),
            device_id_type=MESH,
        )

    def send_low(source, target, towards):
        return pltpu.make_async_remote_copy(
            src_ref=low.at[source],
            dst_ref=low.at[target],
            send_sem=low_send.at[target],
            recv_sem=low_recv.at[target],
            device_id=(my_req, at_spot(towards)),
            device_id_type=MESH,
        )

    def send_down(step):
        return pltpu.make_async_remote_copy(
            src_ref=staging.at[step],
            dst_ref=offered.at[step],
            send_sem=down_send.at[step],
            recv_sem=down_recv.at[step],
            device_id=(at_req(step), my_exp),
            device_id_type=MESH,
        )

    def send_narrow(step):
        return pltpu.make_async_remote_copy(
            src_ref=staging_narrow.at[step],
            dst_ref=offered_narrow.at[step],
            send_sem=narrow_send.at[step],
            recv_sem=narrow_recv.at[step],
            device_id=(at_req(step), my_exp),
            device_id_type=MESH,
        )

    def send_up(step):
        return pltpu.make_async_remote_copy(
            src_ref=up_ref,
            dst_ref=up_all.at[step],
            send_sem=up_send.at[step],
            recv_sem=up_recv.at[step],
            device_id=(at_req(step), my_exp),
            device_id_type=MESH,
        )

    def send_att(slot):
        distance = (slot + 1) // 2 * (1 - 2 * (slot % 2))
        return pltpu.make_async_remote_copy(
            src_ref=att_out.at[slot],
            dst_ref=att_in.at[slot],
            send_sem=att_send.at[slot],
            recv_sem=att_recv.at[slot],
            device_id=(my_req, at_spot(distance)),
            device_id_type=MESH,
        )

    send_rows(0, 1, 1).start()
    send_rows(0, 2, -1).start()
    for step in range(1, req_count):
        send_down(step).start()
    for step in range(1, req_count):
        send_up(step).start()
        send_narrow(step).start()
    for head in range(heads):
        wide[:, head * 256 : head * 256 + 128] = weight_ref[head, :128].T
        wide[:, head * 256 + 128 : head * 256 + 256] = weight_ref[head, HEAD_WIDTH:].T
    for step in range(1, req_count):
        send_down(step).wait_recv()
    own_row = rows_wanted[my_req * count + my_exp]
    source = (my_req - own_row // table_rows + req_count) % req_count
    mine = offered[source]
    lift_out_ref[...] = mine[rank:]
    contract = (((1,), (1,)), ((), ()))
    low[0] = lax.dot_general(
        mine[:rank], rows[0], contract, preferred_element_type=jnp.float32
    ).astype(jnp.bfloat16)
    send_low(0, 1, 1).start()
    send_low(0, 2, -1).start()
    for step in range(1, req_count):
        send_up(step).wait_recv()
        send_narrow(step).wait_recv()
    narrow_out_ref[...] = offered_narrow[source]

    causal = lax.broadcasted_iota(jnp.int32, (seq, seq), 0) >= lax.broadcasted_iota(
        jnp.int32, (seq, seq), 1
    )
    cached_at = lax.broadcasted_iota(jnp.int32, (1, cache_ref.shape[2]), 1)
    kind = lax.broadcasted_iota(jnp.int32, (rank, 128), 0) // ADAPTER_RANK
    first = lax.broadcasted_iota(jnp.int32, (rank, 128), 1) < HEAD_WIDTH
    is_query = (kind == 0) & first
    is_kv = ((kind == 1) & first) | ((kind == 2) & jnp.logical_not(first))
    by_rank = (((0,), (0,)), ((), ()))
    front = lax.broadcasted_iota(jnp.int32, (1, 128), 1) < HEAD_WIDTH
    att_scale = HEAD_WIDTH ** (-0.5)

    def process(slot, carry):
        @pl.when((slot % 2 == 1) & (slot < last))
        def _():
            send_rows(0, slot, 1).wait_recv()

            @pl.when(slot < last - 2)
            def _():
                send_rows(slot, slot + 2, 1).start()

            @pl.when(slot == last - 2)
            def _():
                send_part(slot, 0, 1).start()

            send_rows(0, slot + 1, -1).wait_recv()

            @pl.when(slot < last - 2)
            def _():
                send_rows(slot + 1, slot + 3, -1).start()

            @pl.when(slot == last - 2)
            def _():
                send_part(slot + 1, 1, -1).start()

            send_low(0, slot, 1).wait_recv()
            send_low(slot, slot + 2, 1).start()
            send_low(0, slot + 1, -1).wait_recv()

            @pl.when(slot < last - 2)
            def _():
                send_low(slot + 1, slot + 3, -1).start()

        @pl.when(slot == last)
        def _():
            send_part(0, 0, 1).wait_recv()
            send_part(0, 1, -1).wait_recv()
            send_low(0, last, 1).wait_recv()

        distance = (slot + 1) // 2 * (1 - 2 * (slot % 2))
        owner = at_spot(distance)
        prompt = prompts[owner]
        length = lengths[prompt]
        wanted_row = rows_wanted[my_req * count + owner]
        up_one = up_all[
            (my_req - wanted_row // table_rows + req_count) % req_count, wanted_row % table_rows
        ]
        row_block = rows[slot]
        low_block = low[slot]
        visible = cached_at < length
        parts = []
        for head in range(heads):
            base = jnp.dot(
                row_block,
                wide[:, head * 256 : head * 256 + 256],
                preferred_element_type=jnp.float32,
            )
            up_head = up_one[:, head * 128 : head * 128 + 128]
            zero = jnp.zeros_like(up_head)
            extra_query = lax.dot_general(
                low_block,
                jnp.where(is_query, up_head, zero),
                by_rank,
                preferred_element_type=jnp.float32,
            )
            extra_kv = lax.dot_general(
                low_block,
                jnp.where(is_kv, up_head, zero),
                by_rank,
                preferred_element_type=jnp.float32,
            )
            query = jnp.where(front, base[:, :128], 0.0) + adapter_scale * extra_query
            query = query.astype(jnp.bfloat16)
            query = query * jnp.bfloat16(att_scale)
            own = (base[:, 128:] + adapter_scale * extra_kv).astype(jnp.bfloat16)
            cached = cache_ref[prompt, head]
            pre_scores = lax.dot_general(
                query, cached, contract, preferred_element_type=jnp.float32
            )
            own_scores = lax.dot_general(query, own, contract, preferred_element_type=jnp.float32)
            pre_scores = jnp.where(visible, pre_scores, masked_score)
            own_scores = jnp.where(causal, own_scores, masked_score)
            row_peak = jnp.maximum(
                jnp.max(pre_scores, axis=-1, keepdims=True),
                jnp.max(own_scores, axis=-1, keepdims=True),
            )
            pre_exp = jnp.exp(pre_scores - row_peak)
            own_exp = jnp.exp(own_scores - row_peak)
            denominator = jnp.sum(pre_exp, axis=-1, keepdims=True) + jnp.sum(
                own_exp, axis=-1, keepdims=True
            )
            total = jnp.dot(
                pre_exp.astype(jnp.bfloat16), cached, preferred_element_type=jnp.float32
            )
            total = total + jnp.dot(
                own_exp.astype(jnp.bfloat16), own, preferred_element_type=jnp.float32
            )
            parts.append((total / denominator)[:, HEAD_WIDTH:])
        joined = parts[0] if heads == 1 else jnp.concatenate(parts, axis=1)
        att_out[slot] = joined.astype(jnp.bfloat16)

        @pl.when(slot > 0)
        def _():
            send_att(slot).start()

        return carry

    lax.fori_loop(0, count, process, 0)

    out_ref[my_exp] = att_out[0]
    for slot in range(1, count):
        send_att(slot).wait_recv()
        distance = (slot + 1) // 2 * (2 * (slot % 2) - 1)
        out_ref[at_spot(distance)] = att_in[slot]
    for slot in range(1, last):
        send_rows(0, slot, 1).wait_send()
    send_part(0, 0, 1).wait_send()
    send_part(0, 1, -1).wait_send()
    for slot in range(1, count):
        send_low(0, slot, 1).wait_send()
        send_att(slot).wait_send()
    for step in range(1, req_count):
        send_down(step).wait_send()
        send_narrow(step).wait_send()
        send_up(step).wait_send()


def attend(tokens, gain, weight, cache, down, lift, narrow, up, prompts, lengths, rows_wanted):
    count = lax.axis_size("exp")
    req_count = lax.axis_size("req")
    _, seq, width = tokens.shape
    heads = cache.shape[1]
    wide = heads * HEAD_WIDTH
    rank = down.shape[1]
    packed = (req_count, rank + lift.shape[1], width)
    smem = pl.BlockSpec(memory_space=pltpu.SMEM)
    vmem = pl.BlockSpec(memory_space=pltpu.VMEM)
    dma = pltpu.SemaphoreType.DMA
    return pl.pallas_call(
        functools.partial(layer_kernel, (count, req_count, heads)),
        out_shape=(
            jax.ShapeDtypeStruct((count, seq, wide), jnp.bfloat16),
            jax.ShapeDtypeStruct(lift.shape[1:], jnp.bfloat16),
            jax.ShapeDtypeStruct(narrow.shape[1:], jnp.bfloat16),
        ),
        in_specs=[smem] * 3 + [vmem] * 8,
        out_specs=(vmem, vmem, vmem),
        scratch_shapes=[
            pltpu.VMEM((width, heads * 256), jnp.bfloat16),
            pltpu.VMEM((count, seq, width), jnp.bfloat16),
            pltpu.VMEM((count, rank, seq), jnp.bfloat16),
            pltpu.VMEM((count, seq, wide), jnp.bfloat16),
            pltpu.VMEM((count, seq, wide), jnp.bfloat16),
            pltpu.VMEM(packed, jnp.bfloat16),
            pltpu.VMEM(packed, jnp.bfloat16),
            pltpu.VMEM((req_count,) + narrow.shape[1:], jnp.bfloat16),
            pltpu.VMEM((req_count,) + narrow.shape[1:], jnp.bfloat16),
            pltpu.VMEM((req_count,) + up.shape, jnp.bfloat16),
            dma((count + 1,)),
            dma((count + 1,)),
            dma((count,)),
            dma((count,)),
            dma((count,)),
            dma((count,)),
            dma((req_count,)),
            dma((req_count,)),
            dma((req_count,)),
            dma((req_count,)),
            dma((req_count,)),
            dma((req_count,)),
        ],
        compiler_params=pltpu.CompilerParams(
            collective_id=0, has_side_effects=True, vmem_limit_bytes=52 * 1024 * 1024
        ),
        name="attend",
    )(prompts, lengths, rows_wanted, tokens, gain, weight, cache, down, lift, narrow, up)


def block_kernel(
    prompts,
    lengths,
    adapters,
    slot_rows,
    tokens_ref,
    gain_ref,
    weight_ref,
    cache_ref,
    down_ref,
    lift_ref,
    narrow_ref,
    up_ref,
    output_ref,
    expert_gain_ref,
    router_ref,
    routes_ref,
    slots_ref,
    outgoing_ref,
    hidden_ref,
    combine_ref,
    flat,
    wide_own,
    wide_far,
    keys_own,
    keys_far,
    rows,
    low,
    far_qkv,
    att_out,
    att_in,
    staging,
    offered,
    staging_lift,
    offered_lift,
    staging_narrow,
    offered_narrow,
    up_all,
    up_stage,
    up_far,
    weight_far,
    cache_stage,
    cache_far,
    row_send,
    row_recv,
    low_send,
    low_recv,
    att_send,
    att_recv,
    down_send,
    down_recv,
    lift_send,
    lift_recv,
    narrow_send,
    narrow_recv,
    up_send,
    up_recv,
    far_send,
    far_recv,
    across_send,
    across_recv,
    core_send,
    core_recv,
):
    count, req_count, prompt_rows = 8, 4, 2 * 1024
    seq = tokens_ref.shape[1]
    mid = seq // 2
    table_rows = down_ref.shape[0]
    rank = 3 * ADAPTER_RANK
    my_req = lax.axis_index("req")
    my_exp = lax.axis_index("exp")
    half = my_exp // 4
    my_y = my_exp % 2
    my_z = (my_exp // 2) % 2
    far_exp = (1 - half) * 4 + (1 - my_z) * 2 + my_y
    core_req = my_req + 1 - 2 * (my_req % 2)
    across_req = (my_req + 2) % req_count

    def at_slot(slot):
        return half * 4 + ((my_z + slot // 2) % 2) * 2 + (my_y + slot) % 2

    def mirrored(slot):
        return (1 - half) * 4 + ((my_z + slot // 2 + 1) % 2) * 2 + (my_y + slot) % 2

    def at_req(offset):
        return (my_req + offset) % req_count

    def row_of(request):
        return slot_rows[adapters[request]]

    def remote(source, target, sem_send, sem_recv, device):
        return pltpu.make_async_remote_copy(
            src_ref=source,
            dst_ref=target,
            send_sem=sem_send,
            recv_sem=sem_recv,
            device_id=device,
            device_id_type=MESH,
        )

    barrier = pltpu.get_barrier_semaphore()
    for slot in range(1, 4):
        pl.semaphore_signal(barrier, inc=1, device_id=(my_req, at_slot(slot)), device_id_type=MESH)
    pl.semaphore_signal(barrier, inc=1, device_id=(my_req, far_exp), device_id_type=MESH)
    for step in range(1, req_count):
        pl.semaphore_signal(barrier, inc=1, device_id=(at_req(step), my_exp), device_id_type=MESH)

    for step in range(req_count):
        row = row_of(at_req(step) * count + my_exp) % table_rows
        staging[step] = down_ref[row]
        staging_lift[step] = lift_ref[row]
        staging_narrow[step] = narrow_ref[row]
    offered[0] = staging[0]
    offered_lift[0] = staging_lift[0]
    offered_narrow[0] = staging_narrow[0]
    picked = lax.broadcasted_iota(jnp.int32, (rank, 2 * rank), 1) - 2 * lax.broadcasted_iota(
        jnp.int32, (rank, 2 * rank), 0
    )

    def pack(row, carry):
        table = up_ref[row]
        halves = [
            jnp.dot(
                (picked == head).astype(jnp.bfloat16), table, preferred_element_type=jnp.float32
            )
            for head in range(2)
        ]
        up_all[0, row] = jnp.concatenate(halves, axis=1).astype(jnp.bfloat16)
        return carry

    lax.fori_loop(0, table_rows, pack, 0)
    widened = tokens_ref[0].astype(jnp.float32)
    factor = lax.rsqrt(jnp.mean(widened * widened, axis=-1, keepdims=True) + norm_eps)
    rows[0] = (widened * factor * gain_ref[...]).astype(jnp.bfloat16)
    wq = weight_ref.shape[0] // req_count
    quarter = cache_stage.shape[0]
    third = quarter // 3
    granule = 32
    blocks = 1024 // granule
    ends = []
    total = 0
    for prompt in range(4):
        total = total + (lengths[prompt] + granule - 1) // granule
        ends.append(total)
    starts = [0] + ends[:3]

    def source_of(index):
        prompt = 0
        begin = 0
        for p in range(1, 4):
            past = index >= starts[p]
            prompt = jnp.where(past, p, prompt)
            begin = jnp.where(past, starts[p], begin)
        return prompt * blocks + jnp.minimum(index - begin, blocks - 1)

    def stage(index, carry):
        source = source_of(my_req * quarter + index)
        cache_stage[index] = cache_ref[source]
        return carry

    lax.fori_loop(0, quarter, stage, 0)
    pl.semaphore_wait(barrier, 7)

    def send_row_y():
        return remote(
            rows.at[0], rows.at[1], row_send.at[0], row_recv.at[0], (my_req, at_slot(1))
        )

    def send_row_z():
        return remote(
            rows.at[0], rows.at[2], row_send.at[1], row_recv.at[1], (my_req, at_slot(2))
        )

    def send_row_on():
        return remote(
            rows.at[2], rows.at[3], row_send.at[2], row_recv.at[2], (my_req, at_slot(1))
        )

    def send_low(slot):
        return remote(
            low.at[0], low.at[slot], low_send.at[slot], low_recv.at[slot], (my_req, at_slot(slot))
        )

    def send_att(kind, slot):
        return remote(
            att_out.at[kind, slot],
            att_in.at[kind, slot],
            att_send.at[kind, slot],
            att_recv.at[kind, slot],
            (my_req, at_slot(slot)),
        )

    def to_req(source, target, sem_send, sem_recv, step):
        return remote(
            source, target, sem_send.at[step], sem_recv.at[step], (at_req(step), my_exp)
        )

    def send_down(step):
        return to_req(staging.at[step], offered.at[step], down_send, down_recv, step)

    def send_lift(step):
        return to_req(staging_lift.at[step], offered_lift.at[step], lift_send, lift_recv, step)

    def send_narrow(step):
        return to_req(
            staging_narrow.at[step], offered_narrow.at[step], narrow_send, narrow_recv, step
        )

    def send_up(step):
        return to_req(up_all.at[0], up_all.at[step], up_send, up_recv, step)

    def send_up_far():
        return remote(up_stage, up_far, far_send.at[4], far_recv.at[4], (my_req, far_exp))

    def piece(owner, part):
        if part == 0:
            return weight_far.at[pl.ds(pl.multiple_of(owner * wq, 32), wq)]
        return cache_far.at[pl.ds(owner * quarter + (part - 1) * third, third)]

    def send_far(part):
        if part == 0:
            source = weight_ref.at[pl.ds(pl.multiple_of(my_req * wq, 32), wq)]
        else:
            source = cache_stage.at[pl.ds((part - 1) * third, third)]
        return remote(
            source,
            piece(my_req, part),
            far_send.at[part],
            far_recv.at[part],
            (my_req, far_exp),
        )

    def send_across(part):
        return remote(
            piece(my_req, part),
            piece(my_req, part),
            across_send.at[part],
            across_recv.at[part],
            (across_req, my_exp),
        )

    def take_across(part):
        return remote(
            piece(across_req, part),
            piece(across_req, part),
            across_send.at[part],
            across_recv.at[part],
            (across_req, my_exp),
        )

    def send_core(kind, part):
        owner = my_req if kind == 0 else across_req
        return remote(
            piece(owner, part),
            piece(owner, part),
            core_send.at[kind, part],
            core_recv.at[kind, part],
            (core_req, my_exp),
        )

    def take_core(kind, part):
        owner = core_req if kind == 0 else (core_req + 2) % req_count
        return remote(
            piece(owner, part),
            piece(owner, part),
            core_send.at[kind, part],
            core_recv.at[kind, part],
            (core_req, my_exp),
        )

    def pass_far(part):
        send_far(part).wait_recv()
        send_across(part).start()
        send_core(0, part).start()

    def pass_across(part):
        take_across(part).wait_recv()
        send_core(1, part).start()

    outer = my_z == half
    inner = my_z != half
    send_row_z().start()
    send_row_y().start()
    for step in range(1, req_count):
        send_down(step).start()
    for step in range(1, req_count):
        send_up(step).start()

    @pl.when(inner)
    def _():
        for part in range(4):
            send_far(part).start()

    top = lax.broadcasted_iota(jnp.int32, (128, 1), 0) < HEAD_WIDTH

    def widen(source_ref, target_ref):
        for head in range(2):
            block = source_ref[head * 192 : head * 192 + 128]
            block = jnp.where(top, block, jnp.zeros_like(block))
            target_ref[:, head * 128 : head * 128 + 128] = block.T
            target_ref[:, 256 + head * 128 : 384 + head * 128] = source_ref[
                head * 192 + 64 : head * 192 + 192
            ].T

    row_kind = lax.broadcasted_iota(jnp.int32, (256, 128), 0) % 2
    first_rows = (row_kind == 0).astype(jnp.bfloat16)
    second_rows = (row_kind == 1).astype(jnp.bfloat16)

    def own_keys(index, carry):
        block = cache_ref[pl.ds(index * 4, 4)].reshape(256, 128)
        at = pl.ds(pl.multiple_of(index % 8 * 256, 256), 256)
        keys_own[index // 8, at, :128] = block * first_rows
        keys_own[index // 8, at, 128:] = block * second_rows
        return carry

    widen(weight_ref, wide_own)
    lax.fori_loop(0, 32, own_keys, 0)

    for step in range(1, req_count):
        send_down(step).wait_recv()
    own_row = row_of(my_req * count + my_exp)
    source = (my_req - own_row // table_rows + req_count) % req_count
    contract = (((1,), (1,)), ((), ()))
    low[0] = lax.dot_general(
        offered[source], rows[0], contract, preferred_element_type=jnp.float32
    ).astype(jnp.bfloat16)
    for slot in range(1, 4):
        send_low(slot).start()

    for step in range(1, req_count):
        send_up(step).wait_recv()

    def up_of(request):
        row = row_of(request)
        return up_all[(my_req - row // table_rows + req_count) % req_count, row % table_rows]

    for index in range(4):
        up_stage[index] = up_of(my_req * count + (1 - half) * 4 + index)
    send_up_far().start()
    for step in range(1, req_count):
        send_lift(step).start()
        send_narrow(step).start()

    @pl.when(inner)
    def _():
        pass_far(0)


    column = lax.broadcasted_iota(jnp.int32, (128, 512), 1)
    lane = lax.broadcasted_iota(jnp.int32, (128, 512), 0)
    spread = (lane == (column // 128 % 2) * HEAD_WIDTH + column % HEAD_WIDTH).astype(jnp.bfloat16)
    column = lax.broadcasted_iota(jnp.int32, (rank, 512), 1)
    kind = lax.broadcasted_iota(jnp.int32, (rank, 512), 0) // ADAPTER_RANK
    back = column % 128 // HEAD_WIDTH
    kept = kind == jnp.where(column < 256, 3 * back, 1 + back)
    by_rank = (((0,), (0,)), ((), ()))
    causal = lax.broadcasted_iota(jnp.int32, (seq, seq), 0) >= lax.broadcasted_iota(
        jnp.int32, (seq, seq), 1
    )
    cached_at = lax.broadcasted_iota(jnp.int32, (1, prompt_rows), 1)
    even = lax.broadcasted_iota(jnp.int32, (1, 128), 1) % 2 == 0
    att_scale = HEAD_WIDTH ** (-0.5)

    def project(slot, wide_ref, up_one):
        base = jnp.dot(rows[slot], wide_ref[...], preferred_element_type=jnp.float32)
        up_wide = jnp.dot(up_one, spread, preferred_element_type=jnp.float32)
        up_wide = jnp.where(kept, up_wide, 0.0).astype(jnp.bfloat16)
        extra = lax.dot_general(low[slot], up_wide, by_rank, preferred_element_type=jnp.float32)
        return (base + adapter_scale * extra).astype(jnp.bfloat16)

    def attention(qkv, keys, length):
        query = qkv[:, :256] * jnp.bfloat16(att_scale)
        scores = lax.dot_general(query, keys, contract, preferred_element_type=jnp.float32)
        scores = jnp.where(cached_at < 2 * length, scores, masked_score)
        own_scores = []
        for head in range(2):
            at = slice(head * 128, head * 128 + 128)
            own = qkv[:, 256 + head * 128 : 384 + head * 128]
            one = lax.dot_general(query[:, at], own, contract, preferred_element_type=jnp.float32)
            own_scores.append(jnp.where(causal, one, masked_score))
        tiles = prompt_rows // 128
        most = scores[:, :128]
        for tile in range(1, tiles):
            most = jnp.maximum(most, scores[:, tile * 128 : tile * 128 + 128])
        peaks = []
        for head in range(2):
            mine = even if head == 0 else jnp.logical_not(even)
            peaks.append(
                jnp.maximum(
                    jnp.max(jnp.where(mine, most, masked_score), axis=-1, keepdims=True),
                    jnp.max(own_scores[head], axis=-1, keepdims=True),
                )
            )
        peak = jnp.where(even, peaks[0], peaks[1])
        weights = []
        summed = jnp.zeros((seq, 128), jnp.float32)
        for tile in range(tiles):
            one = jnp.exp(scores[:, tile * 128 : tile * 128 + 128] - peak)
            summed = summed + one
            weights.append(one.astype(jnp.bfloat16))
        total = jnp.dot(
            jnp.concatenate(weights, axis=1), keys, preferred_element_type=jnp.float32
        )
        parts = []
        for head in range(2):
            mine = even if head == 0 else jnp.logical_not(even)
            own = qkv[:, 256 + head * 128 : 384 + head * 128]
            own_exp = jnp.exp(own_scores[head] - peaks[head])
            denominator = jnp.sum(
                jnp.where(mine, summed, 0.0), axis=-1, keepdims=True
            ) + jnp.sum(own_exp, axis=-1, keepdims=True)
            both = total[:, head * 128 : head * 128 + 128] + jnp.dot(
                own_exp.astype(jnp.bfloat16), own, preferred_element_type=jnp.float32
            )
            parts.append((both / denominator)[:, HEAD_WIDTH:])
        return jnp.concatenate(parts, axis=1).astype(jnp.bfloat16)

    def own_heads(slot, carry):
        @pl.when(slot == 1)
        def _():
            send_row_z().wait_recv()
            send_row_on().start()

            @pl.when(outer)
            def _():
                send_row_z().wait_send()
                for part in range(4):
                    send_far(part).start()

            @pl.when(inner)
            def _():
                pass_far(1)
                pass_across(0)

            send_row_y().wait_recv()
            send_low(1).wait_recv()

        @pl.when(slot == 2)
        def _():
            send_low(2).wait_recv()

            @pl.when(inner)
            def _():
                pass_far(2)
                pass_far(3)
                pass_across(1)

        @pl.when(slot == 3)
        def _():
            @pl.when(outer)
            def _():
                pass_far(0)
                pass_far(1)
                pass_across(0)
                pass_far(2)

            send_row_on().wait_recv()
            send_low(3).wait_recv()

            @pl.when(inner)
            def _():
                pass_across(2)

        owner = at_slot(slot)
        prompt = prompts[owner]
        qkv = project(slot, wide_own, up_of(my_req * count + owner))
        att_out[0, slot] = attention(qkv, keys_own[prompt], lengths[prompt])

        @pl.when(slot > 0)
        def _():
            send_att(0, slot).start()

        return carry

    lax.fori_loop(0, 4, own_heads, 0)

    @pl.when(outer)
    def _():
        pass_far(3)
        pass_across(1)
        pass_across(2)

    take_core(0, 0).wait_recv()
    take_core(1, 0).wait_recv()
    send_up_far().wait_recv()
    widen(weight_far, wide_far)

    def far_project(slot, carry):
        index = ((my_z + slot // 2) % 2) * 2 + (my_y + slot) % 2
        far_qkv[slot] = project(slot, wide_far, up_far[index])
        return carry

    lax.fori_loop(0, 4, far_project, 0)

    pass_across(3)

    for part in range(1, 4):
        take_core(0, part).wait_recv()
        take_core(1, part).wait_recv()

    def unpack(index, carry):
        for prompt in range(4):
            for lane in range(4):
                block = cache_far[jnp.minimum(starts[prompt] + index * 4 + lane, 4 * quarter - 1)]
                at = pl.ds(pl.multiple_of(index * 256 + lane * 64, 64), 64)
                keys_far[prompt, at, :128] = block * first_rows[:64]
                keys_far[prompt, at, 128:] = block * second_rows[:64]
        return carry

    lax.fori_loop(0, blocks // 4, unpack, 0)

    def far_keys(slot):
        prompt = prompts[at_slot(slot)]
        return keys_far[prompt], lengths[prompt]

    def far_heads(step, carry):
        first, second = 3 - 2 * step, 2 - 2 * step
        att_first = attention(far_qkv[first], *far_keys(first))
        att_second = attention(far_qkv[second], *far_keys(second))
        att_out[1, first] = att_first
        att_out[1, second] = att_second
        send_att(1, first).start()

        @pl.when(second > 0)
        def _():
            send_att(1, second).start()

        return carry

    lax.fori_loop(0, 2, far_heads, 0)

    for step in range(1, req_count):
        send_lift(step).wait_recv()
        send_narrow(step).wait_recv()
    for kind in range(2):
        for slot in range(4):
            if slot > 0:
                send_att(kind, slot).wait_recv()
            at = pl.ds(pl.multiple_of((at_slot(slot) if kind == 0 else mirrored(slot)) * 128, 128), 128)
            flat[:, at] = att_out[kind, 0] if slot == 0 else att_in[kind, slot]

    attended = flat[...]
    narrow = offered_narrow[source]
    narrow = jnp.concatenate(
        [narrow[at : at + ADAPTER_RANK] for at in range(0, narrow.shape[0], ADAPTER_RANK)], axis=1
    )
    low_out = lax.dot_general(attended, narrow, contract, preferred_element_type=jnp.float32)
    lift = offered_lift[source]
    terms = []
    for _ in range(3):
        terms.append(low_out.astype(jnp.bfloat16))
        low_out = low_out - terms[-1].astype(jnp.float32)
    surplus = jnp.dot(
        jnp.concatenate(terms, axis=1),
        jnp.concatenate([lift] * 3, axis=0),
        preferred_element_type=jnp.float32,
    )
    plain = jnp.dot(attended, output_ref[...], preferred_element_type=jnp.float32)
    hidden = tokens_ref[0].astype(jnp.float32) + (plain + adapter_scale * surplus)
    hidden = hidden.astype(jnp.bfloat16)
    hidden_ref[...] = hidden
    moe_in = rms_norm(hidden, expert_gain_ref[...])
    cells = lax.broadcasted_iota(jnp.int32, (outgoing_ref.shape[0], seq), 0)
    capacity = outgoing_ref.shape[0] // count
    target = jnp.where(slots_ref[...] >= 0, routes_ref[...] * capacity + slots_ref[...], -1)
    sending = jnp.where(cells == target[0:1], 1.0, jnp.where(cells == target[1:2], 1.0, 0.0))
    outgoing_ref[...] = jnp.dot(
        sending.astype(jnp.bfloat16), moe_in, preferred_element_type=jnp.float32
    ).astype(jnp.bfloat16)
    gates = jax.nn.sigmoid(
        lax.dot_general(router_ref[...], moe_in, contract, preferred_element_type=jnp.float32)
    )
    gated = [
        sending[expert * capacity : (expert + 1) * capacity] * gates[expert : expert + 1]
        for expert in range(count)
    ]
    combine_ref[...] = jnp.concatenate(gated, axis=0).T

    send_row_y().wait_send()
    send_row_on().wait_send()

    @pl.when(inner)
    def _():
        send_row_z().wait_send()

    for slot in range(1, 4):
        send_low(slot).wait_send()
        for kind in range(2):
            send_att(kind, slot).wait_send()
    for step in range(1, req_count):
        send_down(step).wait_send()
        send_lift(step).wait_send()
        send_narrow(step).wait_send()
        send_up(step).wait_send()
    send_up_far().wait_send()
    for part in range(4):
        send_far(part).wait_send()
    for part in range(4):
        send_across(part).wait_send()
        send_core(0, part).wait_send()
        send_core(1, part).wait_send()


def attend_block(
    tokens,
    gain,
    weight,
    cache,
    down,
    lift,
    narrow,
    up,
    output,
    expert_gain,
    router,
    routes,
    slots,
    prompts,
    lengths,
    adapters,
    slot_rows,
):
    _, seq, width = tokens.shape
    rank = down.shape[1]
    experts = router.shape[0]
    cells = experts * (5 * seq * TOP // (4 * experts))
    smem = pl.BlockSpec(memory_space=pltpu.SMEM)
    vmem = pl.BlockSpec(memory_space=pltpu.VMEM)
    dma = pltpu.SemaphoreType.DMA

    def bf16(*shape):
        return pltpu.VMEM(shape, jnp.bfloat16)

    return pl.pallas_call(
        block_kernel,
        out_shape=(
            jax.ShapeDtypeStruct((cells, width), jnp.bfloat16),
            jax.ShapeDtypeStruct((seq, width), jnp.bfloat16),
            jax.ShapeDtypeStruct((seq, cells), jnp.float32),
        ),
        in_specs=[smem] * 4 + [vmem] * 13,
        out_specs=(vmem, vmem, vmem),
        scratch_shapes=[
            bf16(seq, width),
            bf16(width, 512),
            bf16(width, 512),
            bf16(4, 2048, 256),
            bf16(4, 2048, 256),
            bf16(4, seq, width),
            bf16(4, rank, seq),
            bf16(4, seq, 512),
            bf16(2, 4, seq, 128),
            bf16(2, 4, seq, 128),
            bf16(4, rank, width),
            bf16(4, rank, width),
            bf16(4, *lift.shape[1:]),
            bf16(4, *lift.shape[1:]),
            bf16(4, *narrow.shape[1:]),
            bf16(4, *narrow.shape[1:]),
            bf16(4, up.shape[0], rank, 128),
            bf16(4, rank, 128),
            bf16(4, rank, 128),
            bf16(*weight.shape),
            bf16(21, *cache.shape[1:]),
            bf16(84, *cache.shape[1:]),
            dma((5,)),
            dma((5,)),
            dma((4,)),
            dma((4,)),
            dma((2, 4)),
            dma((2, 4)),
            dma((4,)),
            dma((4,)),
            dma((4,)),
            dma((4,)),
            dma((4,)),
            dma((4,)),
            dma((4,)),
            dma((4,)),
            dma((5,)),
            dma((5,)),
            dma((4,)),
            dma((4,)),
            dma((2, 4)),
            dma((2, 4)),
        ],
        compiler_params=pltpu.CompilerParams(
            collective_id=2, has_side_effects=True, vmem_limit_bytes=56 * 1024 * 1024
        ),
        name="attend_block",
    )(
        prompts,
        lengths,
        adapters,
        slot_rows,
        tokens,
        gain,
        weight,
        cache,
        down,
        lift,
        narrow,
        up,
        output,
        expert_gain,
        router,
        routes,
        slots,
    )


def expert_block_kernel(
    outgoing_ref,
    gate_up_hbm,
    down_hbm,
    out_ref,
    gate_up,
    down,
    inbox,
    outbox,
    back,
    weight_sem,
    there_send,
    there_recv,
    back_send,
    back_recv,
):
    my_req = lax.axis_index("req")
    my_exp = lax.axis_index("exp")
    half = my_exp // 4
    my_y = my_exp % 2
    my_z = (my_exp // 2) % 2
    load_gate_up = pltpu.make_async_copy(gate_up_hbm.at[0], gate_up, weight_sem.at[0])
    load_down = pltpu.make_async_copy(down_hbm.at[0], down, weight_sem.at[1])
    load_gate_up.start()
    load_down.start()

    def partner(step):
        crossing, slot = step // 4, step % 4
        side = (half + crossing) % 2
        return side * 4 + ((my_z + slot // 2 + crossing) % 2) * 2 + (my_y + slot) % 2

    barrier = pltpu.get_barrier_semaphore()
    for step in range(1, 8):
        pl.semaphore_signal(barrier, inc=1, device_id=(my_req, partner(step)), device_id_type=MESH)
    inbox[0] = outgoing_ref[my_exp]
    pl.semaphore_wait(barrier, 7)

    def send_there(step):
        return pltpu.make_async_remote_copy(
            src_ref=outgoing_ref.at[partner(step)],
            dst_ref=inbox.at[step],
            send_sem=there_send.at[step],
            recv_sem=there_recv.at[step],
            device_id=(my_req, partner(step)),
            device_id_type=MESH,
        )

    def send_back(step):
        return pltpu.make_async_remote_copy(
            src_ref=outbox.at[step],
            dst_ref=back.at[step],
            send_sem=back_send.at[step],
            recv_sem=back_recv.at[step],
            device_id=(my_req, partner(step)),
            device_id_type=MESH,
        )

    for step in (1, 2, 3, 4, 5, 6, 7):
        send_there(step).start()
    load_gate_up.wait()
    load_down.wait()
    cap, width = inbox.shape[1:]
    chunk = FF // 2

    def process(pair, carry):
        @pl.when(pair > 0)
        def _():
            send_there(2 * pair).wait_recv()

        send_there(2 * pair + 1).wait_recv()
        received = inbox[pl.ds(2 * pair, 2)].reshape(2 * cap, width)
        total = jnp.zeros((2 * cap, width), jnp.float32)
        for part in range(2):
            gate = jnp.dot(
                received,
                gate_up[:, part * chunk : (part + 1) * chunk],
                preferred_element_type=jnp.float32,
            )
            up = jnp.dot(
                received,
                gate_up[:, FF + part * chunk : FF + (part + 1) * chunk],
                preferred_element_type=jnp.float32,
            )
            activated = (jax.nn.gelu(gate, approximate=True) * up).astype(jnp.bfloat16)
            total = total + jnp.dot(
                activated,
                down[part * chunk : (part + 1) * chunk],
                preferred_element_type=jnp.float32,
            )
        outbox[pl.ds(2 * pair, 2)] = total.reshape(2, cap, width).astype(jnp.bfloat16)

        @pl.when(pair > 0)
        def _():
            send_back(2 * pair).start()

        send_back(2 * pair + 1).start()
        return carry

    lax.fori_loop(0, 4, process, 0)
    out_ref[my_exp] = outbox[0]
    for step in range(1, 8):
        send_back(step).wait_recv()
        out_ref[partner(step)] = back[step]
    for step in range(1, 8):
        send_there(step).wait_send()
    for step in range(1, 8):
        send_back(step).wait_send()


def expert_kernel(
    count,
    outgoing_ref,
    gate_up_hbm,
    down_hbm,
    out_ref,
    gate_up,
    down,
    inbox,
    outbox,
    back,
    weight_sem,
    there_send,
    there_recv,
    back_send,
    back_recv,
):
    my_req = lax.axis_index("req")
    my_exp = lax.axis_index("exp")
    load_gate_up = pltpu.make_async_copy(gate_up_hbm.at[0], gate_up, weight_sem.at[0])
    load_down = pltpu.make_async_copy(down_hbm.at[0], down, weight_sem.at[1])
    load_gate_up.start()
    load_down.start()

    def at_exp(offset):
        return (my_exp + offset + count) % count

    barrier = pltpu.get_barrier_semaphore()
    for step in range(1, count):
        pl.semaphore_signal(barrier, inc=1, device_id=(my_req, at_exp(step)), device_id_type=MESH)
    inbox[0] = outgoing_ref[my_exp]
    pl.semaphore_wait(barrier, count - 1)

    def send_there(step):
        return pltpu.make_async_remote_copy(
            src_ref=outgoing_ref.at[at_exp(step)],
            dst_ref=inbox.at[step],
            send_sem=there_send.at[step],
            recv_sem=there_recv.at[step],
            device_id=(my_req, at_exp(step)),
            device_id_type=MESH,
        )

    def send_back(step):
        return pltpu.make_async_remote_copy(
            src_ref=outbox.at[step],
            dst_ref=back.at[step],
            send_sem=back_send.at[step],
            recv_sem=back_recv.at[step],
            device_id=(my_req, at_exp(-step)),
            device_id_type=MESH,
        )

    for step in range(1, count):
        send_there(step).start()
    load_gate_up.wait()
    load_down.wait()
    cap, width = inbox.shape[1:]
    chunk = FF // 2

    def process(pair, carry):
        @pl.when(pair > 0)
        def _():
            send_there(2 * pair).wait_recv()

        send_there(2 * pair + 1).wait_recv()
        received = inbox[pl.ds(2 * pair, 2)].reshape(2 * cap, width)
        total = jnp.zeros((2 * cap, width), jnp.float32)
        for part in range(2):
            gate = jnp.dot(
                received,
                gate_up[:, part * chunk : (part + 1) * chunk],
                preferred_element_type=jnp.float32,
            )
            up = jnp.dot(
                received,
                gate_up[:, FF + part * chunk : FF + (part + 1) * chunk],
                preferred_element_type=jnp.float32,
            )
            activated = (jax.nn.gelu(gate, approximate=True) * up).astype(jnp.bfloat16)
            total = total + jnp.dot(
                activated,
                down[part * chunk : (part + 1) * chunk],
                preferred_element_type=jnp.float32,
            )
        outbox[pl.ds(2 * pair, 2)] = total.reshape(2, cap, width).astype(jnp.bfloat16)

        @pl.when(pair > 0)
        def _():
            send_back(2 * pair).start()

        send_back(2 * pair + 1).start()
        return carry

    lax.fori_loop(0, count // 2, process, 0)
    out_ref[my_exp] = outbox[0]
    for step in range(1, count):
        send_back(step).wait_recv()
        out_ref[at_exp(step)] = back[step]
    for step in range(1, count):
        send_there(step).wait_send()
        send_back(step).wait_send()


def run_experts(outgoing, gate_up, down, blocks=False):
    count, cap, width = outgoing.shape
    vmem = pl.BlockSpec(memory_space=pltpu.VMEM)
    hbm = pl.BlockSpec(memory_space=pl.ANY)
    dma = pltpu.SemaphoreType.DMA
    block = pltpu.VMEM(outgoing.shape, jnp.bfloat16)
    return pl.pallas_call(
        expert_block_kernel if blocks else functools.partial(expert_kernel, count),
        out_shape=jax.ShapeDtypeStruct(outgoing.shape, jnp.bfloat16),
        in_specs=[vmem, hbm, hbm],
        out_specs=vmem,
        scratch_shapes=[
            pltpu.VMEM(gate_up.shape[1:], jnp.bfloat16),
            pltpu.VMEM(down.shape[1:], jnp.bfloat16),
            block,
            block,
            block,
            dma((2,)),
            dma((count,)),
            dma((count,)),
            dma((count,)),
            dma((count,)),
        ],
        compiler_params=pltpu.CompilerParams(
            collective_id=3 if blocks else 1, has_side_effects=True, vmem_limit_bytes=52 * 1024 * 1024
        ),
        name="experts",
    )(outgoing, gate_up, down)


def body(
    tokens,
    attention_norm_gain,
    expert_norm_gain,
    query_key_value_weight,
    output_weight,
    prompt_key_value_cache,
    shared_prompt_length,
    prompt_per_request,
    adapter_per_request,
    adapter_slot_rows,
    adapter_down_qkv,
    adapter_up_qkv,
    adapter_down_output,
    adapter_up_output,
    router_weight,
    expert_gate_up_weight,
    expert_down_weight,
    routes,
    slots,
):
    heads_here = query_key_value_weight.shape[1]
    seq_whole = tokens.shape[1]
    table_rows = adapter_down_qkv.shape[0]
    narrow = jnp.swapaxes(adapter_down_output, 2, 3).reshape(table_rows, -1, HEAD_WIDTH)
    if (lax.axis_size("exp"), lax.axis_size("req"), heads_here) == (8, 4, 2):
        outgoing, hidden, combine = attend_block(
            tokens,
            attention_norm_gain[None],
            jnp.transpose(query_key_value_weight, (1, 2, 0)).reshape(-1, MODEL_WIDTH),
            prompt_key_value_cache.reshape(-1, 64, 2 * HEAD_WIDTH),
            jnp.swapaxes(adapter_down_qkv, 1, 2),
            adapter_up_output,
            narrow,
            adapter_up_qkv.reshape(table_rows, 6 * ADAPTER_RANK, HEAD_WIDTH),
            output_weight.reshape(-1, MODEL_WIDTH),
            expert_norm_gain[None],
            router_weight.T,
            routes[0].T,
            slots[0].T,
            prompt_per_request,
            shared_prompt_length,
            adapter_per_request,
            adapter_slot_rows,
        )
        returned = run_experts(
            outgoing.reshape(router_weight.shape[1], -1, MODEL_WIDTH),
            expert_gate_up_weight,
            expert_down_weight,
            blocks=True,
        )
        moe_sum = jnp.dot(
            combine,
            returned.reshape(-1, MODEL_WIDTH).astype(jnp.float32),
            precision=lax.Precision.HIGH,
        )
        return (hidden.astype(jnp.float32) + moe_sum).astype(jnp.bfloat16)[None]

    wanted_all = adapter_slot_rows[adapter_per_request]

    up_twice = jnp.concatenate([adapter_up_qkv, adapter_up_qkv], axis=-1).reshape(
        table_rows, 3 * ADAPTER_RANK, heads_here * 2 * HEAD_WIDTH
    )
    gathered, own_bo, own_ao = attend(
        tokens,
        attention_norm_gain[None],
        jnp.transpose(query_key_value_weight, (1, 2, 0)),
        jnp.swapaxes(prompt_key_value_cache, 1, 2),
        jnp.swapaxes(adapter_down_qkv, 1, 2),
        adapter_up_output,
        narrow,
        up_twice,
        prompt_per_request,
        shared_prompt_length,
        wanted_all,
    )
    flat_att = jnp.swapaxes(gathered, 0, 1).reshape(seq_whole, -1)
    plain_out = jnp.dot(
        flat_att, output_weight.reshape(-1, MODEL_WIDTH), preferred_element_type=jnp.float32
    )
    own_ao = jnp.swapaxes(own_ao.reshape(-1, ADAPTER_RANK, HEAD_WIDTH), 1, 2)
    low_out = jnp.dot(
        flat_att, own_ao.reshape(-1, ADAPTER_RANK), preferred_element_type=jnp.float32
    )
    surplus = lax.dot_general(
        low_out,
        own_bo.astype(jnp.float32),
        (((1,), (0,)), ((), ())),
        precision=lax.Precision.HIGHEST,
    )
    projected_rows = (plain_out + adapter_scale * surplus)[None]
    hidden = (tokens.astype(jnp.float32) + projected_rows).astype(jnp.bfloat16)
    moe_in = rms_norm(hidden, expert_norm_gain)
    rows_here = REQ_DEV * seq_whole
    flat_in = moe_in.reshape(rows_here, MODEL_WIDTH)
    gate_vals = jax.nn.sigmoid(jnp.dot(flat_in, router_weight, preferred_element_type=jnp.float32))
    expert_count = router_weight.shape[1]
    capacity = 5 * rows_here * TOP // (4 * expert_count)
    route_flat = routes.reshape(rows_here, TOP)
    slot_flat = slots.reshape(rows_here, TOP)
    target = jnp.where(slot_flat >= 0, route_flat * capacity + slot_flat, -1)
    cells = jnp.arange(expert_count * capacity, dtype=jnp.int32)
    matched = target[:, :, None] == cells[None, None, :]
    named = route_flat[:, :, None] == jnp.arange(expert_count, dtype=jnp.int32)[None, None, :]
    chosen_gate = jnp.sum(jnp.where(named, gate_vals[:, None, :], 0.0), axis=2)
    combine = jnp.sum(jnp.where(matched, chosen_gate[:, :, None], 0.0), axis=1)
    sending = jnp.any(matched, axis=1).astype(jnp.bfloat16)
    outgoing = jnp.einsum("rc,rd->cd", sending, flat_in, preferred_element_type=jnp.float32).astype(
        jnp.bfloat16
    )
    returned = run_experts(
        outgoing.reshape(expert_count, capacity, MODEL_WIDTH),
        expert_gate_up_weight,
        expert_down_weight,
    )
    returned_wide = returned.reshape(expert_count * capacity, MODEL_WIDTH).astype(jnp.float32)
    moe_sum = jnp.dot(combine, returned_wide, precision=lax.Precision.HIGHEST)
    mixed = (hidden.reshape(rows_here, MODEL_WIDTH).astype(jnp.float32) + moe_sum).astype(
        jnp.bfloat16
    )
    return mixed.reshape(tokens.shape)


def solution(mesh):
    in_specs = (
        P(("req", "exp"), None, None),
        P(),
        P(),
        P(None, "exp", None),
        P(),
        P(None, None, "exp", None),
        P(),
        P("req"),
        P(),
        P(),
        P("req", None, None),
        P("req", None, None, "exp", None),
        P("req", None, None, None),
        P("req", None, None),
        P(),
        P("exp", None, None),
        P("exp", None, None),
        P(("req", "exp"), None, None),
        P(("req", "exp"), None, None),
    )
    out_specs = P(("req", "exp"), None, None)
    return jax.shard_map(body, mesh=mesh, in_specs=in_specs, out_specs=out_specs, check_vma=False)
```

```python
import functools

import jax
import jax.numpy as jnp
from jax import lax
from jax.experimental import pallas as pl
from jax.experimental.pallas import tpu as pltpu
from jax.sharding import PartitionSpec as P

MODEL_WIDTH = 1024
HEAD_WIDTH = 64
FF = 2816
ADAPTER_RANK = 16
TOP = 2
REQ_DEV = 1


adapter_scale = 0.5
norm_eps = 1e-06
MESH = pl.DeviceIdType.MESH
masked_score = -1e30


def rms_norm(values, gain):
    widened = values.astype(jnp.float32)
    factor = lax.rsqrt(jnp.mean(widened * widened, axis=-1, keepdims=True) + norm_eps)
    return (widened * factor * gain).astype(jnp.bfloat16)


def ring_device(spot, count):
    turned = spot // (count // 2)
    return 2 * (spot + turned * (count - 1 - 2 * spot)) + turned


def layer_kernel(
    sizes,
    prompts,
    lengths,
    rows_wanted,
    tokens_ref,
    gain_ref,
    weight_ref,
    cache_ref,
    down_ref,
    lift_ref,
    narrow_ref,
    up_ref,
    out_ref,
    lift_out_ref,
    narrow_out_ref,
    wide,
    rows,
    low,
    att_out,
    att_in,
    staging,
    offered,
    staging_narrow,
    offered_narrow,
    up_all,
    row_send,
    row_recv,
    low_send,
    low_recv,
    att_send,
    att_recv,
    down_send,
    down_recv,
    narrow_send,
    narrow_recv,
    up_send,
    up_recv,
):
    count, req_count, heads = sizes
    half = count // 2
    last = count - 1
    seq = tokens_ref.shape[1]
    mid = seq // 2
    table_rows = down_ref.shape[0]
    rank = 3 * ADAPTER_RANK
    my_req = lax.axis_index("req")
    my_exp = lax.axis_index("exp")
    my_side = my_exp % 2
    my_spot = my_exp // 2 + my_side * (count - 1 - 2 * (my_exp // 2))

    def at_spot(offset):
        return ring_device((my_spot + offset + count) % count, count)

    def at_req(offset):
        return (my_req + offset) % req_count

    barrier = pltpu.get_barrier_semaphore()
    for step in range(1, count):
        pl.semaphore_signal(barrier, inc=1, device_id=(my_req, at_spot(step)), device_id_type=MESH)
    for step in range(1, req_count):
        pl.semaphore_signal(barrier, inc=1, device_id=(at_req(step), my_exp), device_id_type=MESH)

    widened = tokens_ref[0].astype(jnp.float32)
    factor = lax.rsqrt(jnp.mean(widened * widened, axis=-1, keepdims=True) + norm_eps)
    rows[0] = (widened * factor * gain_ref[...]).astype(jnp.bfloat16)
    up_all[0] = up_ref[...]
    for step in range(req_count):
        wanted_row = rows_wanted[at_req(step) * count + my_exp]
        row = wanted_row % table_rows
        staging[step, :rank] = down_ref[row]
        staging[step, rank:] = lift_ref[row]
        staging_narrow[step] = narrow_ref[row]
    offered[0] = staging[0]
    offered_narrow[0] = staging_narrow[0]
    pl.semaphore_wait(barrier, count - 1 + req_count - 1)

    def send_rows(source, target, towards):
        return pltpu.make_async_remote_copy(
            src_ref=rows.at[source],
            dst_ref=rows.at[target],
            send_sem=row_send.at[target],
            recv_sem=row_recv.at[target],
            device_id=(my_req, at_spot(towards)),
            device_id_type=MESH,
        )

    def send_part(source, side, towards):
        part = pl.ds(side * mid, mid)
        return pltpu.make_async_remote_copy(
            src_ref=rows.at[source, part],
            dst_ref=rows.at[last, part],
            send_sem=row_send.at[last + side],
            recv_sem=row_recv.at[last + side],
            device_id=(my_req, at_spot(towards)),
            device_id_type=MESH,
        )

    def send_low(source, target, towards):
        return pltpu.make_async_remote_copy(
            src_ref=low.at[source],
            dst_ref=low.at[target],
            send_sem=low_send.at[target],
            recv_sem=low_recv.at[target],
            device_id=(my_req, at_spot(towards)),
            device_id_type=MESH,
        )

    def send_down(step):
        return pltpu.make_async_remote_copy(
            src_ref=staging.at[step],
            dst_ref=offered.at[step],
            send_sem=down_send.at[step],
            recv_sem=down_recv.at[step],
            device_id=(at_req(step), my_exp),
            device_id_type=MESH,
        )

    def send_narrow(step):
        return pltpu.make_async_remote_copy(
            src_ref=staging_narrow.at[step],
            dst_ref=offered_narrow.at[step],
            send_sem=narrow_send.at[step],
            recv_sem=narrow_recv.at[step],
            device_id=(at_req(step), my_exp),
            device_id_type=MESH,
        )

    def send_up(step):
        return pltpu.make_async_remote_copy(
            src_ref=up_ref,
            dst_ref=up_all.at[step],
            send_sem=up_send.at[step],
            recv_sem=up_recv.at[step],
            device_id=(at_req(step), my_exp),
            device_id_type=MESH,
        )

    def send_att(slot):
        distance = (slot + 1) // 2 * (1 - 2 * (slot % 2))
        return pltpu.make_async_remote_copy(
            src_ref=att_out.at[slot],
            dst_ref=att_in.at[slot],
            send_sem=att_send.at[slot],
            recv_sem=att_recv.at[slot],
            device_id=(my_req, at_spot(distance)),
            device_id_type=MESH,
        )

    send_rows(0, 1, 1).start()
    send_rows(0, 2, -1).start()
    for step in range(1, req_count):
        send_down(step).start()
    for step in range(1, req_count):
        send_up(step).start()
        send_narrow(step).start()
    for head in range(heads):
        wide[:, head * 256 : head * 256 + 128] = weight_ref[head, :128].T
        wide[:, head * 256 + 128 : head * 256 + 256] = weight_ref[head, HEAD_WIDTH:].T
    for step in range(1, req_count):
        send_down(step).wait_recv()
    own_row = rows_wanted[my_req * count + my_exp]
    source = (my_req - own_row // table_rows + req_count) % req_count
    mine = offered[source]
    lift_out_ref[...] = mine[rank:]
    contract = (((1,), (1,)), ((), ()))
    low[0] = lax.dot_general(
        mine[:rank], rows[0], contract, preferred_element_type=jnp.float32
    ).astype(jnp.bfloat16)
    send_low(0, 1, 1).start()
    send_low(0, 2, -1).start()
    for step in range(1, req_count):
        send_up(step).wait_recv()
        send_narrow(step).wait_recv()
    narrow_out_ref[...] = offered_narrow[source]

    causal = lax.broadcasted_iota(jnp.int32, (seq, seq), 0) >= lax.broadcasted_iota(
        jnp.int32, (seq, seq), 1
    )
    cached_at = lax.broadcasted_iota(jnp.int32, (1, cache_ref.shape[2]), 1)
    kind = lax.broadcasted_iota(jnp.int32, (rank, 128), 0) // ADAPTER_RANK
    first = lax.broadcasted_iota(jnp.int32, (rank, 128), 1) < HEAD_WIDTH
    is_query = (kind == 0) & first
    is_kv = ((kind == 1) & first) | ((kind == 2) & jnp.logical_not(first))
    by_rank = (((0,), (0,)), ((), ()))
    front = lax.broadcasted_iota(jnp.int32, (1, 128), 1) < HEAD_WIDTH
    att_scale = HEAD_WIDTH ** (-0.5)

    def process(slot, carry):
        @pl.when((slot % 2 == 1) & (slot < last))
        def _():
            send_rows(0, slot, 1).wait_recv()

            @pl.when(slot < last - 2)
            def _():
                send_rows(slot, slot + 2, 1).start()

            @pl.when(slot == last - 2)
            def _():
                send_part(slot, 0, 1).start()

            send_rows(0, slot + 1, -1).wait_recv()

            @pl.when(slot < last - 2)
            def _():
                send_rows(slot + 1, slot + 3, -1).start()

            @pl.when(slot == last - 2)
            def _():
                send_part(slot + 1, 1, -1).start()

            send_low(0, slot, 1).wait_recv()
            send_low(slot, slot + 2, 1).start()
            send_low(0, slot + 1, -1).wait_recv()

            @pl.when(slot < last - 2)
            def _():
                send_low(slot + 1, slot + 3, -1).start()

        @pl.when(slot == last)
        def _():
            send_part(0, 0, 1).wait_recv()
            send_part(0, 1, -1).wait_recv()
            send_low(0, last, 1).wait_recv()

        distance = (slot + 1) // 2 * (1 - 2 * (slot % 2))
        owner = at_spot(distance)
        prompt = prompts[owner]
        length = lengths[prompt]
        wanted_row = rows_wanted[my_req * count + owner]
        up_one = up_all[
            (my_req - wanted_row // table_rows + req_count) % req_count, wanted_row % table_rows
        ]
        row_block = rows[slot]
        low_block = low[slot]
        visible = cached_at < length
        parts = []
        for head in range(heads):
            base = jnp.dot(
                row_block,
                wide[:, head * 256 : head * 256 + 256],
                preferred_element_type=jnp.float32,
            )
            up_head = up_one[:, head * 128 : head * 128 + 128]
            zero = jnp.zeros_like(up_head)
            extra_query = lax.dot_general(
                low_block,
                jnp.where(is_query, up_head, zero),
                by_rank,
                preferred_element_type=jnp.float32,
            )
            extra_kv = lax.dot_general(
                low_block,
                jnp.where(is_kv, up_head, zero),
                by_rank,
                preferred_element_type=jnp.float32,
            )
            query = jnp.where(front, base[:, :128], 0.0) + adapter_scale * extra_query
            query = query.astype(jnp.bfloat16)
            query = query * jnp.bfloat16(att_scale)
            own = (base[:, 128:] + adapter_scale * extra_kv).astype(jnp.bfloat16)
            cached = cache_ref[prompt, head]
            pre_scores = lax.dot_general(
                query, cached, contract, preferred_element_type=jnp.float32
            )
            own_scores = lax.dot_general(query, own, contract, preferred_element_type=jnp.float32)
            pre_scores = jnp.where(visible, pre_scores, masked_score)
            own_scores = jnp.where(causal, own_scores, masked_score)
            row_peak = jnp.maximum(
                jnp.max(pre_scores, axis=-1, keepdims=True),
                jnp.max(own_scores, axis=-1, keepdims=True),
            )
            pre_exp = jnp.exp(pre_scores - row_peak)
            own_exp = jnp.exp(own_scores - row_peak)
            denominator = jnp.sum(pre_exp, axis=-1, keepdims=True) + jnp.sum(
                own_exp, axis=-1, keepdims=True
            )
            total = jnp.dot(
                pre_exp.astype(jnp.bfloat16), cached, preferred_element_type=jnp.float32
            )
            total = total + jnp.dot(
                own_exp.astype(jnp.bfloat16), own, preferred_element_type=jnp.float32
            )
            parts.append((total / denominator)[:, HEAD_WIDTH:])
        joined = parts[0] if heads == 1 else jnp.concatenate(parts, axis=1)
        att_out[slot] = joined.astype(jnp.bfloat16)

        @pl.when(slot > 0)
        def _():
            send_att(slot).start()

        return carry

    lax.fori_loop(0, count, process, 0)

    out_ref[my_exp] = att_out[0]
    for slot in range(1, count):
        send_att(slot).wait_recv()
        distance = (slot + 1) // 2 * (2 * (slot % 2) - 1)
        out_ref[at_spot(distance)] = att_in[slot]
    for slot in range(1, last):
        send_rows(0, slot, 1).wait_send()
    send_part(0, 0, 1).wait_send()
    send_part(0, 1, -1).wait_send()
    for slot in range(1, count):
        send_low(0, slot, 1).wait_send()
        send_att(slot).wait_send()
    for step in range(1, req_count):
        send_down(step).wait_send()
        send_narrow(step).wait_send()
        send_up(step).wait_send()


def attend(tokens, gain, weight, cache, down, lift, narrow, up, prompts, lengths, rows_wanted):
    count = lax.axis_size("exp")
    req_count = lax.axis_size("req")
    _, seq, width = tokens.shape
    heads = cache.shape[1]
    wide = heads * HEAD_WIDTH
    rank = down.shape[1]
    packed = (req_count, rank + lift.shape[1], width)
    smem = pl.BlockSpec(memory_space=pltpu.SMEM)
    vmem = pl.BlockSpec(memory_space=pltpu.VMEM)
    dma = pltpu.SemaphoreType.DMA
    return pl.pallas_call(
        functools.partial(layer_kernel, (count, req_count, heads)),
        out_shape=(
            jax.ShapeDtypeStruct((count, seq, wide), jnp.bfloat16),
            jax.ShapeDtypeStruct(lift.shape[1:], jnp.bfloat16),
            jax.ShapeDtypeStruct(narrow.shape[1:], jnp.bfloat16),
        ),
        in_specs=[smem] * 3 + [vmem] * 8,
        out_specs=(vmem, vmem, vmem),
        scratch_shapes=[
            pltpu.VMEM((width, heads * 256), jnp.bfloat16),
            pltpu.VMEM((count, seq, width), jnp.bfloat16),
            pltpu.VMEM((count, rank, seq), jnp.bfloat16),
            pltpu.VMEM((count, seq, wide), jnp.bfloat16),
            pltpu.VMEM((count, seq, wide), jnp.bfloat16),
            pltpu.VMEM(packed, jnp.bfloat16),
            pltpu.VMEM(packed, jnp.bfloat16),
            pltpu.VMEM((req_count,) + narrow.shape[1:], jnp.bfloat16),
            pltpu.VMEM((req_count,) + narrow.shape[1:], jnp.bfloat16),
            pltpu.VMEM((req_count,) + up.shape, jnp.bfloat16),
            dma((count + 1,)),
            dma((count + 1,)),
            dma((count,)),
            dma((count,)),
            dma((count,)),
            dma((count,)),
            dma((req_count,)),
            dma((req_count,)),
            dma((req_count,)),
            dma((req_count,)),
            dma((req_count,)),
            dma((req_count,)),
        ],
        compiler_params=pltpu.CompilerParams(
            collective_id=0, has_side_effects=True, vmem_limit_bytes=52 * 1024 * 1024
        ),
        name="attend",
    )(prompts, lengths, rows_wanted, tokens, gain, weight, cache, down, lift, narrow, up)


def block_kernel(
    prompts,
    lengths,
    adapters,
    slot_rows,
    tokens_ref,
    gain_ref,
    weight_ref,
    cache_ref,
    down_ref,
    lift_ref,
    narrow_ref,
    up_ref,
    output_ref,
    expert_gain_ref,
    router_ref,
    routes_ref,
    slots_ref,
    outgoing_ref,
    hidden_ref,
    combine_ref,
    flat,
    wide_own,
    wide_far,
    keys_own,
    keys_far,
    rows,
    low,
    far_qkv,
    att_out,
    att_in,
    staging,
    offered,
    staging_lift,
    offered_lift,
    staging_narrow,
    offered_narrow,
    up_all,
    up_stage,
    up_far,
    weight_far,
    cache_stage,
    cache_far,
    row_send,
    row_recv,
    low_send,
    low_recv,
    att_send,
    att_recv,
    down_send,
    down_recv,
    lift_send,
    lift_recv,
    narrow_send,
    narrow_recv,
    up_send,
    up_recv,
    far_send,
    far_recv,
    across_send,
    across_recv,
    core_send,
    core_recv,
):
    count, req_count, prompt_rows = 8, 4, 2 * 1024
    seq = tokens_ref.shape[1]
    mid = seq // 2
    table_rows = down_ref.shape[0]
    rank = 3 * ADAPTER_RANK
    my_req = lax.axis_index("req")
    my_exp = lax.axis_index("exp")
    half = my_exp // 4
    my_y = my_exp % 2
    my_z = (my_exp // 2) % 2
    far_exp = (1 - half) * 4 + (1 - my_z) * 2 + my_y
    core_req = my_req + 1 - 2 * (my_req % 2)
    across_req = (my_req + 2) % req_count

    def at_slot(slot):
        return half * 4 + ((my_z + slot // 2) % 2) * 2 + (my_y + slot) % 2

    def mirrored(slot):
        return (1 - half) * 4 + ((my_z + slot // 2 + 1) % 2) * 2 + (my_y + slot) % 2

    def at_req(offset):
        return (my_req + offset) % req_count

    def row_of(request):
        return slot_rows[adapters[request]]

    def remote(source, target, sem_send, sem_recv, device):
        return pltpu.make_async_remote_copy(
            src_ref=source,
            dst_ref=target,
            send_sem=sem_send,
            recv_sem=sem_recv,
            device_id=device,
            device_id_type=MESH,
        )

    barrier = pltpu.get_barrier_semaphore()
    for slot in range(1, 4):
        pl.semaphore_signal(barrier, inc=1, device_id=(my_req, at_slot(slot)), device_id_type=MESH)
    pl.semaphore_signal(barrier, inc=1, device_id=(my_req, far_exp), device_id_type=MESH)
    for step in range(1, req_count):
        pl.semaphore_signal(barrier, inc=1, device_id=(at_req(step), my_exp), device_id_type=MESH)

    for step in range(req_count):
        row = row_of(at_req(step) * count + my_exp) % table_rows
        staging[step] = down_ref[row]
        staging_lift[step] = lift_ref[row]
        staging_narrow[step] = narrow_ref[row]
    offered[0] = staging[0]
    offered_lift[0] = staging_lift[0]
    offered_narrow[0] = staging_narrow[0]
    picked = lax.broadcasted_iota(jnp.int32, (rank, 2 * rank), 1) - 2 * lax.broadcasted_iota(
        jnp.int32, (rank, 2 * rank), 0
    )

    def pack(row, carry):
        table = up_ref[row]
        halves = [
            jnp.dot(
                (picked == head).astype(jnp.bfloat16), table, preferred_element_type=jnp.float32
            )
            for head in range(2)
        ]
        up_all[0, row] = jnp.concatenate(halves, axis=1).astype(jnp.bfloat16)
        return carry

    lax.fori_loop(0, table_rows, pack, 0)
    widened = tokens_ref[0].astype(jnp.float32)
    factor = lax.rsqrt(jnp.mean(widened * widened, axis=-1, keepdims=True) + norm_eps)
    rows[0] = (widened * factor * gain_ref[...]).astype(jnp.bfloat16)
    wq = weight_ref.shape[0] // req_count
    quarter = cache_stage.shape[0]
    third = quarter // 3
    granule = 32
    blocks = 1024 // granule
    ends = []
    total = 0
    for prompt in range(4):
        total = total + (lengths[prompt] + granule - 1) // granule
        ends.append(total)
    starts = [0] + ends[:3]

    def source_of(index):
        prompt = 0
        begin = 0
        for p in range(1, 4):
            past = index >= starts[p]
            prompt = jnp.where(past, p, prompt)
            begin = jnp.where(past, starts[p], begin)
        return prompt * blocks + jnp.minimum(index - begin, blocks - 1)

    def stage(index, carry):
        source = source_of(my_req * quarter + index)
        cache_stage[index] = cache_ref[source]
        return carry

    lax.fori_loop(0, quarter, stage, 0)
    pl.semaphore_wait(barrier, 7)

    def send_row_y():
        return remote(
            rows.at[0], rows.at[1], row_send.at[0], row_recv.at[0], (my_req, at_slot(1))
        )

    def send_row_z():
        return remote(
            rows.at[0], rows.at[2], row_send.at[1], row_recv.at[1], (my_req, at_slot(2))
        )

    def send_row_on():
        return remote(
            rows.at[2], rows.at[3], row_send.at[2], row_recv.at[2], (my_req, at_slot(1))
        )

    def send_low(slot):
        return remote(
            low.at[0], low.at[slot], low_send.at[slot], low_recv.at[slot], (my_req, at_slot(slot))
        )

    def send_att(kind, slot):
        return remote(
            att_out.at[kind, slot],
            att_in.at[kind, slot],
            att_send.at[kind, slot],
            att_recv.at[kind, slot],
            (my_req, at_slot(slot)),
        )

    def to_req(source, target, sem_send, sem_recv, step):
        return remote(
            source, target, sem_send.at[step], sem_recv.at[step], (at_req(step), my_exp)
        )

    def send_down(step):
        return to_req(staging.at[step], offered.at[step], down_send, down_recv, step)

    def send_lift(step):
        return to_req(staging_lift.at[step], offered_lift.at[step], lift_send, lift_recv, step)

    def send_narrow(step):
        return to_req(
            staging_narrow.at[step], offered_narrow.at[step], narrow_send, narrow_recv, step
        )

    def send_up(step):
        return to_req(up_all.at[0], up_all.at[step], up_send, up_recv, step)

    def send_up_far():
        return remote(up_stage, up_far, far_send.at[4], far_recv.at[4], (my_req, far_exp))

    def piece(owner, part):
        if part == 0:
            return weight_far.at[pl.ds(pl.multiple_of(owner * wq, 32), wq)]
        return cache_far.at[pl.ds(owner * quarter + (part - 1) * third, third)]

    def send_far(part):
        if part == 0:
            source = weight_ref.at[pl.ds(pl.multiple_of(my_req * wq, 32), wq)]
        else:
            source = cache_stage.at[pl.ds((part - 1) * third, third)]
        return remote(
            source,
            piece(my_req, part),
            far_send.at[part],
            far_recv.at[part],
            (my_req, far_exp),
        )

    def send_across(part):
        return remote(
            piece(my_req, part),
            piece(my_req, part),
            across_send.at[part],
            across_recv.at[part],
            (across_req, my_exp),
        )

    def take_across(part):
        return remote(
            piece(across_req, part),
            piece(across_req, part),
            across_send.at[part],
            across_recv.at[part],
            (across_req, my_exp),
        )

    def send_core(kind, part):
        owner = my_req if kind == 0 else across_req
        return remote(
            piece(owner, part),
            piece(owner, part),
            core_send.at[kind, part],
            core_recv.at[kind, part],
            (core_req, my_exp),
        )

    def take_core(kind, part):
        owner = core_req if kind == 0 else (core_req + 2) % req_count
        return remote(
            piece(owner, part),
            piece(owner, part),
            core_send.at[kind, part],
            core_recv.at[kind, part],
            (core_req, my_exp),
        )

    def pass_far(part):
        send_far(part).wait_recv()
        send_across(part).start()
        send_core(0, part).start()

    def pass_across(part):
        take_across(part).wait_recv()
        send_core(1, part).start()

    outer = my_z == half
    inner = my_z != half
    send_row_z().start()
    send_row_y().start()
    for step in range(1, req_count):
        send_down(step).start()
    for step in range(1, req_count):
        send_up(step).start()

    send_far(0).start()

    @pl.when(inner)
    def _():
        for part in range(1, 4):
            send_far(part).start()

    top = lax.broadcasted_iota(jnp.int32, (128, 1), 0) < HEAD_WIDTH

    def widen(source_ref, target_ref):
        for head in range(2):
            block = source_ref[head * 192 : head * 192 + 128]
            block = jnp.where(top, block, jnp.zeros_like(block))
            target_ref[:, head * 128 : head * 128 + 128] = block.T
            target_ref[:, 256 + head * 128 : 384 + head * 128] = source_ref[
                head * 192 + 64 : head * 192 + 192
            ].T

    row_kind = lax.broadcasted_iota(jnp.int32, (256, 128), 0) % 2
    first_rows = (row_kind == 0).astype(jnp.bfloat16)
    second_rows = (row_kind == 1).astype(jnp.bfloat16)

    def own_keys(index, carry):
        block = cache_ref[pl.ds(index * 4, 4)].reshape(256, 128)
        at = pl.ds(pl.multiple_of(index % 8 * 256, 256), 256)
        keys_own[index // 8, at, :128] = block * first_rows
        keys_own[index // 8, at, 128:] = block * second_rows
        return carry

    widen(weight_ref, wide_own)
    lax.fori_loop(0, 32, own_keys, 0)

    for step in range(1, req_count):
        send_down(step).wait_recv()
    own_row = row_of(my_req * count + my_exp)
    source = (my_req - own_row // table_rows + req_count) % req_count
    contract = (((1,), (1,)), ((), ()))
    low[0] = lax.dot_general(
        offered[source], rows[0], contract, preferred_element_type=jnp.float32
    ).astype(jnp.bfloat16)
    for slot in range(1, 4):
        send_low(slot).start()

    for step in range(1, req_count):
        send_up(step).wait_recv()

    def up_of(request):
        row = row_of(request)
        return up_all[(my_req - row // table_rows + req_count) % req_count, row % table_rows]

    for index in range(4):
        up_stage[index] = up_of(my_req * count + (1 - half) * 4 + index)
    send_up_far().start()
    for step in range(1, req_count):
        send_lift(step).start()
        send_narrow(step).start()

    @pl.when(inner)
    def _():
        pass_far(0)


    column = lax.broadcasted_iota(jnp.int32, (128, 512), 1)
    lane = lax.broadcasted_iota(jnp.int32, (128, 512), 0)
    spread = (lane == (column // 128 % 2) * HEAD_WIDTH + column % HEAD_WIDTH).astype(jnp.bfloat16)
    column = lax.broadcasted_iota(jnp.int32, (rank, 512), 1)
    kind = lax.broadcasted_iota(jnp.int32, (rank, 512), 0) // ADAPTER_RANK
    back = column % 128 // HEAD_WIDTH
    kept = kind == jnp.where(column < 256, 3 * back, 1 + back)
    by_rank = (((0,), (0,)), ((), ()))
    causal = lax.broadcasted_iota(jnp.int32, (seq, seq), 0) >= lax.broadcasted_iota(
        jnp.int32, (seq, seq), 1
    )
    cached_at = lax.broadcasted_iota(jnp.int32, (1, prompt_rows), 1)
    even = lax.broadcasted_iota(jnp.int32, (1, 128), 1) % 2 == 0
    att_scale = HEAD_WIDTH ** (-0.5)

    def project(slot, wide_ref, up_one):
        base = jnp.dot(rows[slot], wide_ref[...], preferred_element_type=jnp.float32)
        up_wide = jnp.dot(up_one, spread, preferred_element_type=jnp.float32)
        up_wide = jnp.where(kept, up_wide, 0.0).astype(jnp.bfloat16)
        extra = lax.dot_general(low[slot], up_wide, by_rank, preferred_element_type=jnp.float32)
        return (base + adapter_scale * extra).astype(jnp.bfloat16)

    def attention(qkv, keys, length):
        query = qkv[:, :256] * jnp.bfloat16(att_scale)
        scores = lax.dot_general(query, keys, contract, preferred_element_type=jnp.float32)
        scores = jnp.where(cached_at < 2 * length, scores, masked_score)
        own_scores = []
        for head in range(2):
            at = slice(head * 128, head * 128 + 128)
            own = qkv[:, 256 + head * 128 : 384 + head * 128]
            one = lax.dot_general(query[:, at], own, contract, preferred_element_type=jnp.float32)
            own_scores.append(jnp.where(causal, one, masked_score))
        tiles = prompt_rows // 128
        most = scores[:, :128]
        for tile in range(1, tiles):
            most = jnp.maximum(most, scores[:, tile * 128 : tile * 128 + 128])
        peaks = []
        for head in range(2):
            mine = even if head == 0 else jnp.logical_not(even)
            peaks.append(
                jnp.maximum(
                    jnp.max(jnp.where(mine, most, masked_score), axis=-1, keepdims=True),
                    jnp.max(own_scores[head], axis=-1, keepdims=True),
                )
            )
        peak = jnp.where(even, peaks[0], peaks[1])
        weights = []
        summed = jnp.zeros((seq, 128), jnp.float32)
        for tile in range(tiles):
            one = jnp.exp(scores[:, tile * 128 : tile * 128 + 128] - peak)
            summed = summed + one
            weights.append(one.astype(jnp.bfloat16))
        total = jnp.dot(
            jnp.concatenate(weights, axis=1), keys, preferred_element_type=jnp.float32
        )
        parts = []
        for head in range(2):
            mine = even if head == 0 else jnp.logical_not(even)
            own = qkv[:, 256 + head * 128 : 384 + head * 128]
            own_exp = jnp.exp(own_scores[head] - peaks[head])
            denominator = jnp.sum(
                jnp.where(mine, summed, 0.0), axis=-1, keepdims=True
            ) + jnp.sum(own_exp, axis=-1, keepdims=True)
            both = total[:, head * 128 : head * 128 + 128] + jnp.dot(
                own_exp.astype(jnp.bfloat16), own, preferred_element_type=jnp.float32
            )
            parts.append((both / denominator)[:, HEAD_WIDTH:])
        return jnp.concatenate(parts, axis=1).astype(jnp.bfloat16)

    def own_heads(slot, carry):
        @pl.when(slot == 1)
        def _():
            send_row_z().wait_recv()
            send_row_on().start()

            @pl.when(outer)
            def _():
                send_row_z().wait_send()
                for part in range(1, 4):
                    send_far(part).start()

            @pl.when(inner)
            def _():
                pass_far(1)
                pass_across(0)

            send_row_y().wait_recv()
            send_low(1).wait_recv()

        @pl.when(slot == 2)
        def _():
            send_low(2).wait_recv()

            @pl.when(outer)
            def _():
                pass_far(0)

            @pl.when(inner)
            def _():
                pass_far(2)
                pass_far(3)
                pass_across(1)

        @pl.when(slot == 3)
        def _():
            @pl.when(outer)
            def _():
                pass_across(0)
                pass_far(1)
                pass_far(2)
                pass_far(3)

            send_row_on().wait_recv()
            send_low(3).wait_recv()

            @pl.when(inner)
            def _():
                pass_across(2)

        owner = at_slot(slot)
        prompt = prompts[owner]
        qkv = project(slot, wide_own, up_of(my_req * count + owner))
        att_out[0, slot] = attention(qkv, keys_own[prompt], lengths[prompt])

        @pl.when(slot > 0)
        def _():
            send_att(0, slot).start()

        return carry

    lax.fori_loop(0, 4, own_heads, 0)

    @pl.when(outer)
    def _():
        pass_across(1)
        pass_across(2)

    take_core(0, 0).wait_recv()
    take_core(1, 0).wait_recv()
    send_up_far().wait_recv()
    widen(weight_far, wide_far)

    def far_project(slot, carry):
        index = ((my_z + slot // 2) % 2) * 2 + (my_y + slot) % 2
        far_qkv[slot] = project(slot, wide_far, up_far[index])
        return carry

    lax.fori_loop(0, 4, far_project, 0)

    pass_across(3)

    for part in range(1, 4):
        take_core(0, part).wait_recv()
        take_core(1, part).wait_recv()

    def unpack(index, carry):
        for prompt in range(4):
            for lane in range(4):
                block = cache_far[jnp.minimum(starts[prompt] + index * 4 + lane, 4 * quarter - 1)]
                at = pl.ds(pl.multiple_of(index * 256 + lane * 64, 64), 64)
                keys_far[prompt, at, :128] = block * first_rows[:64]
                keys_far[prompt, at, 128:] = block * second_rows[:64]
        return carry

    lax.fori_loop(0, blocks // 4, unpack, 0)

    def far_keys(slot):
        prompt = prompts[at_slot(slot)]
        return keys_far[prompt], lengths[prompt]

    def far_heads(step, carry):
        first, second = 3 - 2 * step, 2 - 2 * step
        att_first = attention(far_qkv[first], *far_keys(first))
        att_second = attention(far_qkv[second], *far_keys(second))
        att_out[1, first] = att_first
        att_out[1, second] = att_second
        send_att(1, first).start()

        @pl.when(second > 0)
        def _():
            send_att(1, second).start()

        return carry

    lax.fori_loop(0, 2, far_heads, 0)

    for step in range(1, req_count):
        send_lift(step).wait_recv()
        send_narrow(step).wait_recv()
    for kind in range(2):
        for slot in range(4):
            if slot > 0:
                send_att(kind, slot).wait_recv()
            at = pl.ds(pl.multiple_of((at_slot(slot) if kind == 0 else mirrored(slot)) * 128, 128), 128)
            flat[:, at] = att_out[kind, 0] if slot == 0 else att_in[kind, slot]

    attended = flat[...]
    narrow = offered_narrow[source]
    narrow = jnp.concatenate(
        [narrow[at : at + ADAPTER_RANK] for at in range(0, narrow.shape[0], ADAPTER_RANK)], axis=1
    )
    low_out = lax.dot_general(attended, narrow, contract, preferred_element_type=jnp.float32)
    lift = offered_lift[source]
    terms = []
    for _ in range(3):
        terms.append(low_out.astype(jnp.bfloat16))
        low_out = low_out - terms[-1].astype(jnp.float32)
    surplus = jnp.dot(
        jnp.concatenate(terms, axis=1),
        jnp.concatenate([lift] * 3, axis=0),
        preferred_element_type=jnp.float32,
    )
    plain = jnp.dot(attended, output_ref[...], preferred_element_type=jnp.float32)
    hidden = tokens_ref[0].astype(jnp.float32) + (plain + adapter_scale * surplus)
    hidden = hidden.astype(jnp.bfloat16)
    hidden_ref[...] = hidden
    moe_in = rms_norm(hidden, expert_gain_ref[...])
    cells = lax.broadcasted_iota(jnp.int32, (outgoing_ref.shape[0], seq), 0)
    capacity = outgoing_ref.shape[0] // count
    target = jnp.where(slots_ref[...] >= 0, routes_ref[...] * capacity + slots_ref[...], -1)
    sending = jnp.where(cells == target[0:1], 1.0, jnp.where(cells == target[1:2], 1.0, 0.0))
    outgoing_ref[...] = jnp.dot(
        sending.astype(jnp.bfloat16), moe_in, preferred_element_type=jnp.float32
    ).astype(jnp.bfloat16)
    gates = jax.nn.sigmoid(
        lax.dot_general(router_ref[...], moe_in, contract, preferred_element_type=jnp.float32)
    )
    gated = [
        sending[expert * capacity : (expert + 1) * capacity] * gates[expert : expert + 1]
        for expert in range(count)
    ]
    combine_ref[...] = jnp.concatenate(gated, axis=0).T

    send_row_y().wait_send()
    send_row_on().wait_send()

    @pl.when(inner)
    def _():
        send_row_z().wait_send()

    for slot in range(1, 4):
        send_low(slot).wait_send()
        for kind in range(2):
            send_att(kind, slot).wait_send()
    for step in range(1, req_count):
        send_down(step).wait_send()
        send_lift(step).wait_send()
        send_narrow(step).wait_send()
        send_up(step).wait_send()
    send_up_far().wait_send()
    for part in range(4):
        send_far(part).wait_send()
    for part in range(4):
        send_across(part).wait_send()
        send_core(0, part).wait_send()
        send_core(1, part).wait_send()


def attend_block(
    tokens,
    gain,
    weight,
    cache,
    down,
    lift,
    narrow,
    up,
    output,
    expert_gain,
    router,
    routes,
    slots,
    prompts,
    lengths,
    adapters,
    slot_rows,
):
    _, seq, width = tokens.shape
    rank = down.shape[1]
    experts = router.shape[0]
    cells = experts * (5 * seq * TOP // (4 * experts))
    smem = pl.BlockSpec(memory_space=pltpu.SMEM)
    vmem = pl.BlockSpec(memory_space=pltpu.VMEM)
    dma = pltpu.SemaphoreType.DMA

    def bf16(*shape):
        return pltpu.VMEM(shape, jnp.bfloat16)

    return pl.pallas_call(
        block_kernel,
        out_shape=(
            jax.ShapeDtypeStruct((cells, width), jnp.bfloat16),
            jax.ShapeDtypeStruct((seq, width), jnp.bfloat16),
            jax.ShapeDtypeStruct((seq, cells), jnp.float32),
        ),
        in_specs=[smem] * 4 + [vmem] * 13,
        out_specs=(vmem, vmem, vmem),
        scratch_shapes=[
            bf16(seq, width),
            bf16(width, 512),
            bf16(width, 512),
            bf16(4, 2048, 256),
            bf16(4, 2048, 256),
            bf16(4, seq, width),
            bf16(4, rank, seq),
            bf16(4, seq, 512),
            bf16(2, 4, seq, 128),
            bf16(2, 4, seq, 128),
            bf16(4, rank, width),
            bf16(4, rank, width),
            bf16(4, *lift.shape[1:]),
            bf16(4, *lift.shape[1:]),
            bf16(4, *narrow.shape[1:]),
            bf16(4, *narrow.shape[1:]),
            bf16(4, up.shape[0], rank, 128),
            bf16(4, rank, 128),
            bf16(4, rank, 128),
            bf16(*weight.shape),
            bf16(21, *cache.shape[1:]),
            bf16(84, *cache.shape[1:]),
            dma((5,)),
            dma((5,)),
            dma((4,)),
            dma((4,)),
            dma((2, 4)),
            dma((2, 4)),
            dma((4,)),
            dma((4,)),
            dma((4,)),
            dma((4,)),
            dma((4,)),
            dma((4,)),
            dma((4,)),
            dma((4,)),
            dma((5,)),
            dma((5,)),
            dma((4,)),
            dma((4,)),
            dma((2, 4)),
            dma((2, 4)),
        ],
        compiler_params=pltpu.CompilerParams(
            collective_id=2, has_side_effects=True, vmem_limit_bytes=56 * 1024 * 1024
        ),
        name="attend_block",
    )(
        prompts,
        lengths,
        adapters,
        slot_rows,
        tokens,
        gain,
        weight,
        cache,
        down,
        lift,
        narrow,
        up,
        output,
        expert_gain,
        router,
        routes,
        slots,
    )


def expert_block_kernel(
    outgoing_ref,
    gate_up_hbm,
    down_hbm,
    out_ref,
    gate_up,
    down,
    inbox,
    outbox,
    back,
    weight_sem,
    there_send,
    there_recv,
    back_send,
    back_recv,
):
    my_req = lax.axis_index("req")
    my_exp = lax.axis_index("exp")
    half = my_exp // 4
    my_y = my_exp % 2
    my_z = (my_exp // 2) % 2
    load_gate_up = pltpu.make_async_copy(gate_up_hbm.at[0], gate_up, weight_sem.at[0])
    load_down = pltpu.make_async_copy(down_hbm.at[0], down, weight_sem.at[1])
    load_gate_up.start()
    load_down.start()

    def partner(step):
        crossing, slot = step // 4, step % 4
        side = (half + crossing) % 2
        return side * 4 + ((my_z + slot // 2 + crossing) % 2) * 2 + (my_y + slot) % 2

    barrier = pltpu.get_barrier_semaphore()
    for step in range(1, 8):
        pl.semaphore_signal(barrier, inc=1, device_id=(my_req, partner(step)), device_id_type=MESH)
    inbox[0] = outgoing_ref[my_exp]
    pl.semaphore_wait(barrier, 7)

    def send_there(step):
        return pltpu.make_async_remote_copy(
            src_ref=outgoing_ref.at[partner(step)],
            dst_ref=inbox.at[step],
            send_sem=there_send.at[step],
            recv_sem=there_recv.at[step],
            device_id=(my_req, partner(step)),
            device_id_type=MESH,
        )

    def send_back(step):
        return pltpu.make_async_remote_copy(
            src_ref=outbox.at[step],
            dst_ref=back.at[step],
            send_sem=back_send.at[step],
            recv_sem=back_recv.at[step],
            device_id=(my_req, partner(step)),
            device_id_type=MESH,
        )

    for step in (1, 2, 3, 4, 5, 6, 7):
        send_there(step).start()
    load_gate_up.wait()
    load_down.wait()
    cap, width = inbox.shape[1:]
    chunk = FF // 2

    def process(pair, carry):
        @pl.when(pair > 0)
        def _():
            send_there(2 * pair).wait_recv()

        send_there(2 * pair + 1).wait_recv()
        received = inbox[pl.ds(2 * pair, 2)].reshape(2 * cap, width)
        total = jnp.zeros((2 * cap, width), jnp.float32)
        for part in range(2):
            gate = jnp.dot(
                received,
                gate_up[:, part * chunk : (part + 1) * chunk],
                preferred_element_type=jnp.float32,
            )
            up = jnp.dot(
                received,
                gate_up[:, FF + part * chunk : FF + (part + 1) * chunk],
                preferred_element_type=jnp.float32,
            )
            activated = (jax.nn.gelu(gate, approximate=True) * up).astype(jnp.bfloat16)
            total = total + jnp.dot(
                activated,
                down[part * chunk : (part + 1) * chunk],
                preferred_element_type=jnp.float32,
            )
        outbox[pl.ds(2 * pair, 2)] = total.reshape(2, cap, width).astype(jnp.bfloat16)

        @pl.when(pair > 0)
        def _():
            send_back(2 * pair).start()

        send_back(2 * pair + 1).start()
        return carry

    lax.fori_loop(0, 4, process, 0)
    out_ref[my_exp] = outbox[0]
    for step in range(1, 8):
        send_back(step).wait_recv()
        out_ref[partner(step)] = back[step]
    for step in range(1, 8):
        send_there(step).wait_send()
    for step in range(1, 8):
        send_back(step).wait_send()


def expert_kernel(
    count,
    outgoing_ref,
    gate_up_hbm,
    down_hbm,
    out_ref,
    gate_up,
    down,
    inbox,
    outbox,
    back,
    weight_sem,
    there_send,
    there_recv,
    back_send,
    back_recv,
):
    my_req = lax.axis_index("req")
    my_exp = lax.axis_index("exp")
    load_gate_up = pltpu.make_async_copy(gate_up_hbm.at[0], gate_up, weight_sem.at[0])
    load_down = pltpu.make_async_copy(down_hbm.at[0], down, weight_sem.at[1])
    load_gate_up.start()
    load_down.start()

    def at_exp(offset):
        return (my_exp + offset + count) % count

    barrier = pltpu.get_barrier_semaphore()
    for step in range(1, count):
        pl.semaphore_signal(barrier, inc=1, device_id=(my_req, at_exp(step)), device_id_type=MESH)
    inbox[0] = outgoing_ref[my_exp]
    pl.semaphore_wait(barrier, count - 1)

    def send_there(step):
        return pltpu.make_async_remote_copy(
            src_ref=outgoing_ref.at[at_exp(step)],
            dst_ref=inbox.at[step],
            send_sem=there_send.at[step],
            recv_sem=there_recv.at[step],
            device_id=(my_req, at_exp(step)),
            device_id_type=MESH,
        )

    def send_back(step):
        return pltpu.make_async_remote_copy(
            src_ref=outbox.at[step],
            dst_ref=back.at[step],
            send_sem=back_send.at[step],
            recv_sem=back_recv.at[step],
            device_id=(my_req, at_exp(-step)),
            device_id_type=MESH,
        )

    for step in range(1, count):
        send_there(step).start()
    load_gate_up.wait()
    load_down.wait()
    cap, width = inbox.shape[1:]
    chunk = FF // 2

    def process(pair, carry):
        @pl.when(pair > 0)
        def _():
            send_there(2 * pair).wait_recv()

        send_there(2 * pair + 1).wait_recv()
        received = inbox[pl.ds(2 * pair, 2)].reshape(2 * cap, width)
        total = jnp.zeros((2 * cap, width), jnp.float32)
        for part in range(2):
            gate = jnp.dot(
                received,
                gate_up[:, part * chunk : (part + 1) * chunk],
                preferred_element_type=jnp.float32,
            )
            up = jnp.dot(
                received,
                gate_up[:, FF + part * chunk : FF + (part + 1) * chunk],
                preferred_element_type=jnp.float32,
            )
            activated = (jax.nn.gelu(gate, approximate=True) * up).astype(jnp.bfloat16)
            total = total + jnp.dot(
                activated,
                down[part * chunk : (part + 1) * chunk],
                preferred_element_type=jnp.float32,
            )
        outbox[pl.ds(2 * pair, 2)] = total.reshape(2, cap, width).astype(jnp.bfloat16)

        @pl.when(pair > 0)
        def _():
            send_back(2 * pair).start()

        send_back(2 * pair + 1).start()
        return carry

    lax.fori_loop(0, count // 2, process, 0)
    out_ref[my_exp] = outbox[0]
    for step in range(1, count):
        send_back(step).wait_recv()
        out_ref[at_exp(step)] = back[step]
    for step in range(1, count):
        send_there(step).wait_send()
        send_back(step).wait_send()


def run_experts(outgoing, gate_up, down, blocks=False):
    count, cap, width = outgoing.shape
    vmem = pl.BlockSpec(memory_space=pltpu.VMEM)
    hbm = pl.BlockSpec(memory_space=pl.ANY)
    dma = pltpu.SemaphoreType.DMA
    block = pltpu.VMEM(outgoing.shape, jnp.bfloat16)
    return pl.pallas_call(
        expert_block_kernel if blocks else functools.partial(expert_kernel, count),
        out_shape=jax.ShapeDtypeStruct(outgoing.shape, jnp.bfloat16),
        in_specs=[vmem, hbm, hbm],
        out_specs=vmem,
        scratch_shapes=[
            pltpu.VMEM(gate_up.shape[1:], jnp.bfloat16),
            pltpu.VMEM(down.shape[1:], jnp.bfloat16),
            block,
            block,
            block,
            dma((2,)),
            dma((count,)),
            dma((count,)),
            dma((count,)),
            dma((count,)),
        ],
        compiler_params=pltpu.CompilerParams(
            collective_id=3 if blocks else 1, has_side_effects=True, vmem_limit_bytes=52 * 1024 * 1024
        ),
        name="experts",
    )(outgoing, gate_up, down)


def body(
    tokens,
    attention_norm_gain,
    expert_norm_gain,
    query_key_value_weight,
    output_weight,
    prompt_key_value_cache,
    shared_prompt_length,
    prompt_per_request,
    adapter_per_request,
    adapter_slot_rows,
    adapter_down_qkv,
    adapter_up_qkv,
    adapter_down_output,
    adapter_up_output,
    router_weight,
    expert_gate_up_weight,
    expert_down_weight,
    routes,
    slots,
):
    heads_here = query_key_value_weight.shape[1]
    seq_whole = tokens.shape[1]
    table_rows = adapter_down_qkv.shape[0]
    narrow = jnp.swapaxes(adapter_down_output, 2, 3).reshape(table_rows, -1, HEAD_WIDTH)
    if (lax.axis_size("exp"), lax.axis_size("req"), heads_here) == (8, 4, 2):
        outgoing, hidden, combine = attend_block(
            tokens,
            attention_norm_gain[None],
            jnp.transpose(query_key_value_weight, (1, 2, 0)).reshape(-1, MODEL_WIDTH),
            prompt_key_value_cache.reshape(-1, 64, 2 * HEAD_WIDTH),
            jnp.swapaxes(adapter_down_qkv, 1, 2),
            adapter_up_output,
            narrow,
            adapter_up_qkv.reshape(table_rows, 6 * ADAPTER_RANK, HEAD_WIDTH),
            output_weight.reshape(-1, MODEL_WIDTH),
            expert_norm_gain[None],
            router_weight.T,
            routes[0].T,
            slots[0].T,
            prompt_per_request,
            shared_prompt_length,
            adapter_per_request,
            adapter_slot_rows,
        )
        returned = run_experts(
            outgoing.reshape(router_weight.shape[1], -1, MODEL_WIDTH),
            expert_gate_up_weight,
            expert_down_weight,
            blocks=True,
        )
        moe_sum = jnp.dot(
            combine,
            returned.reshape(-1, MODEL_WIDTH).astype(jnp.float32),
            precision=lax.Precision.HIGH,
        )
        return (hidden.astype(jnp.float32) + moe_sum).astype(jnp.bfloat16)[None]

    wanted_all = adapter_slot_rows[adapter_per_request]

    up_twice = jnp.concatenate([adapter_up_qkv, adapter_up_qkv], axis=-1).reshape(
        table_rows, 3 * ADAPTER_RANK, heads_here * 2 * HEAD_WIDTH
    )
    gathered, own_bo, own_ao = attend(
        tokens,
        attention_norm_gain[None],
        jnp.transpose(query_key_value_weight, (1, 2, 0)),
        jnp.swapaxes(prompt_key_value_cache, 1, 2),
        jnp.swapaxes(adapter_down_qkv, 1, 2),
        adapter_up_output,
        narrow,
        up_twice,
        prompt_per_request,
        shared_prompt_length,
        wanted_all,
    )
    flat_att = jnp.swapaxes(gathered, 0, 1).reshape(seq_whole, -1)
    plain_out = jnp.dot(
        flat_att, output_weight.reshape(-1, MODEL_WIDTH), preferred_element_type=jnp.float32
    )
    own_ao = jnp.swapaxes(own_ao.reshape(-1, ADAPTER_RANK, HEAD_WIDTH), 1, 2)
    low_out = jnp.dot(
        flat_att, own_ao.reshape(-1, ADAPTER_RANK), preferred_element_type=jnp.float32
    )
    surplus = lax.dot_general(
        low_out,
        own_bo.astype(jnp.float32),
        (((1,), (0,)), ((), ())),
        precision=lax.Precision.HIGHEST,
    )
    projected_rows = (plain_out + adapter_scale * surplus)[None]
    hidden = (tokens.astype(jnp.float32) + projected_rows).astype(jnp.bfloat16)
    moe_in = rms_norm(hidden, expert_norm_gain)
    rows_here = REQ_DEV * seq_whole
    flat_in = moe_in.reshape(rows_here, MODEL_WIDTH)
    gate_vals = jax.nn.sigmoid(jnp.dot(flat_in, router_weight, preferred_element_type=jnp.float32))
    expert_count = router_weight.shape[1]
    capacity = 5 * rows_here * TOP // (4 * expert_count)
    route_flat = routes.reshape(rows_here, TOP)
    slot_flat = slots.reshape(rows_here, TOP)
    target = jnp.where(slot_flat >= 0, route_flat * capacity + slot_flat, -1)
    cells = jnp.arange(expert_count * capacity, dtype=jnp.int32)
    matched = target[:, :, None] == cells[None, None, :]
    named = route_flat[:, :, None] == jnp.arange(expert_count, dtype=jnp.int32)[None, None, :]
    chosen_gate = jnp.sum(jnp.where(named, gate_vals[:, None, :], 0.0), axis=2)
    combine = jnp.sum(jnp.where(matched, chosen_gate[:, :, None], 0.0), axis=1)
    sending = jnp.any(matched, axis=1).astype(jnp.bfloat16)
    outgoing = jnp.einsum("rc,rd->cd", sending, flat_in, preferred_element_type=jnp.float32).astype(
        jnp.bfloat16
    )
    returned = run_experts(
        outgoing.reshape(expert_count, capacity, MODEL_WIDTH),
        expert_gate_up_weight,
        expert_down_weight,
    )
    returned_wide = returned.reshape(expert_count * capacity, MODEL_WIDTH).astype(jnp.float32)
    moe_sum = jnp.dot(combine, returned_wide, precision=lax.Precision.HIGHEST)
    mixed = (hidden.reshape(rows_here, MODEL_WIDTH).astype(jnp.float32) + moe_sum).astype(
        jnp.bfloat16
    )
    return mixed.reshape(tokens.shape)


def solution(mesh):
    in_specs = (
        P(("req", "exp"), None, None),
        P(),
        P(),
        P(None, "exp", None),
        P(),
        P(None, None, "exp", None),
        P(),
        P("req"),
        P(),
        P(),
        P("req", None, None),
        P("req", None, None, "exp", None),
        P("req", None, None, None),
        P("req", None, None),
        P(),
        P("exp", None, None),
        P("exp", None, None),
        P(("req", "exp"), None, None),
        P(("req", "exp"), None, None),
    )
    out_specs = P(("req", "exp"), None, None)
    return jax.shard_map(body, mesh=mesh, in_specs=in_specs, out_specs=out_specs, check_vma=False)
```

```python
import functools

import jax
import jax.numpy as jnp
from jax import lax
from jax.experimental import pallas as pl
from jax.experimental.pallas import tpu as pltpu
from jax.sharding import PartitionSpec as P

MODEL_WIDTH = 1024
HEAD_WIDTH = 64
FF = 2816
ADAPTER_RANK = 16
TOP = 2
REQ_DEV = 1


adapter_scale = 0.5
norm_eps = 1e-06
MESH = pl.DeviceIdType.MESH
masked_score = -1e30


def rms_norm(values, gain):
    widened = values.astype(jnp.float32)
    factor = lax.rsqrt(jnp.mean(widened * widened, axis=-1, keepdims=True) + norm_eps)
    return (widened * factor * gain).astype(jnp.bfloat16)


def ring_device(spot, count):
    turned = spot // (count // 2)
    return 2 * (spot + turned * (count - 1 - 2 * spot)) + turned


def layer_kernel(
    sizes,
    prompts,
    lengths,
    rows_wanted,
    tokens_ref,
    gain_ref,
    weight_ref,
    cache_ref,
    down_ref,
    lift_ref,
    narrow_ref,
    up_ref,
    out_ref,
    lift_out_ref,
    narrow_out_ref,
    wide,
    rows,
    low,
    att_out,
    att_in,
    staging,
    offered,
    staging_narrow,
    offered_narrow,
    up_all,
    row_send,
    row_recv,
    low_send,
    low_recv,
    att_send,
    att_recv,
    down_send,
    down_recv,
    narrow_send,
    narrow_recv,
    up_send,
    up_recv,
):
    count, req_count, heads = sizes
    half = count // 2
    last = count - 1
    seq = tokens_ref.shape[1]
    mid = seq // 2
    table_rows = down_ref.shape[0]
    rank = 3 * ADAPTER_RANK
    my_req = lax.axis_index("req")
    my_exp = lax.axis_index("exp")
    my_side = my_exp % 2
    my_spot = my_exp // 2 + my_side * (count - 1 - 2 * (my_exp // 2))

    def at_spot(offset):
        return ring_device((my_spot + offset + count) % count, count)

    def at_req(offset):
        return (my_req + offset) % req_count

    barrier = pltpu.get_barrier_semaphore()
    for step in range(1, count):
        pl.semaphore_signal(barrier, inc=1, device_id=(my_req, at_spot(step)), device_id_type=MESH)
    for step in range(1, req_count):
        pl.semaphore_signal(barrier, inc=1, device_id=(at_req(step), my_exp), device_id_type=MESH)

    widened = tokens_ref[0].astype(jnp.float32)
    factor = lax.rsqrt(jnp.mean(widened * widened, axis=-1, keepdims=True) + norm_eps)
    rows[0] = (widened * factor * gain_ref[...]).astype(jnp.bfloat16)
    up_all[0] = up_ref[...]
    for step in range(req_count):
        wanted_row = rows_wanted[at_req(step) * count + my_exp]
        row = wanted_row % table_rows
        staging[step, :rank] = down_ref[row]
        staging[step, rank:] = lift_ref[row]
        staging_narrow[step] = narrow_ref[row]
    offered[0] = staging[0]
    offered_narrow[0] = staging_narrow[0]
    pl.semaphore_wait(barrier, count - 1 + req_count - 1)

    def send_rows(source, target, towards):
        return pltpu.make_async_remote_copy(
            src_ref=rows.at[source],
            dst_ref=rows.at[target],
            send_sem=row_send.at[target],
            recv_sem=row_recv.at[target],
            device_id=(my_req, at_spot(towards)),
            device_id_type=MESH,
        )

    def send_part(source, side, towards):
        part = pl.ds(side * mid, mid)
        return pltpu.make_async_remote_copy(
            src_ref=rows.at[source, part],
            dst_ref=rows.at[last, part],
            send_sem=row_send.at[last + side],
            recv_sem=row_recv.at[last + side],
            device_id=(my_req, at_spot(towards)),
            device_id_type=MESH,
        )

    def send_low(source, target, towards):
        return pltpu.make_async_remote_copy(
            src_ref=low.at[source],
            dst_ref=low.at[target],
            send_sem=low_send.at[target],
            recv_sem=low_recv.at[target],
            device_id=(my_req, at_spot(towards)),
            device_id_type=MESH,
        )

    def send_down(step):
        return pltpu.make_async_remote_copy(
            src_ref=staging.at[step],
            dst_ref=offered.at[step],
            send_sem=down_send.at[step],
            recv_sem=down_recv.at[step],
            device_id=(at_req(step), my_exp),
            device_id_type=MESH,
        )

    def send_narrow(step):
        return pltpu.make_async_remote_copy(
            src_ref=staging_narrow.at[step],
            dst_ref=offered_narrow.at[step],
            send_sem=narrow_send.at[step],
            recv_sem=narrow_recv.at[step],
            device_id=(at_req(step), my_exp),
            device_id_type=MESH,
        )

    def send_up(step):
        return pltpu.make_async_remote_copy(
            src_ref=up_ref,
            dst_ref=up_all.at[step],
            send_sem=up_send.at[step],
            recv_sem=up_recv.at[step],
            device_id=(at_req(step), my_exp),
            device_id_type=MESH,
        )

    def send_att(slot):
        distance = (slot + 1) // 2 * (1 - 2 * (slot % 2))
        return pltpu.make_async_remote_copy(
            src_ref=att_out.at[slot],
            dst_ref=att_in.at[slot],
            send_sem=att_send.at[slot],
            recv_sem=att_recv.at[slot],
            device_id=(my_req, at_spot(distance)),
            device_id_type=MESH,
        )

    send_rows(0, 1, 1).start()
    send_rows(0, 2, -1).start()
    for step in range(1, req_count):
        send_down(step).start()
    for step in range(1, req_count):
        send_up(step).start()
        send_narrow(step).start()
    for head in range(heads):
        wide[:, head * 256 : head * 256 + 128] = weight_ref[head, :128].T
        wide[:, head * 256 + 128 : head * 256 + 256] = weight_ref[head, HEAD_WIDTH:].T
    for step in range(1, req_count):
        send_down(step).wait_recv()
    own_row = rows_wanted[my_req * count + my_exp]
    source = (my_req - own_row // table_rows + req_count) % req_count
    mine = offered[source]
    lift_out_ref[...] = mine[rank:]
    contract = (((1,), (1,)), ((), ()))
    low[0] = lax.dot_general(
        mine[:rank], rows[0], contract, preferred_element_type=jnp.float32
    ).astype(jnp.bfloat16)
    send_low(0, 1, 1).start()
    send_low(0, 2, -1).start()
    for step in range(1, req_count):
        send_up(step).wait_recv()
        send_narrow(step).wait_recv()
    narrow_out_ref[...] = offered_narrow[source]

    causal = lax.broadcasted_iota(jnp.int32, (seq, seq), 0) >= lax.broadcasted_iota(
        jnp.int32, (seq, seq), 1
    )
    cached_at = lax.broadcasted_iota(jnp.int32, (1, cache_ref.shape[2]), 1)
    kind = lax.broadcasted_iota(jnp.int32, (rank, 128), 0) // ADAPTER_RANK
    first = lax.broadcasted_iota(jnp.int32, (rank, 128), 1) < HEAD_WIDTH
    is_query = (kind == 0) & first
    is_kv = ((kind == 1) & first) | ((kind == 2) & jnp.logical_not(first))
    by_rank = (((0,), (0,)), ((), ()))
    front = lax.broadcasted_iota(jnp.int32, (1, 128), 1) < HEAD_WIDTH
    att_scale = HEAD_WIDTH ** (-0.5)

    def process(slot, carry):
        @pl.when((slot % 2 == 1) & (slot < last))
        def _():
            send_rows(0, slot, 1).wait_recv()

            @pl.when(slot < last - 2)
            def _():
                send_rows(slot, slot + 2, 1).start()

            @pl.when(slot == last - 2)
            def _():
                send_part(slot, 0, 1).start()

            send_rows(0, slot + 1, -1).wait_recv()

            @pl.when(slot < last - 2)
            def _():
                send_rows(slot + 1, slot + 3, -1).start()

            @pl.when(slot == last - 2)
            def _():
                send_part(slot + 1, 1, -1).start()

            send_low(0, slot, 1).wait_recv()
            send_low(slot, slot + 2, 1).start()
            send_low(0, slot + 1, -1).wait_recv()

            @pl.when(slot < last - 2)
            def _():
                send_low(slot + 1, slot + 3, -1).start()

        @pl.when(slot == last)
        def _():
            send_part(0, 0, 1).wait_recv()
            send_part(0, 1, -1).wait_recv()
            send_low(0, last, 1).wait_recv()

        distance = (slot + 1) // 2 * (1 - 2 * (slot % 2))
        owner = at_spot(distance)
        prompt = prompts[owner]
        length = lengths[prompt]
        wanted_row = rows_wanted[my_req * count + owner]
        up_one = up_all[
            (my_req - wanted_row // table_rows + req_count) % req_count, wanted_row % table_rows
        ]
        row_block = rows[slot]
        low_block = low[slot]
        visible = cached_at < length
        parts = []
        for head in range(heads):
            base = jnp.dot(
                row_block,
                wide[:, head * 256 : head * 256 + 256],
                preferred_element_type=jnp.float32,
            )
            up_head = up_one[:, head * 128 : head * 128 + 128]
            zero = jnp.zeros_like(up_head)
            extra_query = lax.dot_general(
                low_block,
                jnp.where(is_query, up_head, zero),
                by_rank,
                preferred_element_type=jnp.float32,
            )
            extra_kv = lax.dot_general(
                low_block,
                jnp.where(is_kv, up_head, zero),
                by_rank,
                preferred_element_type=jnp.float32,
            )
            query = jnp.where(front, base[:, :128], 0.0) + adapter_scale * extra_query
            query = query.astype(jnp.bfloat16)
            query = query * jnp.bfloat16(att_scale)
            own = (base[:, 128:] + adapter_scale * extra_kv).astype(jnp.bfloat16)
            cached = cache_ref[prompt, head]
            pre_scores = lax.dot_general(
                query, cached, contract, preferred_element_type=jnp.float32
            )
            own_scores = lax.dot_general(query, own, contract, preferred_element_type=jnp.float32)
            pre_scores = jnp.where(visible, pre_scores, masked_score)
            own_scores = jnp.where(causal, own_scores, masked_score)
            row_peak = jnp.maximum(
                jnp.max(pre_scores, axis=-1, keepdims=True),
                jnp.max(own_scores, axis=-1, keepdims=True),
            )
            pre_exp = jnp.exp(pre_scores - row_peak)
            own_exp = jnp.exp(own_scores - row_peak)
            denominator = jnp.sum(pre_exp, axis=-1, keepdims=True) + jnp.sum(
                own_exp, axis=-1, keepdims=True
            )
            total = jnp.dot(
                pre_exp.astype(jnp.bfloat16), cached, preferred_element_type=jnp.float32
            )
            total = total + jnp.dot(
                own_exp.astype(jnp.bfloat16), own, preferred_element_type=jnp.float32
            )
            parts.append((total / denominator)[:, HEAD_WIDTH:])
        joined = parts[0] if heads == 1 else jnp.concatenate(parts, axis=1)
        att_out[slot] = joined.astype(jnp.bfloat16)

        @pl.when(slot > 0)
        def _():
            send_att(slot).start()

        return carry

    lax.fori_loop(0, count, process, 0)

    out_ref[my_exp] = att_out[0]
    for slot in range(1, count):
        send_att(slot).wait_recv()
        distance = (slot + 1) // 2 * (2 * (slot % 2) - 1)
        out_ref[at_spot(distance)] = att_in[slot]
    for slot in range(1, last):
        send_rows(0, slot, 1).wait_send()
    send_part(0, 0, 1).wait_send()
    send_part(0, 1, -1).wait_send()
    for slot in range(1, count):
        send_low(0, slot, 1).wait_send()
        send_att(slot).wait_send()
    for step in range(1, req_count):
        send_down(step).wait_send()
        send_narrow(step).wait_send()
        send_up(step).wait_send()


def attend(tokens, gain, weight, cache, down, lift, narrow, up, prompts, lengths, rows_wanted):
    count = lax.axis_size("exp")
    req_count = lax.axis_size("req")
    _, seq, width = tokens.shape
    heads = cache.shape[1]
    wide = heads * HEAD_WIDTH
    rank = down.shape[1]
    packed = (req_count, rank + lift.shape[1], width)
    smem = pl.BlockSpec(memory_space=pltpu.SMEM)
    vmem = pl.BlockSpec(memory_space=pltpu.VMEM)
    dma = pltpu.SemaphoreType.DMA
    return pl.pallas_call(
        functools.partial(layer_kernel, (count, req_count, heads)),
        out_shape=(
            jax.ShapeDtypeStruct((count, seq, wide), jnp.bfloat16),
            jax.ShapeDtypeStruct(lift.shape[1:], jnp.bfloat16),
            jax.ShapeDtypeStruct(narrow.shape[1:], jnp.bfloat16),
        ),
        in_specs=[smem] * 3 + [vmem] * 8,
        out_specs=(vmem, vmem, vmem),
        scratch_shapes=[
            pltpu.VMEM((width, heads * 256), jnp.bfloat16),
            pltpu.VMEM((count, seq, width), jnp.bfloat16),
            pltpu.VMEM((count, rank, seq), jnp.bfloat16),
            pltpu.VMEM((count, seq, wide), jnp.bfloat16),
            pltpu.VMEM((count, seq, wide), jnp.bfloat16),
            pltpu.VMEM(packed, jnp.bfloat16),
            pltpu.VMEM(packed, jnp.bfloat16),
            pltpu.VMEM((req_count,) + narrow.shape[1:], jnp.bfloat16),
            pltpu.VMEM((req_count,) + narrow.shape[1:], jnp.bfloat16),
            pltpu.VMEM((req_count,) + up.shape, jnp.bfloat16),
            dma((count + 1,)),
            dma((count + 1,)),
            dma((count,)),
            dma((count,)),
            dma((count,)),
            dma((count,)),
            dma((req_count,)),
            dma((req_count,)),
            dma((req_count,)),
            dma((req_count,)),
            dma((req_count,)),
            dma((req_count,)),
        ],
        compiler_params=pltpu.CompilerParams(
            collective_id=0, has_side_effects=True, vmem_limit_bytes=52 * 1024 * 1024
        ),
        name="attend",
    )(prompts, lengths, rows_wanted, tokens, gain, weight, cache, down, lift, narrow, up)


def block_kernel(
    prompts,
    lengths,
    adapters,
    slot_rows,
    tokens_ref,
    gain_ref,
    weight_ref,
    cache_ref,
    down_ref,
    lift_ref,
    narrow_ref,
    up_ref,
    output_ref,
    expert_gain_ref,
    router_ref,
    routes_ref,
    slots_ref,
    outgoing_ref,
    hidden_ref,
    combine_ref,
    flat,
    wide_own,
    wide_far,
    keys_own,
    keys_far,
    rows,
    low,
    far_qkv,
    att_out,
    att_in,
    staging,
    offered,
    staging_lift,
    offered_lift,
    staging_narrow,
    offered_narrow,
    up_all,
    up_stage,
    up_far,
    weight_far,
    cache_stage,
    cache_far,
    row_send,
    row_recv,
    low_send,
    low_recv,
    att_send,
    att_recv,
    down_send,
    down_recv,
    lift_send,
    lift_recv,
    narrow_send,
    narrow_recv,
    up_send,
    up_recv,
    far_send,
    far_recv,
    across_send,
    across_recv,
    core_send,
    core_recv,
):
    count, req_count, prompt_rows = 8, 4, 2 * 1024
    seq = tokens_ref.shape[1]
    mid = seq // 2
    table_rows = down_ref.shape[0]
    rank = 3 * ADAPTER_RANK
    my_req = lax.axis_index("req")
    my_exp = lax.axis_index("exp")
    half = my_exp // 4
    my_y = my_exp % 2
    my_z = (my_exp // 2) % 2
    far_exp = (1 - half) * 4 + (1 - my_z) * 2 + my_y
    core_req = my_req + 1 - 2 * (my_req % 2)
    across_req = (my_req + 2) % req_count

    def at_slot(slot):
        return half * 4 + ((my_z + slot // 2) % 2) * 2 + (my_y + slot) % 2

    def mirrored(slot):
        return (1 - half) * 4 + ((my_z + slot // 2 + 1) % 2) * 2 + (my_y + slot) % 2

    def at_req(offset):
        return (my_req + offset) % req_count

    def row_of(request):
        return slot_rows[adapters[request]]

    def remote(source, target, sem_send, sem_recv, device):
        return pltpu.make_async_remote_copy(
            src_ref=source,
            dst_ref=target,
            send_sem=sem_send,
            recv_sem=sem_recv,
            device_id=device,
            device_id_type=MESH,
        )

    barrier = pltpu.get_barrier_semaphore()
    for slot in range(1, 4):
        pl.semaphore_signal(barrier, inc=1, device_id=(my_req, at_slot(slot)), device_id_type=MESH)
    pl.semaphore_signal(barrier, inc=1, device_id=(my_req, far_exp), device_id_type=MESH)
    for step in range(1, req_count):
        pl.semaphore_signal(barrier, inc=1, device_id=(at_req(step), my_exp), device_id_type=MESH)

    for step in range(req_count):
        row = row_of(at_req(step) * count + my_exp) % table_rows
        staging[step] = down_ref[row]
        staging_lift[step] = lift_ref[row]
        staging_narrow[step] = narrow_ref[row]
    offered[0] = staging[0]
    offered_lift[0] = staging_lift[0]
    offered_narrow[0] = staging_narrow[0]
    picked = lax.broadcasted_iota(jnp.int32, (rank, 2 * rank), 1) - 2 * lax.broadcasted_iota(
        jnp.int32, (rank, 2 * rank), 0
    )

    def pack(row, carry):
        table = up_ref[row]
        halves = [
            jnp.dot(
                (picked == head).astype(jnp.bfloat16), table, preferred_element_type=jnp.float32
            )
            for head in range(2)
        ]
        up_all[0, row] = jnp.concatenate(halves, axis=1).astype(jnp.bfloat16)
        return carry

    lax.fori_loop(0, table_rows, pack, 0)
    widened = tokens_ref[0].astype(jnp.float32)
    factor = lax.rsqrt(jnp.mean(widened * widened, axis=-1, keepdims=True) + norm_eps)
    rows[0] = (widened * factor * gain_ref[...]).astype(jnp.bfloat16)
    wq = weight_ref.shape[0] // req_count
    quarter = cache_stage.shape[0]
    third = quarter // 3
    granule = 32
    blocks = 1024 // granule
    ends = []
    total = 0
    for prompt in range(4):
        total = total + (lengths[prompt] + granule - 1) // granule
        ends.append(total)
    starts = [0] + ends[:3]

    def source_of(index):
        prompt = 0
        begin = 0
        for p in range(1, 4):
            past = index >= starts[p]
            prompt = jnp.where(past, p, prompt)
            begin = jnp.where(past, starts[p], begin)
        return prompt * blocks + jnp.minimum(index - begin, blocks - 1)

    def stage(index, carry):
        source = source_of(my_req * quarter + index)
        cache_stage[index] = cache_ref[source]
        return carry

    lax.fori_loop(0, quarter, stage, 0)
    pl.semaphore_wait(barrier, 7)

    def send_row_y():
        return remote(
            rows.at[0], rows.at[1], row_send.at[0], row_recv.at[0], (my_req, at_slot(1))
        )

    def send_row_z():
        return remote(
            rows.at[0], rows.at[2], row_send.at[1], row_recv.at[1], (my_req, at_slot(2))
        )

    def send_row_on():
        return remote(
            rows.at[2], rows.at[3], row_send.at[2], row_recv.at[2], (my_req, at_slot(1))
        )

    def send_low(slot):
        return remote(
            low.at[0], low.at[slot], low_send.at[slot], low_recv.at[slot], (my_req, at_slot(slot))
        )

    def send_att(kind, slot):
        return remote(
            att_out.at[kind, slot],
            att_in.at[kind, slot],
            att_send.at[kind, slot],
            att_recv.at[kind, slot],
            (my_req, at_slot(slot)),
        )

    def to_req(source, target, sem_send, sem_recv, step):
        return remote(
            source, target, sem_send.at[step], sem_recv.at[step], (at_req(step), my_exp)
        )

    def send_down(step):
        return to_req(staging.at[step], offered.at[step], down_send, down_recv, step)

    def send_lift(step):
        return to_req(staging_lift.at[step], offered_lift.at[step], lift_send, lift_recv, step)

    def send_narrow(step):
        return to_req(
            staging_narrow.at[step], offered_narrow.at[step], narrow_send, narrow_recv, step
        )

    def send_up(step):
        return to_req(up_all.at[0], up_all.at[step], up_send, up_recv, step)

    def send_up_far():
        return remote(up_stage, up_far, far_send.at[4], far_recv.at[4], (my_req, far_exp))

    def piece(owner, part):
        if part == 0:
            return weight_far.at[pl.ds(pl.multiple_of(owner * wq, 32), wq)]
        return cache_far.at[pl.ds(owner * quarter + (part - 1) * third, third)]

    def send_far(part):
        if part == 0:
            source = weight_ref.at[pl.ds(pl.multiple_of(my_req * wq, 32), wq)]
        else:
            source = cache_stage.at[pl.ds((part - 1) * third, third)]
        return remote(
            source,
            piece(my_req, part),
            far_send.at[part],
            far_recv.at[part],
            (my_req, far_exp),
        )

    def send_across(part):
        return remote(
            piece(my_req, part),
            piece(my_req, part),
            across_send.at[part],
            across_recv.at[part],
            (across_req, my_exp),
        )

    def take_across(part):
        return remote(
            piece(across_req, part),
            piece(across_req, part),
            across_send.at[part],
            across_recv.at[part],
            (across_req, my_exp),
        )

    def send_core(kind, part):
        owner = my_req if kind == 0 else across_req
        return remote(
            piece(owner, part),
            piece(owner, part),
            core_send.at[kind, part],
            core_recv.at[kind, part],
            (core_req, my_exp),
        )

    def take_core(kind, part):
        owner = core_req if kind == 0 else (core_req + 2) % req_count
        return remote(
            piece(owner, part),
            piece(owner, part),
            core_send.at[kind, part],
            core_recv.at[kind, part],
            (core_req, my_exp),
        )

    def pass_far(part):
        send_far(part).wait_recv()
        send_across(part).start()
        send_core(0, part).start()

    def pass_across(part):
        take_across(part).wait_recv()
        send_core(1, part).start()

    outer = my_z == half
    inner = my_z != half
    send_row_z().start()
    send_row_y().start()
    for step in range(1, req_count):
        send_down(step).start()
    for step in range(1, req_count):
        send_up(step).start()

    send_far(0).start()

    @pl.when(inner)
    def _():
        for part in range(1, 4):
            send_far(part).start()

    top = lax.broadcasted_iota(jnp.int32, (128, 1), 0) < HEAD_WIDTH

    def widen(source_ref, target_ref):
        for head in range(2):
            block = source_ref[head * 192 : head * 192 + 128]
            block = jnp.where(top, block, jnp.zeros_like(block))
            target_ref[:, head * 128 : head * 128 + 128] = block.T
            target_ref[:, 256 + head * 128 : 384 + head * 128] = source_ref[
                head * 192 + 64 : head * 192 + 192
            ].T

    row_kind = lax.broadcasted_iota(jnp.int32, (256, 128), 0) % 2
    first_rows = (row_kind == 0).astype(jnp.bfloat16)
    second_rows = (row_kind == 1).astype(jnp.bfloat16)

    def own_keys(index, carry):
        block = cache_ref[pl.ds(index * 4, 4)].reshape(256, 128)
        at = pl.ds(pl.multiple_of(index % 8 * 256, 256), 256)
        keys_own[index // 8, at, :128] = block * first_rows
        keys_own[index // 8, at, 128:] = block * second_rows
        return carry

    widen(weight_ref, wide_own)
    lax.fori_loop(0, 32, own_keys, 0)

    for step in range(1, req_count):
        send_down(step).wait_recv()
    own_row = row_of(my_req * count + my_exp)
    source = (my_req - own_row // table_rows + req_count) % req_count
    contract = (((1,), (1,)), ((), ()))
    low[0] = lax.dot_general(
        offered[source], rows[0], contract, preferred_element_type=jnp.float32
    ).astype(jnp.bfloat16)
    for slot in range(1, 4):
        send_low(slot).start()

    for step in range(1, req_count):
        send_up(step).wait_recv()

    def up_of(request):
        row = row_of(request)
        return up_all[(my_req - row // table_rows + req_count) % req_count, row % table_rows]

    for index in range(4):
        up_stage[index] = up_of(my_req * count + (1 - half) * 4 + index)
    send_up_far().start()

    @pl.when(inner)
    def _():
        pass_far(0)


    column = lax.broadcasted_iota(jnp.int32, (128, 512), 1)
    lane = lax.broadcasted_iota(jnp.int32, (128, 512), 0)
    spread = (lane == (column // 128 % 2) * HEAD_WIDTH + column % HEAD_WIDTH).astype(jnp.bfloat16)
    column = lax.broadcasted_iota(jnp.int32, (rank, 512), 1)
    kind = lax.broadcasted_iota(jnp.int32, (rank, 512), 0) // ADAPTER_RANK
    back = column % 128 // HEAD_WIDTH
    kept = kind == jnp.where(column < 256, 3 * back, 1 + back)
    by_rank = (((0,), (0,)), ((), ()))
    causal = lax.broadcasted_iota(jnp.int32, (seq, seq), 0) >= lax.broadcasted_iota(
        jnp.int32, (seq, seq), 1
    )
    cached_at = lax.broadcasted_iota(jnp.int32, (1, prompt_rows), 1)
    even = lax.broadcasted_iota(jnp.int32, (1, 128), 1) % 2 == 0
    att_scale = HEAD_WIDTH ** (-0.5)

    def project(slot, wide_ref, up_one):
        base = jnp.dot(rows[slot], wide_ref[...], preferred_element_type=jnp.float32)
        up_wide = jnp.dot(up_one, spread, preferred_element_type=jnp.float32)
        up_wide = jnp.where(kept, up_wide, 0.0).astype(jnp.bfloat16)
        extra = lax.dot_general(low[slot], up_wide, by_rank, preferred_element_type=jnp.float32)
        return (base + adapter_scale * extra).astype(jnp.bfloat16)

    def attention(qkv, keys, length):
        query = qkv[:, :256] * jnp.bfloat16(att_scale)
        scores = lax.dot_general(query, keys, contract, preferred_element_type=jnp.float32)
        scores = jnp.where(cached_at < 2 * length, scores, masked_score)
        own_scores = []
        for head in range(2):
            at = slice(head * 128, head * 128 + 128)
            own = qkv[:, 256 + head * 128 : 384 + head * 128]
            one = lax.dot_general(query[:, at], own, contract, preferred_element_type=jnp.float32)
            own_scores.append(jnp.where(causal, one, masked_score))
        tiles = prompt_rows // 128
        most = scores[:, :128]
        for tile in range(1, tiles):
            most = jnp.maximum(most, scores[:, tile * 128 : tile * 128 + 128])
        peaks = []
        for head in range(2):
            mine = even if head == 0 else jnp.logical_not(even)
            peaks.append(
                jnp.maximum(
                    jnp.max(jnp.where(mine, most, masked_score), axis=-1, keepdims=True),
                    jnp.max(own_scores[head], axis=-1, keepdims=True),
                )
            )
        peak = jnp.where(even, peaks[0], peaks[1])
        weights = []
        summed = jnp.zeros((seq, 128), jnp.float32)
        for tile in range(tiles):
            one = jnp.exp(scores[:, tile * 128 : tile * 128 + 128] - peak)
            summed = summed + one
            weights.append(one.astype(jnp.bfloat16))
        total = jnp.dot(
            jnp.concatenate(weights, axis=1), keys, preferred_element_type=jnp.float32
        )
        parts = []
        for head in range(2):
            mine = even if head == 0 else jnp.logical_not(even)
            own = qkv[:, 256 + head * 128 : 384 + head * 128]
            own_exp = jnp.exp(own_scores[head] - peaks[head])
            denominator = jnp.sum(
                jnp.where(mine, summed, 0.0), axis=-1, keepdims=True
            ) + jnp.sum(own_exp, axis=-1, keepdims=True)
            both = total[:, head * 128 : head * 128 + 128] + jnp.dot(
                own_exp.astype(jnp.bfloat16), own, preferred_element_type=jnp.float32
            )
            parts.append((both / denominator)[:, HEAD_WIDTH:])
        return jnp.concatenate(parts, axis=1).astype(jnp.bfloat16)

    def own_heads(slot, carry):
        @pl.when(slot == 1)
        def _():
            send_row_z().wait_recv()
            send_row_on().start()

            @pl.when(outer)
            def _():
                send_row_z().wait_send()
                for part in range(1, 4):
                    send_far(part).start()

            @pl.when(inner)
            def _():
                pass_far(1)
                pass_across(0)

            send_row_y().wait_recv()
            send_low(1).wait_recv()

        @pl.when(slot == 2)
        def _():
            send_low(2).wait_recv()
            for step in range(1, req_count):
                send_lift(step).start()
                send_narrow(step).start()

            @pl.when(outer)
            def _():
                pass_far(0)

            @pl.when(inner)
            def _():
                pass_far(2)
                pass_far(3)
                pass_across(1)

        @pl.when(slot == 3)
        def _():
            @pl.when(outer)
            def _():
                pass_across(0)
                pass_far(1)
                pass_far(2)
                pass_far(3)

            send_row_on().wait_recv()
            send_low(3).wait_recv()

            @pl.when(inner)
            def _():
                pass_across(2)

        owner = at_slot(slot)
        prompt = prompts[owner]
        qkv = project(slot, wide_own, up_of(my_req * count + owner))
        att_out[0, slot] = attention(qkv, keys_own[prompt], lengths[prompt])

        @pl.when(slot > 0)
        def _():
            send_att(0, slot).start()

        return carry

    lax.fori_loop(0, 4, own_heads, 0)

    @pl.when(outer)
    def _():
        pass_across(1)
        pass_across(2)

    take_core(0, 0).wait_recv()
    take_core(1, 0).wait_recv()
    send_up_far().wait_recv()
    widen(weight_far, wide_far)

    def far_project(slot, carry):
        index = ((my_z + slot // 2) % 2) * 2 + (my_y + slot) % 2
        far_qkv[slot] = project(slot, wide_far, up_far[index])
        return carry

    lax.fori_loop(0, 4, far_project, 0)

    pass_across(3)

    for part in range(1, 4):
        take_core(0, part).wait_recv()
        take_core(1, part).wait_recv()

    def unpack(index, carry):
        for prompt in range(4):
            for lane in range(4):
                block = cache_far[jnp.minimum(starts[prompt] + index * 4 + lane, 4 * quarter - 1)]
                at = pl.ds(pl.multiple_of(index * 256 + lane * 64, 64), 64)
                keys_far[prompt, at, :128] = block * first_rows[:64]
                keys_far[prompt, at, 128:] = block * second_rows[:64]
        return carry

    lax.fori_loop(0, blocks // 4, unpack, 0)

    def far_keys(slot):
        prompt = prompts[at_slot(slot)]
        return keys_far[prompt], lengths[prompt]

    def far_heads(step, carry):
        first, second = 3 - 2 * step, 2 - 2 * step
        att_first = attention(far_qkv[first], *far_keys(first))
        att_second = attention(far_qkv[second], *far_keys(second))
        att_out[1, first] = att_first
        att_out[1, second] = att_second
        send_att(1, first).start()

        @pl.when(second > 0)
        def _():
            send_att(1, second).start()

        return carry

    lax.fori_loop(0, 2, far_heads, 0)

    for step in range(1, req_count):
        send_lift(step).wait_recv()
        send_narrow(step).wait_recv()
    for kind in range(2):
        for slot in range(4):
            if slot > 0:
                send_att(kind, slot).wait_recv()
            at = pl.ds(pl.multiple_of((at_slot(slot) if kind == 0 else mirrored(slot)) * 128, 128), 128)
            flat[:, at] = att_out[kind, 0] if slot == 0 else att_in[kind, slot]

    attended = flat[...]
    narrow = offered_narrow[source]
    narrow = jnp.concatenate(
        [narrow[at : at + ADAPTER_RANK] for at in range(0, narrow.shape[0], ADAPTER_RANK)], axis=1
    )
    low_out = lax.dot_general(attended, narrow, contract, preferred_element_type=jnp.float32)
    lift = offered_lift[source]
    terms = []
    for _ in range(3):
        terms.append(low_out.astype(jnp.bfloat16))
        low_out = low_out - terms[-1].astype(jnp.float32)
    surplus = jnp.dot(
        jnp.concatenate(terms, axis=1),
        jnp.concatenate([lift] * 3, axis=0),
        preferred_element_type=jnp.float32,
    )
    plain = jnp.dot(attended, output_ref[...], preferred_element_type=jnp.float32)
    hidden = tokens_ref[0].astype(jnp.float32) + (plain + adapter_scale * surplus)
    hidden = hidden.astype(jnp.bfloat16)
    hidden_ref[...] = hidden
    moe_in = rms_norm(hidden, expert_gain_ref[...])
    cells = lax.broadcasted_iota(jnp.int32, (outgoing_ref.shape[0], seq), 0)
    capacity = outgoing_ref.shape[0] // count
    target = jnp.where(slots_ref[...] >= 0, routes_ref[...] * capacity + slots_ref[...], -1)
    sending = jnp.where(cells == target[0:1], 1.0, jnp.where(cells == target[1:2], 1.0, 0.0))
    outgoing_ref[...] = jnp.dot(
        sending.astype(jnp.bfloat16), moe_in, preferred_element_type=jnp.float32
    ).astype(jnp.bfloat16)
    gates = jax.nn.sigmoid(
        lax.dot_general(router_ref[...], moe_in, contract, preferred_element_type=jnp.float32)
    )
    gated = [
        sending[expert * capacity : (expert + 1) * capacity] * gates[expert : expert + 1]
        for expert in range(count)
    ]
    combine_ref[...] = jnp.concatenate(gated, axis=0).T

    send_row_y().wait_send()
    send_row_on().wait_send()

    @pl.when(inner)
    def _():
        send_row_z().wait_send()

    for slot in range(1, 4):
        send_low(slot).wait_send()
        for kind in range(2):
            send_att(kind, slot).wait_send()
    for step in range(1, req_count):
        send_down(step).wait_send()
        send_lift(step).wait_send()
        send_narrow(step).wait_send()
        send_up(step).wait_send()
    send_up_far().wait_send()
    for part in range(4):
        send_far(part).wait_send()
    for part in range(4):
        send_across(part).wait_send()
        send_core(0, part).wait_send()
        send_core(1, part).wait_send()


def attend_block(
    tokens,
    gain,
    weight,
    cache,
    down,
    lift,
    narrow,
    up,
    output,
    expert_gain,
    router,
    routes,
    slots,
    prompts,
    lengths,
    adapters,
    slot_rows,
):
    _, seq, width = tokens.shape
    rank = down.shape[1]
    experts = router.shape[0]
    cells = experts * (5 * seq * TOP // (4 * experts))
    smem = pl.BlockSpec(memory_space=pltpu.SMEM)
    vmem = pl.BlockSpec(memory_space=pltpu.VMEM)
    dma = pltpu.SemaphoreType.DMA

    def bf16(*shape):
        return pltpu.VMEM(shape, jnp.bfloat16)

    return pl.pallas_call(
        block_kernel,
        out_shape=(
            jax.ShapeDtypeStruct((cells, width), jnp.bfloat16),
            jax.ShapeDtypeStruct((seq, width), jnp.bfloat16),
            jax.ShapeDtypeStruct((seq, cells), jnp.float32),
        ),
        in_specs=[smem] * 4 + [vmem] * 13,
        out_specs=(vmem, vmem, vmem),
        scratch_shapes=[
            bf16(seq, width),
            bf16(width, 512),
            bf16(width, 512),
            bf16(4, 2048, 256),
            bf16(4, 2048, 256),
            bf16(4, seq, width),
            bf16(4, rank, seq),
            bf16(4, seq, 512),
            bf16(2, 4, seq, 128),
            bf16(2, 4, seq, 128),
            bf16(4, rank, width),
            bf16(4, rank, width),
            bf16(4, *lift.shape[1:]),
            bf16(4, *lift.shape[1:]),
            bf16(4, *narrow.shape[1:]),
            bf16(4, *narrow.shape[1:]),
            bf16(4, up.shape[0], rank, 128),
            bf16(4, rank, 128),
            bf16(4, rank, 128),
            bf16(*weight.shape),
            bf16(21, *cache.shape[1:]),
            bf16(84, *cache.shape[1:]),
            dma((5,)),
            dma((5,)),
            dma((4,)),
            dma((4,)),
            dma((2, 4)),
            dma((2, 4)),
            dma((4,)),
            dma((4,)),
            dma((4,)),
            dma((4,)),
            dma((4,)),
            dma((4,)),
            dma((4,)),
            dma((4,)),
            dma((5,)),
            dma((5,)),
            dma((4,)),
            dma((4,)),
            dma((2, 4)),
            dma((2, 4)),
        ],
        compiler_params=pltpu.CompilerParams(
            collective_id=2, has_side_effects=True, vmem_limit_bytes=56 * 1024 * 1024
        ),
        name="attend_block",
    )(
        prompts,
        lengths,
        adapters,
        slot_rows,
        tokens,
        gain,
        weight,
        cache,
        down,
        lift,
        narrow,
        up,
        output,
        expert_gain,
        router,
        routes,
        slots,
    )


def expert_block_kernel(
    outgoing_ref,
    gate_up_hbm,
    down_hbm,
    out_ref,
    gate_up,
    down,
    inbox,
    outbox,
    back,
    weight_sem,
    there_send,
    there_recv,
    back_send,
    back_recv,
):
    my_req = lax.axis_index("req")
    my_exp = lax.axis_index("exp")
    half = my_exp // 4
    my_y = my_exp % 2
    my_z = (my_exp // 2) % 2
    load_gate_up = pltpu.make_async_copy(gate_up_hbm.at[0], gate_up, weight_sem.at[0])
    load_down = pltpu.make_async_copy(down_hbm.at[0], down, weight_sem.at[1])
    load_gate_up.start()
    load_down.start()

    def partner(step):
        crossing, slot = step // 4, step % 4
        side = (half + crossing) % 2
        return side * 4 + ((my_z + slot // 2 + crossing) % 2) * 2 + (my_y + slot) % 2

    barrier = pltpu.get_barrier_semaphore()
    for step in range(1, 8):
        pl.semaphore_signal(barrier, inc=1, device_id=(my_req, partner(step)), device_id_type=MESH)
    inbox[0] = outgoing_ref[my_exp]
    pl.semaphore_wait(barrier, 7)

    def send_there(step):
        return pltpu.make_async_remote_copy(
            src_ref=outgoing_ref.at[partner(step)],
            dst_ref=inbox.at[step],
            send_sem=there_send.at[step],
            recv_sem=there_recv.at[step],
            device_id=(my_req, partner(step)),
            device_id_type=MESH,
        )

    def send_back(step):
        return pltpu.make_async_remote_copy(
            src_ref=outbox.at[step],
            dst_ref=back.at[step],
            send_sem=back_send.at[step],
            recv_sem=back_recv.at[step],
            device_id=(my_req, partner(step)),
            device_id_type=MESH,
        )

    for step in (1, 2, 3, 4, 5, 6, 7):
        send_there(step).start()
    load_gate_up.wait()
    load_down.wait()
    cap, width = inbox.shape[1:]
    chunk = FF // 2

    def process(pair, carry):
        @pl.when(pair > 0)
        def _():
            send_there(2 * pair).wait_recv()

        send_there(2 * pair + 1).wait_recv()
        received = inbox[pl.ds(2 * pair, 2)].reshape(2 * cap, width)
        total = jnp.zeros((2 * cap, width), jnp.float32)
        for part in range(2):
            gate = jnp.dot(
                received,
                gate_up[:, part * chunk : (part + 1) * chunk],
                preferred_element_type=jnp.float32,
            )
            up = jnp.dot(
                received,
                gate_up[:, FF + part * chunk : FF + (part + 1) * chunk],
                preferred_element_type=jnp.float32,
            )
            activated = (jax.nn.gelu(gate, approximate=True) * up).astype(jnp.bfloat16)
            total = total + jnp.dot(
                activated,
                down[part * chunk : (part + 1) * chunk],
                preferred_element_type=jnp.float32,
            )
        outbox[pl.ds(2 * pair, 2)] = total.reshape(2, cap, width).astype(jnp.bfloat16)

        @pl.when(pair > 0)
        def _():
            send_back(2 * pair).start()

        send_back(2 * pair + 1).start()
        return carry

    lax.fori_loop(0, 4, process, 0)
    out_ref[my_exp] = outbox[0]
    for step in range(1, 8):
        send_back(step).wait_recv()
        out_ref[partner(step)] = back[step]
    for step in range(1, 8):
        send_there(step).wait_send()
    for step in range(1, 8):
        send_back(step).wait_send()


def expert_kernel(
    count,
    outgoing_ref,
    gate_up_hbm,
    down_hbm,
    out_ref,
    gate_up,
    down,
    inbox,
    outbox,
    back,
    weight_sem,
    there_send,
    there_recv,
    back_send,
    back_recv,
):
    my_req = lax.axis_index("req")
    my_exp = lax.axis_index("exp")
    load_gate_up = pltpu.make_async_copy(gate_up_hbm.at[0], gate_up, weight_sem.at[0])
    load_down = pltpu.make_async_copy(down_hbm.at[0], down, weight_sem.at[1])
    load_gate_up.start()
    load_down.start()

    def at_exp(offset):
        return (my_exp + offset + count) % count

    barrier = pltpu.get_barrier_semaphore()
    for step in range(1, count):
        pl.semaphore_signal(barrier, inc=1, device_id=(my_req, at_exp(step)), device_id_type=MESH)
    inbox[0] = outgoing_ref[my_exp]
    pl.semaphore_wait(barrier, count - 1)

    def send_there(step):
        return pltpu.make_async_remote_copy(
            src_ref=outgoing_ref.at[at_exp(step)],
            dst_ref=inbox.at[step],
            send_sem=there_send.at[step],
            recv_sem=there_recv.at[step],
            device_id=(my_req, at_exp(step)),
            device_id_type=MESH,
        )

    def send_back(step):
        return pltpu.make_async_remote_copy(
            src_ref=outbox.at[step],
            dst_ref=back.at[step],
            send_sem=back_send.at[step],
            recv_sem=back_recv.at[step],
            device_id=(my_req, at_exp(-step)),
            device_id_type=MESH,
        )

    for step in range(1, count):
        send_there(step).start()
    load_gate_up.wait()
    load_down.wait()
    cap, width = inbox.shape[1:]
    chunk = FF // 2

    def process(pair, carry):
        @pl.when(pair > 0)
        def _():
            send_there(2 * pair).wait_recv()

        send_there(2 * pair + 1).wait_recv()
        received = inbox[pl.ds(2 * pair, 2)].reshape(2 * cap, width)
        total = jnp.zeros((2 * cap, width), jnp.float32)
        for part in range(2):
            gate = jnp.dot(
                received,
                gate_up[:, part * chunk : (part + 1) * chunk],
                preferred_element_type=jnp.float32,
            )
            up = jnp.dot(
                received,
                gate_up[:, FF + part * chunk : FF + (part + 1) * chunk],
                preferred_element_type=jnp.float32,
            )
            activated = (jax.nn.gelu(gate, approximate=True) * up).astype(jnp.bfloat16)
            total = total + jnp.dot(
                activated,
                down[part * chunk : (part + 1) * chunk],
                preferred_element_type=jnp.float32,
            )
        outbox[pl.ds(2 * pair, 2)] = total.reshape(2, cap, width).astype(jnp.bfloat16)

        @pl.when(pair > 0)
        def _():
            send_back(2 * pair).start()

        send_back(2 * pair + 1).start()
        return carry

    lax.fori_loop(0, count // 2, process, 0)
    out_ref[my_exp] = outbox[0]
    for step in range(1, count):
        send_back(step).wait_recv()
        out_ref[at_exp(step)] = back[step]
    for step in range(1, count):
        send_there(step).wait_send()
        send_back(step).wait_send()


def run_experts(outgoing, gate_up, down, blocks=False):
    count, cap, width = outgoing.shape
    vmem = pl.BlockSpec(memory_space=pltpu.VMEM)
    hbm = pl.BlockSpec(memory_space=pl.ANY)
    dma = pltpu.SemaphoreType.DMA
    block = pltpu.VMEM(outgoing.shape, jnp.bfloat16)
    return pl.pallas_call(
        expert_block_kernel if blocks else functools.partial(expert_kernel, count),
        out_shape=jax.ShapeDtypeStruct(outgoing.shape, jnp.bfloat16),
        in_specs=[vmem, hbm, hbm],
        out_specs=vmem,
        scratch_shapes=[
            pltpu.VMEM(gate_up.shape[1:], jnp.bfloat16),
            pltpu.VMEM(down.shape[1:], jnp.bfloat16),
            block,
            block,
            block,
            dma((2,)),
            dma((count,)),
            dma((count,)),
            dma((count,)),
            dma((count,)),
        ],
        compiler_params=pltpu.CompilerParams(
            collective_id=3 if blocks else 1, has_side_effects=True, vmem_limit_bytes=52 * 1024 * 1024
        ),
        name="experts",
    )(outgoing, gate_up, down)


def body(
    tokens,
    attention_norm_gain,
    expert_norm_gain,
    query_key_value_weight,
    output_weight,
    prompt_key_value_cache,
    shared_prompt_length,
    prompt_per_request,
    adapter_per_request,
    adapter_slot_rows,
    adapter_down_qkv,
    adapter_up_qkv,
    adapter_down_output,
    adapter_up_output,
    router_weight,
    expert_gate_up_weight,
    expert_down_weight,
    routes,
    slots,
):
    heads_here = query_key_value_weight.shape[1]
    seq_whole = tokens.shape[1]
    table_rows = adapter_down_qkv.shape[0]
    narrow = jnp.swapaxes(adapter_down_output, 2, 3).reshape(table_rows, -1, HEAD_WIDTH)
    if (lax.axis_size("exp"), lax.axis_size("req"), heads_here) == (8, 4, 2):
        outgoing, hidden, combine = attend_block(
            tokens,
            attention_norm_gain[None],
            jnp.transpose(query_key_value_weight, (1, 2, 0)).reshape(-1, MODEL_WIDTH),
            prompt_key_value_cache.reshape(-1, 64, 2 * HEAD_WIDTH),
            jnp.swapaxes(adapter_down_qkv, 1, 2),
            adapter_up_output,
            narrow,
            adapter_up_qkv.reshape(table_rows, 6 * ADAPTER_RANK, HEAD_WIDTH),
            output_weight.reshape(-1, MODEL_WIDTH),
            expert_norm_gain[None],
            router_weight.T,
            routes[0].T,
            slots[0].T,
            prompt_per_request,
            shared_prompt_length,
            adapter_per_request,
            adapter_slot_rows,
        )
        returned = run_experts(
            outgoing.reshape(router_weight.shape[1], -1, MODEL_WIDTH),
            expert_gate_up_weight,
            expert_down_weight,
            blocks=True,
        )
        moe_sum = jnp.dot(
            combine,
            returned.reshape(-1, MODEL_WIDTH).astype(jnp.float32),
            precision=lax.Precision.HIGH,
        )
        return (hidden.astype(jnp.float32) + moe_sum).astype(jnp.bfloat16)[None]

    wanted_all = adapter_slot_rows[adapter_per_request]

    up_twice = jnp.concatenate([adapter_up_qkv, adapter_up_qkv], axis=-1).reshape(
        table_rows, 3 * ADAPTER_RANK, heads_here * 2 * HEAD_WIDTH
    )
    gathered, own_bo, own_ao = attend(
        tokens,
        attention_norm_gain[None],
        jnp.transpose(query_key_value_weight, (1, 2, 0)),
        jnp.swapaxes(prompt_key_value_cache, 1, 2),
        jnp.swapaxes(adapter_down_qkv, 1, 2),
        adapter_up_output,
        narrow,
        up_twice,
        prompt_per_request,
        shared_prompt_length,
        wanted_all,
    )
    flat_att = jnp.swapaxes(gathered, 0, 1).reshape(seq_whole, -1)
    plain_out = jnp.dot(
        flat_att, output_weight.reshape(-1, MODEL_WIDTH), preferred_element_type=jnp.float32
    )
    own_ao = jnp.swapaxes(own_ao.reshape(-1, ADAPTER_RANK, HEAD_WIDTH), 1, 2)
    low_out = jnp.dot(
        flat_att, own_ao.reshape(-1, ADAPTER_RANK), preferred_element_type=jnp.float32
    )
    surplus = lax.dot_general(
        low_out,
        own_bo.astype(jnp.float32),
        (((1,), (0,)), ((), ())),
        precision=lax.Precision.HIGHEST,
    )
    projected_rows = (plain_out + adapter_scale * surplus)[None]
    hidden = (tokens.astype(jnp.float32) + projected_rows).astype(jnp.bfloat16)
    moe_in = rms_norm(hidden, expert_norm_gain)
    rows_here = REQ_DEV * seq_whole
    flat_in = moe_in.reshape(rows_here, MODEL_WIDTH)
    gate_vals = jax.nn.sigmoid(jnp.dot(flat_in, router_weight, preferred_element_type=jnp.float32))
    expert_count = router_weight.shape[1]
    capacity = 5 * rows_here * TOP // (4 * expert_count)
    route_flat = routes.reshape(rows_here, TOP)
    slot_flat = slots.reshape(rows_here, TOP)
    target = jnp.where(slot_flat >= 0, route_flat * capacity + slot_flat, -1)
    cells = jnp.arange(expert_count * capacity, dtype=jnp.int32)
    matched = target[:, :, None] == cells[None, None, :]
    named = route_flat[:, :, None] == jnp.arange(expert_count, dtype=jnp.int32)[None, None, :]
    chosen_gate = jnp.sum(jnp.where(named, gate_vals[:, None, :], 0.0), axis=2)
    combine = jnp.sum(jnp.where(matched, chosen_gate[:, :, None], 0.0), axis=1)
    sending = jnp.any(matched, axis=1).astype(jnp.bfloat16)
    outgoing = jnp.einsum("rc,rd->cd", sending, flat_in, preferred_element_type=jnp.float32).astype(
        jnp.bfloat16
    )
    returned = run_experts(
        outgoing.reshape(expert_count, capacity, MODEL_WIDTH),
        expert_gate_up_weight,
        expert_down_weight,
    )
    returned_wide = returned.reshape(expert_count * capacity, MODEL_WIDTH).astype(jnp.float32)
    moe_sum = jnp.dot(combine, returned_wide, precision=lax.Precision.HIGHEST)
    mixed = (hidden.reshape(rows_here, MODEL_WIDTH).astype(jnp.float32) + moe_sum).astype(
        jnp.bfloat16
    )
    return mixed.reshape(tokens.shape)


def solution(mesh):
    in_specs = (
        P(("req", "exp"), None, None),
        P(),
        P(),
        P(None, "exp", None),
        P(),
        P(None, None, "exp", None),
        P(),
        P("req"),
        P(),
        P(),
        P("req", None, None),
        P("req", None, None, "exp", None),
        P("req", None, None, None),
        P("req", None, None),
        P(),
        P("exp", None, None),
        P("exp", None, None),
        P(("req", "exp"), None, None),
        P(("req", "exp"), None, None),
    )
    out_specs = P(("req", "exp"), None, None)
    return jax.shard_map(body, mesh=mesh, in_specs=in_specs, out_specs=out_specs, check_vma=False)
```
